32 devices in a mesh: fsdp: 8 (over y, x, core), dp: 4 (over z).
Axes of the slice: x: 2, y: 2, z: 4, core: 2. Of those that a mesh axis runs over, the one named last changes fastest.
Arguments:
- hidden_in: bfloat16 [17408, 1024], P(('fsdp', 'dp')), may hold values from -6 to 6
- cotangent: bfloat16 [17408, 1024], P(('fsdp', 'dp')), may hold values from -6 to 6
- segment_ids: int32 [32, 544], P(('fsdp', 'dp')), may hold values from 0 to 7, never falling along the last dimension, each value on 1 to 128 neighbouring positions
- box_left: int32 [32, 544], P(('fsdp', 'dp')), may hold values from 0 to 63
- box_top: int32 [32, 544], P(('fsdp', 'dp')), may hold values from 0 to 63
- query_weight: bfloat16 [1024, 1024], P('fsdp'), may hold values from -0.1875 to 0.1875
- query_bias: bfloat16 [1024], P('fsdp'), may hold values from -3 to 3
- key_weight: bfloat16 [1024, 1024], P('fsdp'), may hold values from -0.1875 to 0.1875
- value_weight: bfloat16 [1024, 1024], P('fsdp'), may hold values from -0.1875 to 0.1875
- value_bias: bfloat16 [1024], P('fsdp'), may hold values from -3 to 3
- output_weight: bfloat16 [1024, 1024], P('fsdp'), may hold values from -0.75 to 0.75
- output_bias: bfloat16 [1024], P('fsdp'), may hold values from -2 to 2
- first_gain: bfloat16 [1024], P('fsdp'), may hold values from 0.25 to 1.75
- first_shift: bfloat16 [1024], P('fsdp'), may hold values from -2 to 2
- inner_weight: bfloat16 [1024, 4096], P('fsdp'), may hold values from -0.1875 to 0.1875
- inner_bias: bfloat16 [4096], P('fsdp'), may hold values from -3 to 3
- outer_weight: bfloat16 [4096, 1024], P('fsdp'), may hold values from -0.125 to 0.125
- outer_bias: bfloat16 [1024], P('fsdp'), may hold values from -2 to 2
- second_gain: bfloat16 [1024], P('fsdp'), may hold values from 0.25 to 1.75
- second_shift: bfloat16 [1024], P('fsdp'), may hold values from -2 to 2
- bucket_table: bfloat16 [6144], P('fsdp'), may hold values from -5 to 5
Outputs:
- layer_out: bfloat16 [17408, 1024], P(('fsdp', 'dp'))
- input_grad: float32 [17408, 1024], P(('fsdp', 'dp'))
- query_weight_grad: float32 [1024, 1024], P('fsdp')
- query_bias_grad: float32 [1024], P('fsdp')
- key_weight_grad: float32 [1024, 1024], P('fsdp')
- value_weight_grad: float32 [1024, 1024], P('fsdp')
- value_bias_grad: float32 [1024], P('fsdp')
- output_weight_grad: float32 [1024, 1024], P('fsdp')
- output_bias_grad: float32 [1024], P('fsdp')
- first_gain_grad: float32 [1024], P('fsdp')
- first_shift_grad: float32 [1024], P('fsdp')
- inner_weight_grad: float32 [1024, 4096], P('fsdp')
- inner_bias_grad: float32 [4096], P('fsdp')
- outer_weight_grad: float32 [4096, 1024], P('fsdp')
- outer_bias_grad: float32 [1024], P('fsdp')
- second_gain_grad: float32 [1024], P('fsdp')
- second_shift_grad: float32 [1024], P('fsdp')
- bucket_table_grad: float32 [6144], P('fsdp')
The draws below stay inside these ranges and needn't reach their ends.
Inputs may be any that keep to these rules, and one draw needn't show every extreme that they name: `segment_ids`: within each packed row page numbers never fall, each page holds 1 to 128 slots, and one page of the row holds exactly 128.
All inputs are finite; a program needn't handle non-finite values.
Results may differ from the reference program's by a relative error of at most 0.017.
Values may be sent and summed in bfloat16 or wider, within the bound.
No kernel may reach another device: no remote copies, remote signals or barrier semaphores. Data moves between devices by JAX's collectives and lax.ppermute only.
A program may use at most 256 MiB of HBM per device.

```python
import math
from functools import partial
import jax
import jax.numpy as jnp
import numpy as np
from jax import lax

D = 1024
HEADS = 16
HEAD_DIM = 64
FF = 4096
NB = 128
SLOTS = 544
PAGES = 8
PAGE_MOST = 128
ROWS = 32
TOKENS = 17408


def with_ends(values, key, smallest, largest):
    longest = values.shape.index(max(values.shape))
    spots = []
    for shift in (0, 1):
        where = [jax.random.randint(jax.random.fold_in(key, axis), (), 0, length) for axis, length in enumerate(values.shape)]
        where[longest] = (where[longest] + shift) % values.shape[longest]
        spots.append(tuple(where))
    return values.at[spots[0]].set(smallest).at[spots[1]].set(largest)


def with_spikes(result, own_key, source, target, blocks, factor):
    owner, partner = [(jnp.arange(result.shape[dim]) // (result.shape[dim] // blocks)).reshape([-1 if axis == dim else 1 for axis in range(result.ndim)]) for dim in (source, target)]
    chosen = jax.random.permutation(own_key, blocks)[partner]
    strong = (owner == chosen) | (owner == (partner + blocks // 2) % blocks)
    return jnp.where(strong, factor * result, result)


def block_scale(stream_key, dims, pieces, least, high):
    factor_of = 1.0
    for axis_at, shards_of in pieces:
        draws = jax.random.uniform(jax.random.fold_in(jax.random.fold_in(stream_key, 6), axis_at), (shards_of,), jnp.float32, least / len(pieces), high / len(pieces))
        factor_of = factor_of * jnp.repeat(jnp.exp(draws), dims[axis_at] // shards_of).reshape((-1,) + (1,) * (len(dims) - 1 - axis_at))
    return factor_of


def split_up(number_of, total, limit, skew):
    weights = [(1 << 20) // math.isqrt(standing ** skew) + 1 for standing in range(2, number_of + 1)]
    spare, holding = total - limit - (number_of - 1), [1] * (number_of - 1)
    while spare > 0:
        free = [i for i in range(number_of - 1) if holding[i] < limit]
        mass, left = sum([weights[i] for i in free]), spare
        for i in free:
            extra = min(limit - holding[i], max(1, left * weights[i] // mass), spare)
            holding[i] = holding[i] + extra
            spare = spare - extra
    return np.array([limit] + holding)


def ragged(stream_key, amount, total, reach, slope):
    if amount == 2:
        one = jax.random.randint(stream_key, (), max(1, total - reach), min(reach, total - 1) + 1)
        return jnp.stack([one, total - one])
    sizes = jnp.asarray(split_up(amount, total, reach, slope), jnp.int32)
    twos = (amount - 1) // 2
    donor, taker = sizes[1:1 + 2 * twos:2], sizes[2:2 + 2 * twos:2]
    margin = jnp.minimum(donor - 1, reach - taker)
    passed = jax.random.randint(jax.random.fold_in(stream_key, 1), (twos,), 0, 1 << 20) % (margin + 1)
    sizes = sizes.at[1:1 + 2 * twos:2].set(donor - passed).at[2:2 + 2 * twos:2].set(taker + passed)
    return sizes[jax.random.permutation(jax.random.fold_in(stream_key, 2), amount)]


def bell_draw(rng, shape, scale, reach, shards=(), kind=jnp.bfloat16):
    drawn = jax.random.normal(rng, shape, jnp.float32) * scale
    if len(shards) > 0:
        drawn = block_scale(rng, shape, shards, -0.22, 0.18) * drawn
    return jnp.clip(drawn, min=-reach, max=reach).astype(kind)


def heavy_noise(own_key, extent, scale, limit, pieces, heavy, kind=jnp.bfloat16):
    drawn = scale * jax.random.normal(own_key, extent, jnp.float32)
    if pieces:
        drawn = drawn * block_scale(own_key, extent, pieces, -0.22, 0.18)
    return jnp.clip(with_spikes(drawn, jax.random.fold_in(own_key, 3), *heavy), -limit, limit).astype(kind)


def setup_inputs(seed: int = 0) -> dict:
    key_of = jax.random.split(jax.random.key(seed), 22)
    hidden_in = heavy_noise(key_of[0], (TOKENS, D), 1.0, 6.0, ((0, 32),), (0, 1, 32, 2.75))
    cotangent = heavy_noise(key_of[1], (TOKENS, D), 1.0, 6.0, ((0, 32),), (0, 1, 32, 2.75))
    segment_ids = jax.vmap(lambda own: jnp.searchsorted(jnp.cumsum(ragged(own, PAGES, SLOTS, PAGE_MOST, 0)), jnp.arange(SLOTS), side="right"))(jax.random.split(key_of[2], ROWS)).reshape((ROWS, SLOTS)).astype(jnp.int32)
    box_left = with_ends(jax.random.randint(key_of[3], (ROWS, SLOTS), 0, NB // 2), jax.random.fold_in(key_of[3], 1), 0, (NB // 2) - 1).astype(jnp.int32)
    box_top = with_ends(jax.random.randint(key_of[4], (ROWS, SLOTS), 0, NB // 2), jax.random.fold_in(key_of[4], 1), 0, (NB // 2) - 1).astype(jnp.int32)
    query_weight = bell_draw(key_of[5], (D, D), D ** -0.5, 0.1875, ((0, 8),))
    query_bias = bell_draw(key_of[6], (D,), 0.5, 3.0, ((0, 8),))
    key_weight = bell_draw(key_of[7], (D, D), D ** -0.5, 0.1875, ((0, 8),))
    value_weight = bell_draw(key_of[8], (D, D), D ** -0.5, 0.1875, ((0, 8),))
    value_bias = bell_draw(key_of[9], (D,), 0.5, 3.0, ((0, 8),))
    output_weight = bell_draw(key_of[10], (D, D), (D // 16) ** -0.5, 0.75, ((0, 8),))
    output_bias = bell_draw(key_of[11], (D,), 0.3, 2.0, ((0, 8),))
    first_gain = jnp.clip(1.0 + 0.15 * jax.random.normal(key_of[12], (D,), jnp.float32), 0.25, 1.75).astype(jnp.bfloat16)
    first_shift = bell_draw(key_of[13], (D,), 0.3, 2.0, ((0, 8),))
    inner_weight = bell_draw(key_of[14], (D, FF), D ** -0.5, 0.1875, ((0, 8),))
    inner_bias = bell_draw(key_of[15], (FF,), 0.5, 3.0, ((0, 8),))
    outer_weight = bell_draw(key_of[16], (FF, D), (FF // 2) ** -0.5, 0.125, ((0, 8),))
    outer_bias = bell_draw(key_of[17], (D,), 0.3, 2.0, ((0, 8),))
    second_gain = jnp.clip(1.0 + 0.15 * jax.random.normal(key_of[18], (D,), jnp.float32), 0.25, 1.75).astype(jnp.bfloat16)
    second_shift = bell_draw(key_of[19], (D,), 0.3, 2.0, ((0, 8),))
    bucket_table = bell_draw(key_of[20], (3 * NB * HEADS,), 1.0, 5.0, ((0, 8),))
    return {"hidden_in": hidden_in, "cotangent": cotangent, "segment_ids": segment_ids, "box_left": box_left, "box_top": box_top, "query_weight": query_weight, "query_bias": query_bias, "key_weight": key_weight, "value_weight": value_weight, "value_bias": value_bias, "output_weight": output_weight, "output_bias": output_bias, "first_gain": first_gain, "first_shift": first_shift, "inner_weight": inner_weight, "inner_bias": inner_bias, "outer_weight": outer_weight, "outer_bias": outer_bias, "second_gain": second_gain, "second_shift": second_shift, "bucket_table": bucket_table}


EPSILON = 1e-05
BLOCKED = -1e+30
precise = lax.Precision.HIGHEST

@jax.custom_vjp
def low(v):
    return lax.optimization_barrier(v.astype(jnp.bfloat16)).astype(jnp.float32)

@jax.custom_vjp
def low_back(v):
    return v

def low_keep(v):
    return (low(v), None)

def low_pass(kept, grad):
    return (grad,)

def back_keep(v):
    return (v, None)

def back_low(kept, grad):
    return (low(grad),)
low.defvjp(low_keep, low_pass)
low_back.defvjp(back_keep, back_low)

def page_positions(segment_ids):
    slot_count = segment_ids.shape[1]
    slot_index = jnp.arange(slot_count, dtype=jnp.int32)
    previous = jnp.concatenate([segment_ids[:, :1] - 1, segment_ids[:, :-1]], axis=1)
    starts = jnp.where(segment_ids != previous, slot_index[None, :], jnp.int32(0)).astype(jnp.int32)
    return (slot_index[None, :] - lax.cummax(starts, axis=1)).astype(jnp.int32)

def relative(coords, midpoint):
    offsets = coords[None, :] - coords[:, None]
    return (jnp.clip(offsets, -midpoint, midpoint - 1) + midpoint).astype(jnp.int32)

def bucket_ids(position, box_left, box_top):

    def one_row(row_pos, row_left, row_top):
        return jnp.stack([relative(row_pos, NB // 2), relative(row_left, NB // 2), relative(row_top, NB // 2)])
    return jax.vmap(one_row)(position, box_left, box_top)

def norm_layer(values, norm_gain, norm_shift):
    center = lax.optimization_barrier(jnp.mean(values, axis=-1, keepdims=True))
    centered = values - center
    spread = lax.rsqrt(lax.optimization_barrier(jnp.mean(centered * centered, axis=-1, keepdims=True)) + EPSILON)
    return centered * spread * norm_gain + norm_shift

def matmul(left_side, right_side):
    return jnp.dot(left_side, right_side, precision=precise, preferred_element_type=jnp.float32)

def attend_row(row_items, bias_table):
    row_queries, row_keys, row_values, row_ids, row_mask = row_items
    scores = jnp.einsum('qhe,khe->hqk', row_queries, row_keys, precision=precise, preferred_element_type=jnp.float32) * HEAD_DIM ** (-0.5)
    pair_bias = bias_table[0][row_ids[0]] + bias_table[1][row_ids[1]] + bias_table[2][row_ids[2]]
    logits = low_back(scores + jnp.transpose(pair_bias, (2, 0, 1)))
    logits = jnp.where(row_mask[None], logits, BLOCKED)
    probs = jax.nn.softmax(logits, axis=-1)
    context = jnp.einsum('hqk,khe->qhe', low(probs), row_values, precision=precise, preferred_element_type=jnp.float32)
    return context.reshape(row_queries.shape[0], HEADS * HEAD_DIM)

def layer_forward(pair_ids, page_mask, hidden, query_weight, query_bias, key_weight, value_weight, value_bias, output_weight, output_bias, first_gain, first_shift, inner_weight, inner_bias, outer_weight, outer_bias, second_gain, second_shift, bucket_table):
    row_count = pair_ids.shape[0]
    slot_count = pair_ids.shape[-1]
    by_rows = (row_count, slot_count, HEADS, HEAD_DIM)
    queries = low(low_back(matmul(hidden, query_weight) + query_bias))
    keys_low = low(low_back(matmul(hidden, key_weight)))
    values_low = low(low_back(matmul(hidden, value_weight) + value_bias))
    bias_table = bucket_table.reshape(3, NB, HEADS)
    row_fn = jax.checkpoint(partial(attend_row, bias_table=bias_table))
    context = lax.map(row_fn, (queries.reshape(by_rows), keys_low.reshape(by_rows), values_low.reshape(by_rows), pair_ids, page_mask))
    context = low(low_back(context.reshape(row_count * slot_count, HEADS * HEAD_DIM)))
    attn_out = low_back(matmul(context, output_weight) + output_bias)
    first_out = norm_layer(hidden + attn_out, first_gain, first_shift)
    inner = low_back(matmul(low(first_out), inner_weight) + inner_bias)
    active = low(jax.nn.gelu(inner, approximate=False))
    outer = low_back(matmul(active, outer_weight) + outer_bias)
    return norm_layer(first_out + outer, second_gain, second_shift)

def reference(hidden_in, cotangent, segment_ids, box_left, box_top, query_weight, query_bias, key_weight, value_weight, value_bias, output_weight, output_bias, first_gain, first_shift, inner_weight, inner_bias, outer_weight, outer_bias, second_gain, second_shift, bucket_table):
    position = page_positions(segment_ids)
    pair_ids = bucket_ids(position, box_left, box_top)
    page_mask = segment_ids[:, :, None] == segment_ids[:, None, :]
    params = (query_weight, query_bias, key_weight, value_weight, value_bias, output_weight, output_bias, first_gain, first_shift, inner_weight, inner_bias, outer_weight, outer_bias, second_gain, second_shift, bucket_table)
    params = tuple((item.astype(jnp.float32) for item in params))
    forward_fn = partial(layer_forward, pair_ids, page_mask)
    outputs, pullback = jax.vjp(forward_fn, hidden_in.astype(jnp.float32), *params)
    grads = pullback(cotangent.astype(jnp.float32))
    return (outputs.astype(jnp.bfloat16), grads[0], grads[1], grads[2], grads[3], grads[4], grads[5], grads[6], grads[7], grads[8], grads[9], grads[10], grads[11], grads[12], grads[13], grads[14], grads[15], grads[16])
```

```python
from functools import partial

import jax
import jax.numpy as jnp
import numpy as np
from jax import lax
from jax.experimental import pallas as pl
from jax.experimental.pallas import tpu as pltpu
from jax.sharding import PartitionSpec as P

HEADS = 16
HEAD_DIM = 64
PAIRS = HEADS // 2
NB = 128
PAGE = 128
PAGES = 8
EPSILON = 1e-05
BLOCKED = -1e30
BF = jnp.bfloat16
F32 = jnp.float32
VMEM_LIMIT = 48 * 1024 * 1024
NT = (((1,), (1,)), ((), ()))
TN = (((0,), (0,)), ((), ()))


def dot(left_side, right_side, dims=(((1,), (0,)), ((), ()))):
    return lax.dot_general(left_side, right_side, dims, preferred_element_type=F32)


def flips(bit_of):
    return [(i, i ^ bit_of(i & 1)) for i in range(8)]


NEAR = flips(lambda c: 2 if c else 4)
FAR = flips(lambda c: 4 if c else 2)
TWIN = flips(lambda c: 1)


def block_order(me):
    rel0 = np.array([0, 4, 2, 6, 1, 3, 5, 7], np.int32)
    rel1 = np.array([0, 2, 4, 6, 1, 5, 3, 7], np.int32)
    rel = jnp.where((me & 1) == 0, rel0, rel1)
    return jnp.bitwise_xor(me, rel).astype(jnp.int32)


def hop(value, pairs):
    return lax.ppermute(value, "fsdp", pairs)


def gather_blocks(own):
    near = hop(own, NEAR)
    far = hop(own, FAR)
    both = hop(near, FAR)
    mine = [own, near, far, both]
    return mine + [hop(item, TWIN) for item in mine]


def scatter_blocks(keep, send):
    other = hop(send, TWIN)
    away = keep[2:] + other[2:]
    stay = keep[:2] + other[:2]
    other = hop(away, FAR)
    away = stay[1] + other[1]
    stay = stay[0] + other[0]
    return stay + hop(away, NEAR)


def sum_line(value):
    rows = value.shape[0] // 4
    quarters = value.reshape((4, rows) + value.shape[1:])
    at = lax.axis_index("dp")

    def take(index):
        return lax.dynamic_index_in_dim(quarters, jnp.clip(index, 0, 3), 0, keepdims=False)

    up, down = take(at + 3), take(at - 3)
    for t in range(1, 4):
        up = lax.ppermute(up, "dp", [(i, i + 1) for i in range(t)])
        down = lax.ppermute(down, "dp", [(3 - i, 2 - i) for i in range(t)])
        if t < 3:
            up = up + take(at + 3 - t)
            down = down + take(at - 3 + t)
    mine = take(at) + up + down
    ups, downs = [mine], [mine]
    for t in range(1, 4):
        ups.append(lax.ppermute(ups[-1], "dp", [(i, i + 1) for i in range(t - 1, 3)]))
        downs.append(lax.ppermute(downs[-1], "dp", [(i, i - 1) for i in range(1, 5 - t)]))
    parts = []
    for q in range(4):
        part = mine
        for t in range(1, 4):
            part = jnp.where(at - q == t, ups[t], part)
            part = jnp.where(q - at == t, downs[t], part)
        parts.append(part)
    return jnp.concatenate(parts, axis=0)


def sum_line_small(value):
    value = value + lax.ppermute(value, "dp", [(i, i ^ 1) for i in range(4)])
    return value + lax.ppermute(value, "dp", [(i, i ^ 2) for i in range(4)])


def place_kernel(parts, order_ref, *refs):
    blocks, outs, sem = refs[:8], refs[8:-1], refs[-1]
    rows = blocks[0].shape[0] // parts
    columns = blocks[0].shape[1]
    copies = []
    for k in range(8):
        start = pl.multiple_of(order_ref[k] * rows, rows)
        for j in range(parts):
            copies.append(
                pltpu.make_async_copy(
                    blocks[k].at[pl.ds(j * rows, rows), :],
                    outs[0].at[pl.ds(start, rows), pl.ds(j * columns, columns)],
                    sem.at[k, j],
                )
            )
    for copy in copies:
        copy.start()
    for copy in copies:
        copy.wait()


def place(order, blocks, parts=1):
    rows, columns = blocks[0].shape
    return pl.pallas_call(
        partial(place_kernel, parts),
        out_shape=jax.ShapeDtypeStruct((8 * rows // parts, parts * columns), blocks[0].dtype),
        in_specs=[pl.BlockSpec(memory_space=pltpu.SMEM)]
        + [pl.BlockSpec(memory_space=pl.ANY)] * 8,
        out_specs=pl.BlockSpec(memory_space=pl.ANY),
        scratch_shapes=[pltpu.SemaphoreType.DMA((8, parts))],
        cost_estimate=pl.CostEstimate(
            flops=0, bytes_accessed=32 * rows * columns, transcendentals=0
        ),
    )(order, *blocks)


def pick_kernel(order_ref, grad_ref, keep_ref, send_ref, sem):
    rows = keep_ref.shape[1]
    copies = []
    for k in range(8):
        start = pl.multiple_of(order_ref[k] * rows, rows)
        target = keep_ref if k < 4 else send_ref
        copies.append(
            pltpu.make_async_copy(
                grad_ref.at[pl.ds(start, rows), :], target.at[k % 4], sem.at[k]
            )
        )
    for copy in copies:
        copy.start()
    for copy in copies:
        copy.wait()


def pick(order, grad):
    rows, columns = grad.shape[0] // 8, grad.shape[1]
    shape = jax.ShapeDtypeStruct((4, rows, columns), grad.dtype)
    return pl.pallas_call(
        pick_kernel,
        out_shape=(shape, shape),
        in_specs=[
            pl.BlockSpec(memory_space=pltpu.SMEM),
            pl.BlockSpec(memory_space=pl.ANY),
        ],
        out_specs=(pl.BlockSpec(memory_space=pl.ANY),) * 2,
        scratch_shapes=[pltpu.SemaphoreType.DMA((8,))],
        cost_estimate=pl.CostEstimate(
            flops=0, bytes_accessed=32 * rows * columns, transcendentals=0
        ),
    )(order, grad)


def tables_kernel(position_ref, box_ref, lookup_ref, slide_ref):
    row = lax.broadcasted_iota(jnp.int32, (NB, NB), 0)
    lane = lax.broadcasted_iota(jnp.int32, (NB, NB), 1)
    same = (row < 64) == (lane < 64)
    for head in range(HEADS):
        base = jnp.broadcast_to(position_ref[head : head + 1, :], (PAGE, 2 * PAGE))
        slid = pltpu.roll(base, 0, 1, stride=1, stride_axis=0)
        half = (head % 2) * PAGE
        slide_ref[head // 2, :, half : half + PAGE] = slid[:, :PAGE]
        left = jnp.broadcast_to(box_ref[0, head : head + 1, :], (64, NB))
        top = jnp.broadcast_to(box_ref[1, head : head + 1, :], (64, NB))
        slid = pltpu.roll(
            jnp.concatenate([left, top], axis=0), 0, 1, stride=1, stride_axis=0
        )
        lookup_ref[:, head * NB : (head + 1) * NB] = jnp.where(same, slid, 0.0).astype(BF)


def make_tables(table):
    spot = np.zeros((2 * PAGE, NB), np.float32)
    for m in range(2 * PAGE):
        offset = -m if m <= PAGE else 2 * PAGE - m
        spot[m, min(max(offset, -64), 63) + 64] = 1.0
    position = lax.dot_general(
        table[0], jnp.asarray(spot, BF), (((0,), (1,)), ((), ())), preferred_element_type=F32
    )
    box = jnp.roll(table[1:].astype(F32).transpose(0, 2, 1), 64, axis=2)
    return pl.pallas_call(
        tables_kernel,
        out_shape=(
            jax.ShapeDtypeStruct((NB, HEADS * NB), BF),
            jax.ShapeDtypeStruct((PAIRS, PAGE, 2 * PAGE), F32),
        ),
    )(position, box)


def split_heads(tile):
    lane = lax.broadcasted_iota(jnp.int32, tile.shape, 1)
    zero = jnp.zeros_like(tile)
    return jnp.concatenate(
        [jnp.where(lane < HEAD_DIM, tile, zero), jnp.where(lane >= HEAD_DIM, tile, zero)],
        axis=0,
    )


def join_heads(tall):
    lane = lax.broadcasted_iota(jnp.int32, (PAGE, NB), 1)
    return jnp.where(lane < HEAD_DIM, tall[:PAGE, :NB], tall[PAGE:, :NB])


def attend_kernel(
    length_ref, q_ref, k_ref, v_ref, box_ref, lookup_ref, slide_ref, context_ref, prob_ref
):
    length = length_ref[pl.program_id(0)]
    inside = lax.broadcasted_iota(jnp.int32, (PAGE, 2 * PAGE), 0) < length
    boxes = box_ref[...]
    for pair in range(PAIRS):
        at = slice(pair * NB, (pair + 1) * NB)
        looked = dot(boxes, lookup_ref[:, 2 * pair * NB : 2 * (pair + 1) * NB]).astype(BF)
        looked = jnp.concatenate([looked[:, :NB], looked[:, NB:]], axis=0)
        asked = jnp.concatenate([split_heads(q_ref[:, at]), looked], axis=1)
        offered = jnp.concatenate([k_ref[:, at], boxes], axis=1)
        logits = dot(offered, asked, NT) + slide_ref[pair]
        logits = jnp.where(inside, logits, BLOCKED)
        peak = jnp.max(logits, axis=0, keepdims=True)
        grown = jnp.exp(logits - peak)
        total = jnp.sum(grown, axis=0, keepdims=True)
        prob = (grown * (1.0 / total)).astype(BF)
        prob_ref[0, pair] = prob
        context_ref[:, at] = join_heads(dot(prob, v_ref[:, at], TN)).astype(BF)


def attend(lengths, queries, keys, values, boxes, lookup, slide):
    wide = pl.BlockSpec((PAGE, HEADS * HEAD_DIM), lambda i, n: (i, 0))
    return pl.pallas_call(
        attend_kernel,
        grid_spec=pltpu.PrefetchScalarGridSpec(
            num_scalar_prefetch=1,
            grid=(PAGES,),
            in_specs=[
                wide,
                wide,
                wide,
                pl.BlockSpec((PAGE, NB), lambda i, n: (i, 0)),
                pl.BlockSpec((NB, HEADS * NB), lambda i, n: (0, 0)),
                pl.BlockSpec((PAIRS, PAGE, 2 * PAGE), lambda i, n: (0, 0, 0)),
            ],
            out_specs=(
                wide,
                pl.BlockSpec((1, PAIRS, PAGE, 2 * PAGE), lambda i, n: (i, 0, 0, 0)),
            ),
        ),
        out_shape=(
            jax.ShapeDtypeStruct((PAGES * PAGE, HEADS * HEAD_DIM), BF),
            jax.ShapeDtypeStruct((PAGES, PAIRS, PAGE, 2 * PAGE), BF),
        ),
        compiler_params=pltpu.CompilerParams(vmem_limit_bytes=VMEM_LIMIT),
        cost_estimate=pl.CostEstimate(
            flops=6 * 10**9, bytes_accessed=14 * 2**20, transcendentals=2 * 2**20
        ),
    )(lengths, queries, keys, values, boxes, lookup, slide)


def attend_back_kernel(
    q_ref,
    k_ref,
    v_ref,
    g_ref,
    box_ref,
    flip_ref,
    prob_ref,
    grad_ref,
    slide_sum_ref,
    box_sum_ref,
    slide_acc,
    box_acc,
):
    page = pl.program_id(0)

    @pl.when(page == 0)
    def _():
        slide_acc[...] = jnp.zeros_like(slide_acc)
        box_acc[...] = jnp.zeros_like(box_acc)

    boxes = box_ref[...]
    flipped = flip_ref[...]
    width = HEADS * HEAD_DIM
    for pair in range(PAIRS):
        at = slice(pair * NB, (pair + 1) * NB)
        prob = prob_ref[0, pair]
        pulled = split_heads(g_ref[:, at])
        d_prob = dot(v_ref[:, at], pulled, NT)
        prob_full = prob.astype(F32)
        inner = jnp.sum(prob_full * d_prob, axis=0, keepdims=True)
        d_logit = (prob_full * (d_prob - inner)).astype(BF)
        slide_acc[pair] += d_logit.astype(F32)
        offered = jnp.concatenate([k_ref[:, at], boxes], axis=1)
        back = dot(d_logit, offered, TN)
        scale = HEAD_DIM ** (-0.5)
        grad_ref[:, at] = (join_heads(back) * scale).astype(BF)
        grad_ref[:, width + pair * NB : width + (pair + 1) * NB] = dot(
            d_logit, split_heads(q_ref[:, at])
        ).astype(BF)
        grad_ref[:, 2 * width + pair * NB : 2 * width + (pair + 1) * NB] = dot(
            prob, pulled
        ).astype(BF)
        boxed = back[:, NB:].astype(BF)
        boxed = jnp.concatenate([boxed[:PAGE], boxed[PAGE:]], axis=1)
        box_acc[:, 2 * pair * NB : 2 * (pair + 1) * NB] += dot(flipped, boxed)

    @pl.when(page == PAGES - 1)
    def _():
        row = lax.broadcasted_iota(jnp.int32, (NB, NB), 0)
        lane = lax.broadcasted_iota(jnp.int32, (NB, NB), 1)
        mirror = (row + lane == NB - 1).astype(F32)
        same = (row < 64) == (lane >= 64)
        for head in range(HEADS):
            half = (head % 2) * PAGE
            block = slide_acc[head // 2, :, half : half + PAGE]
            block = lax.dot_general(
                mirror,
                block,
                (((1,), (0,)), ((), ())),
                precision=lax.Precision.HIGHEST,
                preferred_element_type=F32,
            )
            block = jnp.concatenate([block, jnp.zeros_like(block)], axis=1)
            slid = pltpu.roll(block, 0, 1, stride=1, stride_axis=0)
            slide_sum_ref[head : head + 1, :] = jnp.sum(slid, axis=0, keepdims=True)
            block = jnp.where(same, box_acc[:, head * NB : (head + 1) * NB], 0.0)
            slid = pltpu.roll(block, 0, 1, stride=1, stride_axis=0)
            box_sum_ref[1, head : head + 1, :] = jnp.sum(slid[:64], axis=0, keepdims=True)
            box_sum_ref[0, head : head + 1, :] = jnp.sum(slid[64:], axis=0, keepdims=True)


def attend_back(queries, keys, values, d_context, boxes, flipped, prob):
    width = HEADS * HEAD_DIM
    wide = pl.BlockSpec((PAGE, width), lambda i: (i, 0))
    return pl.pallas_call(
        attend_back_kernel,
        grid=(PAGES,),
        in_specs=[
            wide,
            wide,
            wide,
            wide,
            pl.BlockSpec((PAGE, NB), lambda i: (i, 0)),
            pl.BlockSpec((NB, PAGE), lambda i: (0, i)),
            pl.BlockSpec((1, PAIRS, PAGE, 2 * PAGE), lambda i: (i, 0, 0, 0)),
        ],
        out_specs=(
            pl.BlockSpec((PAGE, 3 * width), lambda i: (i, 0)),
            pl.BlockSpec((HEADS, 2 * PAGE), lambda i: (0, 0)),
            pl.BlockSpec((2, HEADS, NB), lambda i: (0, 0, 0)),
        ),
        out_shape=(
            jax.ShapeDtypeStruct((PAGES * PAGE, 3 * width), BF),
            jax.ShapeDtypeStruct((HEADS, 2 * PAGE), F32),
            jax.ShapeDtypeStruct((2, HEADS, NB), F32),
        ),
        scratch_shapes=[
            pltpu.VMEM((PAIRS, PAGE, 2 * PAGE), F32),
            pltpu.VMEM((NB, HEADS * NB), F32),
        ],
        compiler_params=pltpu.CompilerParams(vmem_limit_bytes=VMEM_LIMIT),
        cost_estimate=pl.CostEstimate(
            flops=10 * 10**9, bytes_accessed=20 * 2**20, transcendentals=0
        ),
    )(queries, keys, values, d_context, boxes, flipped, prob)


def fold_sums(slide_sum, box_sum):
    spot = np.zeros((2 * PAGE, NB), np.float32)
    for c in range(2 * PAGE - 1):
        spot[c, min(max(PAGE - 1 - c, -64), 63) + 64] = 1.0
    position = lax.dot_general(
        slide_sum,
        jnp.asarray(spot),
        (((1,), (0,)), ((), ())),
        precision=lax.Precision.HIGHEST,
        preferred_element_type=F32,
    )
    box = jnp.roll(box_sum, 65, axis=2)
    return jnp.concatenate([position[None], box], axis=0).transpose(0, 2, 1)


def norm_parts(values):
    center = jnp.mean(values, axis=-1, keepdims=True)
    centered = values - center
    spread = lax.rsqrt(jnp.mean(centered * centered, axis=-1, keepdims=True) + EPSILON)
    return centered * spread, spread


def norm_back(normed, spread, pulled):
    level = jnp.mean(pulled, axis=-1, keepdims=True)
    slope = jnp.mean(pulled * normed, axis=-1, keepdims=True)
    return spread * (pulled - level - normed * slope)


def on_device(line, *args):
    (
        hidden_in,
        cotangent,
        segment_ids,
        box_left,
        box_top,
        query_weight,
        query_bias,
        key_weight,
        value_weight,
        value_bias,
        output_weight,
        output_bias,
        first_gain,
        first_shift,
        inner_weight,
        inner_bias,
        outer_weight,
        outer_bias,
        second_gain,
        second_shift,
        bucket_table,
    ) = args
    row_count, slot_count = segment_ids.shape
    width = hidden_in.shape[1]
    vectors = (
        query_bias,
        value_bias,
        output_bias,
        first_gain,
        first_shift,
        inner_bias,
        outer_bias,
        second_gain,
        second_shift,
        bucket_table,
    )
    cuts = np.cumsum([0] + [item.shape[0] for item in vectors])
    small = jnp.concatenate(vectors)
    in_shard = jnp.concatenate([query_weight, key_weight, value_weight], axis=0)
    if line:
        me = lax.axis_index("fsdp")
        order = block_order(me)
        put = (order[None, :] == jnp.arange(8)[:, None]).astype(F32)
        small_all = dot(
            put.astype(BF), jnp.stack(gather_blocks(small.reshape(-1, 128))).reshape(8, -1)
        )
        in_all = place(order, gather_blocks(in_shard), 3)
        output_all = place(order, gather_blocks(output_weight))
        inner_all = place(order, gather_blocks(inner_weight))
        outer_all = place(order, gather_blocks(outer_weight))
    else:
        gather = partial(lax.all_gather, axis_name="fsdp", axis=0)
        small_all = gather(small).astype(F32)
        in_all = gather(in_shard).reshape(-1, 3, query_weight.shape[0], width)
        in_all = in_all.transpose(0, 2, 1, 3).reshape(width, 3 * width)
        output_all = gather(output_weight, tiled=True)
        inner_all = gather(inner_weight, tiled=True)
        outer_all = gather(outer_weight, tiled=True)
    fulls = [
        small_all[:, cuts[i] : cuts[i + 1]].reshape(-1) for i in range(len(vectors))
    ]
    (q_bias, v_bias, o_bias, gain1, shift1, i_bias, u_bias, gain2, shift2, table) = fulls

    slot = lax.iota(jnp.int32, slot_count)
    pages = lax.iota(jnp.int32, PAGES)
    member = segment_ids[:, None, :] == pages[None, :, None]
    lengths = jnp.sum(member, axis=2, dtype=jnp.int32)
    starts = jnp.sum(
        segment_ids[:, None, :] < pages[None, :, None], axis=2, dtype=jnp.int32
    )
    start_of = jnp.sum(jnp.where(member, starts[:, :, None], 0), axis=1)
    target = segment_ids * PAGE + slot[None, :] - start_of
    padded = lax.iota(jnp.int32, PAGES * PAGE)
    lookup, slide = make_tables(table.reshape(3, NB, HEADS).astype(BF))

    in_bias = jnp.concatenate([q_bias, jnp.zeros_like(q_bias), v_bias])
    rows = []
    for r in range(row_count):
        row = slice(r * slot_count, (r + 1) * slot_count)
        spread = (padded[:, None] == target[r][None, :]).astype(BF)
        coords = lax.iota(jnp.int32, 64)
        marks = jnp.concatenate(
            [box_left[r][:, None] == coords[None], box_top[r][:, None] == coords[None]], axis=1
        ).astype(BF)
        boxes = dot(spread, marks).astype(BF)
        flipped = dot(marks[:, ::-1], spread, (((0,), (1,)), ((), ()))).astype(BF)
        hidden = dot(spread, hidden_in[row]).astype(BF)
        mixed = dot(hidden, in_all) + in_bias
        queries = (mixed[:, :width] * HEAD_DIM ** (-0.5)).astype(BF)
        keys = mixed[:, width : 2 * width].astype(BF)
        values = mixed[:, 2 * width :].astype(BF)
        context, prob = attend(lengths[r], queries, keys, values, boxes, lookup, slide)
        context = dot(spread, context, TN).astype(BF)
        rows.append((spread, boxes, flipped, hidden, queries, keys, values, context, prob))
    context = jnp.concatenate([item[7] for item in rows], axis=0)

    attn_out = dot(context, output_all) + o_bias
    normed1, spread1 = norm_parts(hidden_in.astype(F32) + attn_out)
    first_out = normed1 * gain1 + shift1
    first_low = first_out.astype(BF)
    inner = dot(first_low, inner_all) + i_bias
    share = 0.5 * (1.0 + lax.erf(inner * np.float32(0.5**0.5)))
    active = (inner * share).astype(BF)
    steep = share + inner * jnp.exp(-0.5 * inner * inner) * np.float32((2 * np.pi) ** -0.5)
    steep = steep.astype(BF)
    outer = dot(active, outer_all) + u_bias
    normed2, spread2 = norm_parts(first_out + outer)
    layer_out = (normed2 * gain2 + shift2).astype(BF)

    upstream = cotangent.astype(F32)
    second_gain_grad = jnp.sum(upstream * normed2, axis=0)
    second_shift_grad = jnp.sum(upstream, axis=0)
    d_second = norm_back(normed2, spread2, upstream * gain2)
    d_outer = d_second.astype(BF)
    outer_bias_grad = jnp.sum(d_outer, axis=0, dtype=F32)
    outer_grad = dot(active, d_outer, TN).astype(BF)
    d_inner = (dot(d_outer, outer_all, NT) * steep).astype(BF)
    inner_bias_grad = jnp.sum(d_inner, axis=0, dtype=F32)
    inner_grad = dot(first_low, d_inner, TN).astype(BF)
    d_first = d_second + dot(d_inner, inner_all, NT)
    first_gain_grad = jnp.sum(d_first * normed1, axis=0)
    first_shift_grad = jnp.sum(d_first, axis=0)
    d_summed = norm_back(normed1, spread1, d_first * gain1)
    d_attn = d_summed.astype(BF)
    output_bias_grad = jnp.sum(d_attn, axis=0, dtype=F32)
    output_grad = dot(context, d_attn, TN).astype(BF)
    d_context = dot(d_attn, output_all, NT).astype(BF)

    pulled, in_grad, slide_sum, box_sum, in_bias_grad = [], 0.0, 0.0, 0.0, 0.0
    for r in range(row_count):
        row = slice(r * slot_count, (r + 1) * slot_count)
        spread, boxes, flipped, hidden, queries, keys, values, _, prob = rows[r]
        d_padded = dot(spread, d_context[row]).astype(BF)
        d_mixed, slide_part, box_part = attend_back(
            queries, keys, values, d_padded, boxes, flipped, prob
        )
        in_grad = in_grad + dot(hidden, d_mixed, TN)
        in_bias_grad = in_bias_grad + jnp.sum(d_mixed, axis=0, dtype=F32)
        slide_sum, box_sum = slide_sum + slide_part, box_sum + box_part
        back = dot(d_mixed, in_all, NT).astype(BF)
        pulled.append(dot(spread, back, TN))
    in_grad = in_grad.astype(BF)
    input_grad = d_summed + jnp.concatenate(pulled, axis=0)
    table_grad = fold_sums(slide_sum, box_sum).reshape(-1)

    grads = (
        in_bias_grad[:width],
        in_bias_grad[2 * width :],
        output_bias_grad,
        first_gain_grad,
        first_shift_grad,
        inner_bias_grad,
        outer_bias_grad,
        second_gain_grad,
        second_shift_grad,
        table_grad,
    )
    small_grad = jnp.concatenate(
        [item.reshape(small_all.shape[0], -1) for item in grads], axis=1
    )
    if line:
        picked = jnp.einsum(
            "bk,bn->kn", put, small_grad, precision=lax.Precision.HIGHEST
        ).reshape(8, -1, 128)
        outer_own = sum_line(scatter_blocks(*pick(order, outer_grad)))
        inner_own = sum_line(scatter_blocks(*pick(order, inner_grad)))
        output_own = sum_line(scatter_blocks(*pick(order, output_grad)))
        in_own = sum_line(scatter_blocks(*pick(order, in_grad)))
        small_own = sum_line_small(scatter_blocks(picked[:4], picked[4:])).reshape(-1)
    else:

        def reduce(value):
            value = lax.psum_scatter(value, "fsdp", scatter_dimension=0, tiled=True)
            return lax.psum(value, "dp")

        outer_own = reduce(outer_grad)
        inner_own = reduce(inner_grad)
        output_own = reduce(output_grad)
        in_own = reduce(in_grad)
        small_own = reduce(small_grad).reshape(-1)
    owned = [small_own[cuts[i] : cuts[i + 1]] for i in range(len(vectors))]
    in_own = in_own.astype(F32)
    return (
        layer_out,
        input_grad,
        in_own[:, :width],
        owned[0],
        in_own[:, width : 2 * width],
        in_own[:, 2 * width :],
        owned[1],
        output_own.astype(F32),
        owned[2],
        owned[3],
        owned[4],
        inner_own.astype(F32),
        owned[5],
        outer_own.astype(F32),
        owned[6],
        owned[7],
        owned[8],
        owned[9],
    )


def solution(mesh):
    line = mesh.shape["fsdp"] == 8 and mesh.shape["dp"] == 4
    both, across, flat = P(("fsdp", "dp"), None), P("fsdp", None), P("fsdp")
    return jax.shard_map(
        partial(on_device, line),
        mesh=mesh,
        in_specs=(both,) * 5
        + (across, flat, across, across, flat, across, flat, flat, flat)
        + (across, flat, across, flat, flat, flat, flat),
        out_specs=(both, both)
        + (across, flat, across, across, flat, across, flat, flat, flat)
        + (across, flat, across, flat, flat, flat, flat),
        check_vma=False,
    )
```

```python
from functools import partial

import jax
import jax.numpy as jnp
import numpy as np
from jax import lax
from jax.experimental import pallas as pl
from jax.experimental.pallas import tpu as pltpu
from jax.sharding import PartitionSpec as P

HEADS = 16
HEAD_DIM = 64
PAIRS = HEADS // 2
NB = 128
PAGE = 128
PAGES = 8
EPSILON = 1e-05
BLOCKED = -1e30
BF = jnp.bfloat16
F32 = jnp.float32
VMEM_LIMIT = 48 * 1024 * 1024
NT = (((1,), (1,)), ((), ()))
TN = (((0,), (0,)), ((), ()))


def dot(left_side, right_side, dims=(((1,), (0,)), ((), ()))):
    return lax.dot_general(left_side, right_side, dims, preferred_element_type=F32)


def flips(bit_of):
    return [(i, i ^ bit_of(i & 1)) for i in range(8)]


NEAR = flips(lambda c: 2 if c else 4)
FAR = flips(lambda c: 4 if c else 2)
TWIN = flips(lambda c: 1)


def block_order(me):
    rel0 = np.array([0, 4, 2, 6, 1, 3, 5, 7], np.int32)
    rel1 = np.array([0, 2, 4, 6, 1, 5, 3, 7], np.int32)
    rel = jnp.where((me & 1) == 0, rel0, rel1)
    return jnp.bitwise_xor(me, rel).astype(jnp.int32)


def hop(value, pairs):
    return lax.ppermute(value, "fsdp", pairs)


def gather_blocks(own):
    near = hop(own, NEAR)
    far = hop(own, FAR)
    both = hop(near, FAR)
    mine = [own, near, far, both]
    return mine + [hop(item, TWIN) for item in mine]


def scatter_blocks(keep, send):
    other = hop(send, TWIN)
    away = keep[2:] + other[2:]
    stay = keep[:2] + other[:2]
    other = hop(away, FAR)
    away = stay[1] + other[1]
    stay = stay[0] + other[0]
    return stay + hop(away, NEAR)


def sum_line(value):
    rows = value.shape[0] // 4
    quarters = value.reshape((4, rows) + value.shape[1:])
    at = lax.axis_index("dp")

    def take(index):
        return lax.dynamic_index_in_dim(quarters, jnp.clip(index, 0, 3), 0, keepdims=False)

    up, down = take(at + 3), take(at - 3)
    for t in range(1, 4):
        up = lax.ppermute(up, "dp", [(i, i + 1) for i in range(t)])
        down = lax.ppermute(down, "dp", [(3 - i, 2 - i) for i in range(t)])
        if t < 3:
            up = up + take(at + 3 - t)
            down = down + take(at - 3 + t)
    mine = take(at) + up + down
    ups, downs = [mine], [mine]
    for t in range(1, 4):
        ups.append(lax.ppermute(ups[-1], "dp", [(i, i + 1) for i in range(t - 1, 3)]))
        downs.append(lax.ppermute(downs[-1], "dp", [(i, i - 1) for i in range(1, 5 - t)]))
    parts = []
    for q in range(4):
        part = mine
        for t in range(1, 4):
            part = jnp.where(at - q == t, ups[t], part)
            part = jnp.where(q - at == t, downs[t], part)
        parts.append(part)
    return jnp.concatenate(parts, axis=0)


def sum_line_small(value):
    value = value + lax.ppermute(value, "dp", [(i, i ^ 1) for i in range(4)])
    return value + lax.ppermute(value, "dp", [(i, i ^ 2) for i in range(4)])


def place_kernel(parts, order_ref, *refs):
    blocks, out_ref, sem = refs[:8], refs[8], refs[9]
    rows = blocks[0].shape[0] // parts
    columns = blocks[0].shape[1]
    copies = []
    for k in range(8):
        start = pl.multiple_of(order_ref[k] * rows, rows)
        for j in range(parts):
            copies.append(
                pltpu.make_async_copy(
                    blocks[k].at[pl.ds(j * rows, rows), :],
                    out_ref.at[pl.ds(start, rows), pl.ds(j * columns, columns)],
                    sem.at[k, j],
                )
            )
    for copy in copies:
        copy.start()
    for copy in copies:
        copy.wait()


def place(order, blocks, parts=1):
    rows, columns = blocks[0].shape
    return pl.pallas_call(
        partial(place_kernel, parts),
        out_shape=jax.ShapeDtypeStruct((8 * rows // parts, parts * columns), blocks[0].dtype),
        in_specs=[pl.BlockSpec(memory_space=pltpu.SMEM)]
        + [pl.BlockSpec(memory_space=pl.ANY)] * 8,
        out_specs=pl.BlockSpec(memory_space=pltpu.VMEM),
        scratch_shapes=[pltpu.SemaphoreType.DMA((8, parts))],
        compiler_params=pltpu.CompilerParams(vmem_limit_bytes=VMEM_LIMIT),
        cost_estimate=pl.CostEstimate(
            flops=0, bytes_accessed=32 * rows * columns, transcendentals=0
        ),
    )(order, *blocks)


def grad_kernel(first, order_ref, left_ref, right_ref, out_ref, turned):
    rows = out_ref.shape[1]

    @pl.when(pl.program_id(0) == 0)
    def _():
        for k in range(4):
            start = pl.multiple_of(order_ref[first + k] * rows, rows)
            turned[k * rows : (k + 1) * rows, :] = left_ref[:, pl.ds(start, rows)].T

    for k in range(4):
        out_ref[k] = dot(turned[k * rows : (k + 1) * rows, :], right_ref[...]).astype(BF)


def grad_blocks(order, first, left, right, tile):
    depth, rows, columns = left.shape[0], left.shape[1] // 8, right.shape[1]
    return pl.pallas_call(
        partial(grad_kernel, first),
        grid_spec=pltpu.PrefetchScalarGridSpec(
            num_scalar_prefetch=1,
            grid=(columns // tile,),
            in_specs=[
                pl.BlockSpec((depth, 8 * rows), lambda i, n: (0, 0)),
                pl.BlockSpec((depth, tile), lambda i, n: (0, i)),
            ],
            out_specs=pl.BlockSpec((4, rows, tile), lambda i, n: (0, 0, i)),
            scratch_shapes=[pltpu.VMEM((4 * rows, depth), left.dtype)],
        ),
        out_shape=jax.ShapeDtypeStruct((4, rows, columns), BF),
        compiler_params=pltpu.CompilerParams(vmem_limit_bytes=VMEM_LIMIT),
        cost_estimate=pl.CostEstimate(
            flops=8 * depth * rows * columns,
            bytes_accessed=2 * (depth * (8 * rows + columns) + 4 * rows * columns),
            transcendentals=0,
        ),
    )(order, left, right)


def scatter_grad(order, left, right, tile):
    send = grad_blocks(order, 4, left, right, tile)
    keep = grad_blocks(order, 0, left, right, tile)
    return scatter_blocks(keep, send)


def tables_kernel(position_ref, box_ref, lookup_ref, slide_ref):
    row = lax.broadcasted_iota(jnp.int32, (NB, NB), 0)
    lane = lax.broadcasted_iota(jnp.int32, (NB, NB), 1)
    same = (row < 64) == (lane < 64)
    for head in range(HEADS):
        base = jnp.broadcast_to(position_ref[head : head + 1, :], (PAGE, 2 * PAGE))
        slid = pltpu.roll(base, 0, 1, stride=1, stride_axis=0)
        half = (head % 2) * PAGE
        slide_ref[head // 2, :, half : half + PAGE] = slid[:, :PAGE]
        left = jnp.broadcast_to(box_ref[0, head : head + 1, :], (64, NB))
        top = jnp.broadcast_to(box_ref[1, head : head + 1, :], (64, NB))
        slid = pltpu.roll(
            jnp.concatenate([left, top], axis=0), 0, 1, stride=1, stride_axis=0
        )
        lookup_ref[:, head * NB : (head + 1) * NB] = jnp.where(same, slid, 0.0).astype(BF)


def make_tables(table):
    spot = np.zeros((2 * PAGE, NB), np.float32)
    for m in range(2 * PAGE):
        offset = -m if m <= PAGE else 2 * PAGE - m
        spot[m, min(max(offset, -64), 63) + 64] = 1.0
    position = lax.dot_general(
        table[0], jnp.asarray(spot, BF), (((0,), (1,)), ((), ())), preferred_element_type=F32
    )
    box = jnp.roll(table[1:].astype(F32).transpose(0, 2, 1), 64, axis=2)
    return pl.pallas_call(
        tables_kernel,
        out_shape=(
            jax.ShapeDtypeStruct((NB, HEADS * NB), BF),
            jax.ShapeDtypeStruct((PAIRS, PAGE, 2 * PAGE), F32),
        ),
    )(position, box)


def split_heads(tile):
    lane = lax.broadcasted_iota(jnp.int32, tile.shape, 1)
    zero = jnp.zeros_like(tile)
    return jnp.concatenate(
        [jnp.where(lane < HEAD_DIM, tile, zero), jnp.where(lane >= HEAD_DIM, tile, zero)],
        axis=0,
    )


def join_heads(tall):
    lane = lax.broadcasted_iota(jnp.int32, (PAGE, NB), 1)
    return jnp.where(lane < HEAD_DIM, tall[:PAGE, :NB], tall[PAGE:, :NB])


def attend_kernel(
    length_ref, q_ref, k_ref, v_ref, box_ref, lookup_ref, slide_ref, context_ref, prob_ref
):
    length = length_ref[pl.program_id(0)]
    inside = lax.broadcasted_iota(jnp.int32, (PAGE, 2 * PAGE), 0) < length
    boxes = box_ref[...]
    for pair in range(PAIRS):
        at = slice(pair * NB, (pair + 1) * NB)
        looked = dot(boxes, lookup_ref[:, 2 * pair * NB : 2 * (pair + 1) * NB]).astype(BF)
        looked = jnp.concatenate([looked[:, :NB], looked[:, NB:]], axis=0)
        asked = jnp.concatenate([split_heads(q_ref[:, at]), looked], axis=1)
        offered = jnp.concatenate([k_ref[:, at], boxes], axis=1)
        logits = dot(offered, asked, NT) + slide_ref[pair]
        logits = jnp.where(inside, logits, BLOCKED)
        peak = jnp.max(logits, axis=0, keepdims=True)
        grown = jnp.exp(logits - peak)
        total = jnp.sum(grown, axis=0, keepdims=True)
        prob = (grown * (1.0 / total)).astype(BF)
        prob_ref[0, pair] = prob
        context_ref[:, at] = join_heads(dot(prob, v_ref[:, at], TN)).astype(BF)


def attend(lengths, queries, keys, values, boxes, lookup, slide):
    wide = pl.BlockSpec((PAGE, HEADS * HEAD_DIM), lambda i, n: (i, 0))
    return pl.pallas_call(
        attend_kernel,
        grid_spec=pltpu.PrefetchScalarGridSpec(
            num_scalar_prefetch=1,
            grid=(PAGES,),
            in_specs=[
                wide,
                wide,
                wide,
                pl.BlockSpec((PAGE, NB), lambda i, n: (i, 0)),
                pl.BlockSpec((NB, HEADS * NB), lambda i, n: (0, 0)),
                pl.BlockSpec((PAIRS, PAGE, 2 * PAGE), lambda i, n: (0, 0, 0)),
            ],
            out_specs=(
                wide,
                pl.BlockSpec((1, PAIRS, PAGE, 2 * PAGE), lambda i, n: (i, 0, 0, 0)),
            ),
        ),
        out_shape=(
            jax.ShapeDtypeStruct((PAGES * PAGE, HEADS * HEAD_DIM), BF),
            jax.ShapeDtypeStruct((PAGES, PAIRS, PAGE, 2 * PAGE), BF),
        ),
        compiler_params=pltpu.CompilerParams(vmem_limit_bytes=VMEM_LIMIT),
        cost_estimate=pl.CostEstimate(
            flops=6 * 10**9, bytes_accessed=14 * 2**20, transcendentals=2 * 2**20
        ),
    )(lengths, queries, keys, values, boxes, lookup, slide)


def attend_back_kernel(
    q_ref,
    k_ref,
    v_ref,
    g_ref,
    box_ref,
    flip_ref,
    prob_ref,
    grad_ref,
    slide_sum_ref,
    box_sum_ref,
    slide_acc,
    box_acc,
):
    page = pl.program_id(0)

    @pl.when(page == 0)
    def _():
        slide_acc[...] = jnp.zeros_like(slide_acc)
        box_acc[...] = jnp.zeros_like(box_acc)

    boxes = box_ref[...]
    flipped = flip_ref[...]
    width = HEADS * HEAD_DIM
    for pair in range(PAIRS):
        at = slice(pair * NB, (pair + 1) * NB)
        prob = prob_ref[0, pair]
        pulled = split_heads(g_ref[:, at])
        d_prob = dot(v_ref[:, at], pulled, NT)
        prob_full = prob.astype(F32)
        inner = jnp.sum(prob_full * d_prob, axis=0, keepdims=True)
        d_logit = (prob_full * (d_prob - inner)).astype(BF)
        slide_acc[pair] += d_logit.astype(F32)
        offered = jnp.concatenate([k_ref[:, at], boxes], axis=1)
        back = dot(d_logit, offered, TN)
        scale = HEAD_DIM ** (-0.5)
        grad_ref[:, at] = (join_heads(back) * scale).astype(BF)
        grad_ref[:, width + pair * NB : width + (pair + 1) * NB] = dot(
            d_logit, split_heads(q_ref[:, at])
        ).astype(BF)
        grad_ref[:, 2 * width + pair * NB : 2 * width + (pair + 1) * NB] = dot(
            prob, pulled
        ).astype(BF)
        boxed = back[:, NB:].astype(BF)
        boxed = jnp.concatenate([boxed[:PAGE], boxed[PAGE:]], axis=1)
        box_acc[:, 2 * pair * NB : 2 * (pair + 1) * NB] += dot(flipped, boxed)

    @pl.when(page == PAGES - 1)
    def _():
        row = lax.broadcasted_iota(jnp.int32, (NB, NB), 0)
        lane = lax.broadcasted_iota(jnp.int32, (NB, NB), 1)
        mirror = (row + lane == NB - 1).astype(F32)
        same = (row < 64) == (lane >= 64)
        for head in range(HEADS):
            half = (head % 2) * PAGE
            block = slide_acc[head // 2, :, half : half + PAGE]
            block = lax.dot_general(
                mirror,
                block,
                (((1,), (0,)), ((), ())),
                precision=lax.Precision.HIGHEST,
                preferred_element_type=F32,
            )
            block = jnp.concatenate([block, jnp.zeros_like(block)], axis=1)
            slid = pltpu.roll(block, 0, 1, stride=1, stride_axis=0)
            slide_sum_ref[head : head + 1, :] = jnp.sum(slid, axis=0, keepdims=True)
            block = jnp.where(same, box_acc[:, head * NB : (head + 1) * NB], 0.0)
            slid = pltpu.roll(block, 0, 1, stride=1, stride_axis=0)
            box_sum_ref[1, head : head + 1, :] = jnp.sum(slid[:64], axis=0, keepdims=True)
            box_sum_ref[0, head : head + 1, :] = jnp.sum(slid[64:], axis=0, keepdims=True)


def attend_back(queries, keys, values, d_context, boxes, flipped, prob):
    width = HEADS * HEAD_DIM
    wide = pl.BlockSpec((PAGE, width), lambda i: (i, 0))
    return pl.pallas_call(
        attend_back_kernel,
        grid=(PAGES,),
        in_specs=[
            wide,
            wide,
            wide,
            wide,
            pl.BlockSpec((PAGE, NB), lambda i: (i, 0)),
            pl.BlockSpec((NB, PAGE), lambda i: (0, i)),
            pl.BlockSpec((1, PAIRS, PAGE, 2 * PAGE), lambda i: (i, 0, 0, 0)),
        ],
        out_specs=(
            pl.BlockSpec((PAGE, 3 * width), lambda i: (i, 0)),
            pl.BlockSpec((HEADS, 2 * PAGE), lambda i: (0, 0)),
            pl.BlockSpec((2, HEADS, NB), lambda i: (0, 0, 0)),
        ),
        out_shape=(
            jax.ShapeDtypeStruct((PAGES * PAGE, 3 * width), BF),
            jax.ShapeDtypeStruct((HEADS, 2 * PAGE), F32),
            jax.ShapeDtypeStruct((2, HEADS, NB), F32),
        ),
        scratch_shapes=[
            pltpu.VMEM((PAIRS, PAGE, 2 * PAGE), F32),
            pltpu.VMEM((NB, HEADS * NB), F32),
        ],
        compiler_params=pltpu.CompilerParams(vmem_limit_bytes=VMEM_LIMIT),
        cost_estimate=pl.CostEstimate(
            flops=10 * 10**9, bytes_accessed=20 * 2**20, transcendentals=0
        ),
    )(queries, keys, values, d_context, boxes, flipped, prob)


def fold_sums(slide_sum, box_sum):
    spot = np.zeros((2 * PAGE, NB), np.float32)
    for c in range(2 * PAGE - 1):
        spot[c, min(max(PAGE - 1 - c, -64), 63) + 64] = 1.0
    position = lax.dot_general(
        slide_sum,
        jnp.asarray(spot),
        (((1,), (0,)), ((), ())),
        precision=lax.Precision.HIGHEST,
        preferred_element_type=F32,
    )
    box = jnp.roll(box_sum, 65, axis=2)
    return jnp.concatenate([position[None], box], axis=0).transpose(0, 2, 1)


def norm_parts(values):
    center = jnp.mean(values, axis=-1, keepdims=True)
    centered = values - center
    spread = lax.rsqrt(jnp.mean(centered * centered, axis=-1, keepdims=True) + EPSILON)
    return centered * spread, spread


def norm_back(normed, spread, pulled):
    level = jnp.mean(pulled, axis=-1, keepdims=True)
    slope = jnp.mean(pulled * normed, axis=-1, keepdims=True)
    return spread * (pulled - level - normed * slope)


def on_device(line, *args):
    (
        hidden_in,
        cotangent,
        segment_ids,
        box_left,
        box_top,
        query_weight,
        query_bias,
        key_weight,
        value_weight,
        value_bias,
        output_weight,
        output_bias,
        first_gain,
        first_shift,
        inner_weight,
        inner_bias,
        outer_weight,
        outer_bias,
        second_gain,
        second_shift,
        bucket_table,
    ) = args
    row_count, slot_count = segment_ids.shape
    width = hidden_in.shape[1]
    vectors = (
        query_bias,
        value_bias,
        output_bias,
        first_gain,
        first_shift,
        inner_bias,
        outer_bias,
        second_gain,
        second_shift,
        bucket_table,
    )
    cuts = np.cumsum([0] + [item.shape[0] for item in vectors])
    small = jnp.concatenate(vectors)
    in_shard = jnp.concatenate([query_weight, key_weight, value_weight], axis=0)
    if line:
        me = lax.axis_index("fsdp")
        order = block_order(me)
        put = (order[None, :] == jnp.arange(8)[:, None]).astype(F32)
        small_all = dot(
            put.astype(BF), jnp.stack(gather_blocks(small.reshape(-1, 128))).reshape(8, -1)
        )
        in_all = place(order, gather_blocks(in_shard), 3)
        output_all = place(order, gather_blocks(output_weight))
        inner_all = place(order, gather_blocks(inner_weight))
        outer_all = place(order, gather_blocks(outer_weight))
    else:
        gather = partial(lax.all_gather, axis_name="fsdp", axis=0)
        small_all = gather(small).astype(F32)
        in_all = gather(in_shard).reshape(-1, 3, query_weight.shape[0], width)
        in_all = in_all.transpose(0, 2, 1, 3).reshape(width, 3 * width)
        output_all = gather(output_weight, tiled=True)
        inner_all = gather(inner_weight, tiled=True)
        outer_all = gather(outer_weight, tiled=True)
    fulls = [
        small_all[:, cuts[i] : cuts[i + 1]].reshape(-1) for i in range(len(vectors))
    ]
    (q_bias, v_bias, o_bias, gain1, shift1, i_bias, u_bias, gain2, shift2, table) = fulls

    slot = lax.iota(jnp.int32, slot_count)
    pages = lax.iota(jnp.int32, PAGES)
    member = segment_ids[:, None, :] == pages[None, :, None]
    lengths = jnp.sum(member, axis=2, dtype=jnp.int32)
    starts = jnp.sum(
        segment_ids[:, None, :] < pages[None, :, None], axis=2, dtype=jnp.int32
    )
    start_of = jnp.sum(jnp.where(member, starts[:, :, None], 0), axis=1)
    target = segment_ids * PAGE + slot[None, :] - start_of
    padded = lax.iota(jnp.int32, PAGES * PAGE)
    lookup, slide = make_tables(table.reshape(3, NB, HEADS).astype(BF))

    in_bias = jnp.concatenate([q_bias, jnp.zeros_like(q_bias), v_bias])
    rows = []
    for r in range(row_count):
        row = slice(r * slot_count, (r + 1) * slot_count)
        spread = (padded[:, None] == target[r][None, :]).astype(BF)
        coords = lax.iota(jnp.int32, 64)
        marks = jnp.concatenate(
            [box_left[r][:, None] == coords[None], box_top[r][:, None] == coords[None]], axis=1
        ).astype(BF)
        boxes = dot(spread, marks).astype(BF)
        flipped = dot(marks[:, ::-1], spread, (((0,), (1,)), ((), ()))).astype(BF)
        hidden = dot(spread, hidden_in[row]).astype(BF)
        mixed = dot(hidden, in_all) + in_bias
        queries = (mixed[:, :width] * HEAD_DIM ** (-0.5)).astype(BF)
        keys = mixed[:, width : 2 * width].astype(BF)
        values = mixed[:, 2 * width :].astype(BF)
        context, prob = attend(lengths[r], queries, keys, values, boxes, lookup, slide)
        context = dot(spread, context, TN).astype(BF)
        rows.append((spread, boxes, flipped, hidden, queries, keys, values, context, prob))
    context = jnp.concatenate([item[7] for item in rows], axis=0)

    attn_out = dot(context, output_all) + o_bias
    normed1, spread1 = norm_parts(hidden_in.astype(F32) + attn_out)
    first_out = normed1 * gain1 + shift1
    first_low = first_out.astype(BF)
    inner = dot(first_low, inner_all) + i_bias
    share = 0.5 * (1.0 + lax.erf(inner * np.float32(0.5**0.5)))
    active = (inner * share).astype(BF)
    steep = share + inner * jnp.exp(-0.5 * inner * inner) * np.float32((2 * np.pi) ** -0.5)
    steep = steep.astype(BF)
    outer = dot(active, outer_all) + u_bias
    normed2, spread2 = norm_parts(first_out + outer)
    layer_out = (normed2 * gain2 + shift2).astype(BF)

    upstream = cotangent.astype(F32)
    second_gain_grad = jnp.sum(upstream * normed2, axis=0)
    second_shift_grad = jnp.sum(upstream, axis=0)
    d_second = norm_back(normed2, spread2, upstream * gain2)
    d_outer = d_second.astype(BF)
    outer_bias_grad = jnp.sum(d_outer, axis=0, dtype=F32)
    d_inner = (dot(d_outer, outer_all, NT) * steep).astype(BF)
    inner_bias_grad = jnp.sum(d_inner, axis=0, dtype=F32)
    d_first = d_second + dot(d_inner, inner_all, NT)
    first_gain_grad = jnp.sum(d_first * normed1, axis=0)
    first_shift_grad = jnp.sum(d_first, axis=0)
    d_summed = norm_back(normed1, spread1, d_first * gain1)
    d_attn = d_summed.astype(BF)
    output_bias_grad = jnp.sum(d_attn, axis=0, dtype=F32)
    d_context = dot(d_attn, output_all, NT).astype(BF)

    pulled, mixed_grads, slide_sum, box_sum, in_bias_grad = [], [], 0.0, 0.0, 0.0
    for r in range(row_count):
        row = slice(r * slot_count, (r + 1) * slot_count)
        spread, boxes, flipped, hidden, queries, keys, values, _, prob = rows[r]
        d_padded = dot(spread, d_context[row]).astype(BF)
        d_mixed, slide_part, box_part = attend_back(
            queries, keys, values, d_padded, boxes, flipped, prob
        )
        mixed_grads.append(d_mixed)
        in_bias_grad = in_bias_grad + jnp.sum(d_mixed, axis=0, dtype=F32)
        slide_sum, box_sum = slide_sum + slide_part, box_sum + box_part
        back = dot(d_mixed, in_all, NT).astype(BF)
        pulled.append(dot(spread, back, TN))
    hidden = jnp.concatenate([item[3] for item in rows], axis=0)
    d_mixed = jnp.concatenate(mixed_grads, axis=0)
    input_grad = d_summed + jnp.concatenate(pulled, axis=0)
    table_grad = fold_sums(slide_sum, box_sum).reshape(-1)

    grads = (
        in_bias_grad[:width],
        in_bias_grad[2 * width :],
        output_bias_grad,
        first_gain_grad,
        first_shift_grad,
        inner_bias_grad,
        outer_bias_grad,
        second_gain_grad,
        second_shift_grad,
        table_grad,
    )
    small_grad = jnp.concatenate(
        [item.reshape(small_all.shape[0], -1) for item in grads], axis=1
    )
    if line:
        picked = jnp.einsum(
            "bk,bn->kn", put, small_grad, precision=lax.Precision.HIGHEST
        ).reshape(8, -1, 128)
        outer_own = sum_line(scatter_grad(order, active, d_outer, 256))
        inner_own = sum_line(scatter_grad(order, first_low, d_inner, 1024))
        output_own = sum_line(scatter_grad(order, context, d_attn, 512))
        in_own = sum_line(scatter_grad(order, hidden, d_mixed, 1024))
        small_own = sum_line_small(scatter_blocks(picked[:4], picked[4:])).reshape(-1)
    else:

        def reduce(value):
            value = lax.psum_scatter(value, "fsdp", scatter_dimension=0, tiled=True)
            return lax.psum(value, "dp")

        outer_own = reduce(dot(active, d_outer, TN).astype(BF))
        inner_own = reduce(dot(first_low, d_inner, TN).astype(BF))
        output_own = reduce(dot(context, d_attn, TN).astype(BF))
        in_own = reduce(dot(hidden, d_mixed, TN).astype(BF))
        small_own = reduce(small_grad).reshape(-1)
    owned = [small_own[cuts[i] : cuts[i + 1]] for i in range(len(vectors))]
    in_own = in_own.astype(F32)
    return (
        layer_out,
        input_grad,
        in_own[:, :width],
        owned[0],
        in_own[:, width : 2 * width],
        in_own[:, 2 * width :],
        owned[1],
        output_own.astype(F32),
        owned[2],
        owned[3],
        owned[4],
        inner_own.astype(F32),
        owned[5],
        outer_own.astype(F32),
        owned[6],
        owned[7],
        owned[8],
        owned[9],
    )


def solution(mesh):
    line = mesh.shape["fsdp"] == 8 and mesh.shape["dp"] == 4
    both, across, flat = P(("fsdp", "dp"), None), P("fsdp", None), P("fsdp")
    return jax.shard_map(
        partial(on_device, line),
        mesh=mesh,
        in_specs=(both,) * 5
        + (across, flat, across, across, flat, across, flat, flat, flat)
        + (across, flat, across, flat, flat, flat, flat),
        out_specs=(both, both)
        + (across, flat, across, across, flat, across, flat, flat, flat)
        + (across, flat, across, flat, flat, flat, flat),
        check_vma=False,
    )
```

```python
from functools import partial

import jax
import jax.numpy as jnp
import numpy as np
from jax import lax
from jax.experimental import pallas as pl
from jax.experimental.pallas import tpu as pltpu
from jax.sharding import PartitionSpec as P

HEADS = 16
HEAD_DIM = 64
PAIRS = HEADS // 2
NB = 128
PAGE = 128
PAGES = 8
EPSILON = 1e-05
BLOCKED = -1e30
BF = jnp.bfloat16
F32 = jnp.float32
VMEM_LIMIT = 48 * 1024 * 1024
BRIEF = pl.CostEstimate(flops=1, bytes_accessed=1, transcendentals=0)
NT = (((1,), (1,)), ((), ()))
TN = (((0,), (0,)), ((), ()))


def dot(left_side, right_side, dims=(((1,), (0,)), ((), ()))):
    return lax.dot_general(left_side, right_side, dims, preferred_element_type=F32)


def flips(bit_of):
    return [(i, i ^ bit_of(i & 1)) for i in range(8)]


NEAR = flips(lambda c: 2 if c else 4)
FAR = flips(lambda c: 4 if c else 2)
TWIN = flips(lambda c: 1)


def block_order(me):
    rel0 = np.array([0, 4, 2, 6, 1, 3, 5, 7], np.int32)
    rel1 = np.array([0, 2, 4, 6, 1, 5, 3, 7], np.int32)
    rel = jnp.where((me & 1) == 0, rel0, rel1)
    return jnp.bitwise_xor(me, rel).astype(jnp.int32)


def hop(value, pairs):
    return lax.ppermute(value, "fsdp", pairs)


def after(value, *others):
    return lax.optimization_barrier((value,) + others)[0]


def first_hops(own):
    return own, hop(own, NEAR), hop(own, FAR)


def last_hops(own, near, far):
    mine = [own, near, far, hop(near, FAR)]
    return mine + [hop(item, TWIN) for item in mine]


def gather_blocks(own):
    return last_hops(*first_hops(own))


def fold_twin(keep, other):
    return keep[:2] + other[:2], keep[2:] + other[2:]


def fold_far(stay, other):
    return stay[0] + other[0], stay[1] + other[1]


def trade(value, bit):
    return lax.ppermute(value, "dp", [(i, i ^ bit) for i in range(4)])


def cut(value, bit):
    high = (lax.axis_index("dp") & bit) // bit
    halves = value.reshape((2, value.shape[0] // 2) + value.shape[1:])
    return (
        lax.dynamic_index_in_dim(halves, high, 0, keepdims=False),
        lax.dynamic_index_in_dim(halves, 1 - high, 0, keepdims=False),
    )


def paste(mine, other, bit):
    high = (lax.axis_index("dp") & bit) != 0
    return jnp.concatenate([jnp.where(high, other, mine), jnp.where(high, mine, other)], axis=0)


def shift(value, step):
    return lax.ppermute(value, "dp", [(i, (i + step) % 4) for i in range(4)])


def line_pieces(value):
    quarters = value.reshape((4, value.shape[0] // 4) + value.shape[1:])
    at = lax.axis_index("dp")

    def piece(step):
        return lax.dynamic_index_in_dim(quarters, (at + step) % 4, 0, keepdims=False)

    return piece(0), [shift(piece(step), step) for step in (1, 2, 3)]


def line_share(kept, others):
    total = kept + others[0] + others[1] + others[2]
    return [total] + [shift(total, step) for step in (1, 2, 3)]


def line_join(found):
    at = lax.axis_index("dp")
    parts = []
    for q in range(4):
        back = (at - q) % 4
        part = found[0]
        for step in (1, 2, 3):
            part = jnp.where(back == step, found[step], part)
        parts.append(part)
    return jnp.concatenate(parts, axis=0)


def pack_kernel(shapes, *refs):
    items, out_ref, sem = refs[: len(shapes) + 3], refs[-2], refs[-1]
    rows = items[0].shape[0]
    copies = [
        pltpu.make_async_copy(items[j], out_ref.at[pl.ds(j * rows, rows), :], sem.at[j])
        for j in range(3)
    ]
    for copy in copies:
        copy.start()
    spot = 0
    out_ref[3 * rows :, :] = jnp.zeros((16, out_ref.shape[1]), BF)
    for item, count in zip(items[3:], shapes):
        for i in range(count):
            row, lane = 3 * rows + spot // 8, spot % 8 * 128
            out_ref[row : row + 1, lane : lane + 128] = item[i : i + 1, :]
            spot += 1
    for copy in copies:
        copy.wait()


def pack(weights, vectors):
    rows, columns = weights[0].shape
    vectors = [item.reshape(-1, 128) for item in vectors]
    return pl.pallas_call(
        partial(pack_kernel, tuple(item.shape[0] for item in vectors)),
        out_shape=jax.ShapeDtypeStruct((3 * rows + 16, columns), BF),
        in_specs=[pl.BlockSpec(memory_space=pltpu.HBM)] * 3
        + [pl.BlockSpec(memory_space=pltpu.VMEM)] * len(vectors),
        out_specs=pl.BlockSpec(memory_space=pltpu.VMEM),
        scratch_shapes=[pltpu.SemaphoreType.DMA((3,))],
        cost_estimate=BRIEF,
    )(*weights, *vectors)


def grad_kernel(first, order_ref, left_ref, right_ref, out_ref, turned):
    rows = out_ref.shape[1]

    @pl.when(pl.program_id(0) == 0)
    def _():
        for k in range(4):
            start = pl.multiple_of(order_ref[first + k] * rows, rows)
            turned[k * rows : (k + 1) * rows, :] = left_ref[:, pl.ds(start, rows)].T

    found = dot(turned[...], right_ref[...])
    for k in range(4):
        out_ref[k] = found[k * rows : (k + 1) * rows].astype(BF)


def grad_blocks(order, first, left, right, tile):
    depth, rows, columns = left.shape[0], left.shape[1] // 8, right.shape[1]
    return pl.pallas_call(
        partial(grad_kernel, first),
        grid_spec=pltpu.PrefetchScalarGridSpec(
            num_scalar_prefetch=1,
            grid=(columns // tile,),
            in_specs=[
                pl.BlockSpec((depth, 8 * rows), lambda i, n: (0, 0)),
                pl.BlockSpec((depth, tile), lambda i, n: (0, i)),
            ],
            out_specs=pl.BlockSpec((4, rows, tile), lambda i, n: (0, 0, i)),
            scratch_shapes=[pltpu.VMEM((4 * rows, depth), left.dtype)],
        ),
        out_shape=jax.ShapeDtypeStruct((4, rows, columns), BF),
        compiler_params=pltpu.CompilerParams(vmem_limit_bytes=VMEM_LIMIT),
        cost_estimate=BRIEF,
    )(order, left, right)


def turned_kernel(order_ref, left_ref, right_ref, out_ref, turned):
    @pl.when(pl.program_id(0) == 0)
    def _():
        turned[...] = right_ref[...].T

    out_ref[0] = dot(turned[...], left_ref[...]).astype(BF)


def turned_blocks(order, first, left, right):
    depth, rows, columns = left.shape[0], left.shape[1] // 8, right.shape[1]
    return pl.pallas_call(
        turned_kernel,
        grid_spec=pltpu.PrefetchScalarGridSpec(
            num_scalar_prefetch=1,
            grid=(4,),
            in_specs=[
                pl.BlockSpec((depth, rows), lambda i, n: (0, n[first + i])),
                pl.BlockSpec((depth, columns), lambda i, n: (0, 0)),
            ],
            out_specs=pl.BlockSpec((1, columns, rows), lambda i, n: (i, 0, 0)),
            scratch_shapes=[pltpu.VMEM((columns, depth), left.dtype)],
        ),
        out_shape=jax.ShapeDtypeStruct((4, columns, rows), BF),
        compiler_params=pltpu.CompilerParams(vmem_limit_bytes=VMEM_LIMIT),
        cost_estimate=BRIEF,
    )(order, left, right)


def tables_kernel(position_ref, box_ref, lookup_ref, slide_ref):
    row = lax.broadcasted_iota(jnp.int32, (NB, NB), 0)
    lane = lax.broadcasted_iota(jnp.int32, (NB, NB), 1)
    same = (row < 64) == (lane < 64)
    for head in range(HEADS):
        base = jnp.broadcast_to(position_ref[head : head + 1, :], (PAGE, 2 * PAGE))
        slid = pltpu.roll(base, 0, 1, stride=1, stride_axis=0)
        half = (head % 2) * PAGE
        slide_ref[head // 2, :, half : half + PAGE] = slid[:, :PAGE]
        left = jnp.broadcast_to(box_ref[0, head : head + 1, :], (64, NB))
        top = jnp.broadcast_to(box_ref[1, head : head + 1, :], (64, NB))
        slid = pltpu.roll(
            jnp.concatenate([left, top], axis=0), 0, 1, stride=1, stride_axis=0
        )
        lookup_ref[:, head * NB : (head + 1) * NB] = jnp.where(same, slid, 0.0).astype(BF)


def make_tables(table):
    spot = np.zeros((2 * PAGE, NB), np.float32)
    for m in range(2 * PAGE):
        offset = -m if m <= PAGE else 2 * PAGE - m
        spot[m, min(max(offset, -64), 63) + 64] = 1.0
    position = lax.dot_general(
        table[0], jnp.asarray(spot, BF), (((0,), (1,)), ((), ())), preferred_element_type=F32
    )
    box = jnp.roll(table[1:].astype(F32).transpose(0, 2, 1), 64, axis=2)
    return pl.pallas_call(
        tables_kernel,
        out_shape=(
            jax.ShapeDtypeStruct((NB, HEADS * NB), BF),
            jax.ShapeDtypeStruct((PAIRS, PAGE, 2 * PAGE), F32),
        ),
    )(position, box)


def split_heads(tile):
    lane = lax.broadcasted_iota(jnp.int32, tile.shape, 1)
    zero = jnp.zeros_like(tile)
    return jnp.concatenate(
        [jnp.where(lane < HEAD_DIM, tile, zero), jnp.where(lane >= HEAD_DIM, tile, zero)],
        axis=0,
    )


def join_heads(tall):
    lane = lax.broadcasted_iota(jnp.int32, (PAGE, NB), 1)
    return jnp.where(lane < HEAD_DIM, tall[:PAGE, :NB], tall[PAGE:, :NB])


def attend_kernel(
    length_ref, q_ref, k_ref, v_ref, box_ref, lookup_ref, slide_ref, context_ref, prob_ref, logit
):
    length = length_ref[pl.program_id(0)]
    inside = lax.broadcasted_iota(jnp.int32, (PAGE, 2 * PAGE), 0) < length
    boxes = box_ref[...]
    for pair in range(PAIRS):
        at = slice(pair * NB, (pair + 1) * NB)
        looked = dot(boxes, lookup_ref[:, 2 * pair * NB : 2 * (pair + 1) * NB]).astype(BF)
        looked = jnp.concatenate([looked[:, :NB], looked[:, NB:]], axis=0)
        asked = jnp.concatenate([split_heads(q_ref[:, at]), looked], axis=1)
        offered = jnp.concatenate([k_ref[:, at], boxes], axis=1)
        logit[pair] = dot(offered, asked, NT)
    for pair in range(PAIRS):
        logits = jnp.where(inside, logit[pair] + slide_ref[pair], BLOCKED)
        peak = jnp.max(logits, axis=0, keepdims=True)
        grown = jnp.exp(logits - peak)
        total = jnp.sum(grown, axis=0, keepdims=True)
        prob_ref[0, pair] = (grown * (1.0 / total)).astype(BF)
    for pair in range(PAIRS):
        at = slice(pair * NB, (pair + 1) * NB)
        context_ref[:, at] = join_heads(dot(prob_ref[0, pair], v_ref[:, at], TN)).astype(BF)


def attend(lengths, queries, keys, values, boxes, lookup, slide):
    wide = pl.BlockSpec((PAGE, HEADS * HEAD_DIM), lambda i, n: (i, 0))
    return pl.pallas_call(
        attend_kernel,
        grid_spec=pltpu.PrefetchScalarGridSpec(
            num_scalar_prefetch=1,
            grid=(PAGES,),
            in_specs=[
                wide,
                wide,
                wide,
                pl.BlockSpec((PAGE, NB), lambda i, n: (i, 0)),
                pl.BlockSpec((NB, HEADS * NB), lambda i, n: (0, 0)),
                pl.BlockSpec((PAIRS, PAGE, 2 * PAGE), lambda i, n: (0, 0, 0)),
            ],
            out_specs=(
                wide,
                pl.BlockSpec((1, PAIRS, PAGE, 2 * PAGE), lambda i, n: (i, 0, 0, 0)),
            ),
            scratch_shapes=[pltpu.VMEM((PAIRS, PAGE, 2 * PAGE), F32)],
        ),
        out_shape=(
            jax.ShapeDtypeStruct((PAGES * PAGE, HEADS * HEAD_DIM), BF),
            jax.ShapeDtypeStruct((PAGES, PAIRS, PAGE, 2 * PAGE), BF),
        ),
        compiler_params=pltpu.CompilerParams(vmem_limit_bytes=VMEM_LIMIT),
        cost_estimate=BRIEF,
    )(lengths, queries, keys, values, boxes, lookup, slide)


def attend_back_kernel(
    q_ref,
    k_ref,
    v_ref,
    g_ref,
    box_ref,
    flip_ref,
    prob_ref,
    grad_ref,
    slide_sum_ref,
    box_sum_ref,
    slide_acc,
    box_acc,
    d_prob,
    d_logit,
    boxed,
):
    page = pl.program_id(0)

    @pl.when(page == 0)
    def _():
        slide_acc[...] = jnp.zeros_like(slide_acc)
        box_acc[...] = jnp.zeros_like(box_acc)

    boxes = box_ref[...]
    width = HEADS * HEAD_DIM
    scale = HEAD_DIM ** (-0.5)
    for pair in range(PAIRS):
        at = slice(pair * NB, (pair + 1) * NB)
        pulled = split_heads(g_ref[:, at])
        d_prob[pair] = dot(v_ref[:, at], pulled, NT)
        grad_ref[:, 2 * width + pair * NB : 2 * width + (pair + 1) * NB] = dot(
            prob_ref[0, pair], pulled
        ).astype(BF)
    for pair in range(PAIRS):
        prob = prob_ref[0, pair].astype(F32)
        inner = jnp.sum(prob * d_prob[pair], axis=0, keepdims=True)
        found = prob * (d_prob[pair] - inner)
        slide_acc[pair] += found
        d_logit[pair] = found.astype(BF)
    for pair in range(PAIRS):
        at = slice(pair * NB, (pair + 1) * NB)
        offered = jnp.concatenate([k_ref[:, at], boxes], axis=1)
        back = dot(d_logit[pair], offered, TN)
        grad_ref[:, at] = (join_heads(back) * scale).astype(BF)
        grad_ref[:, width + pair * NB : width + (pair + 1) * NB] = dot(
            d_logit[pair], split_heads(q_ref[:, at])
        ).astype(BF)
        tall = back[:, NB:].astype(BF)
        boxed[:, 2 * pair * NB : 2 * (pair + 1) * NB] = jnp.concatenate(
            [tall[:PAGE], tall[PAGE:]], axis=1
        )
    box_acc[...] += dot(flip_ref[...], boxed[...])

    @pl.when(page == PAGES - 1)
    def _():
        row = lax.broadcasted_iota(jnp.int32, (NB, NB), 0)
        lane = lax.broadcasted_iota(jnp.int32, (NB, NB), 1)
        mirror = (row + lane == NB - 1).astype(BF)
        same = (row < 64) == (lane >= 64)
        for head in range(HEADS):
            half = (head % 2) * PAGE
            block = slide_acc[head // 2, :, half : half + PAGE]
            high = block.astype(BF)
            low = (block - high.astype(F32)).astype(BF)
            block = dot(mirror, high) + dot(mirror, low)
            block = jnp.concatenate([block, jnp.zeros_like(block)], axis=1)
            slid = pltpu.roll(block, 0, 1, stride=1, stride_axis=0)
            slide_sum_ref[head : head + 1, :] = jnp.sum(slid, axis=0, keepdims=True)
            block = jnp.where(same, box_acc[:, head * NB : (head + 1) * NB], 0.0)
            slid = pltpu.roll(block, 0, 1, stride=1, stride_axis=0)
            box_sum_ref[1, head : head + 1, :] = jnp.sum(slid[:64], axis=0, keepdims=True)
            box_sum_ref[0, head : head + 1, :] = jnp.sum(slid[64:], axis=0, keepdims=True)


def attend_back(queries, keys, values, d_context, boxes, flipped, prob):
    width = HEADS * HEAD_DIM
    wide = pl.BlockSpec((PAGE, width), lambda i: (i, 0))
    return pl.pallas_call(
        attend_back_kernel,
        grid=(PAGES,),
        in_specs=[
            wide,
            wide,
            wide,
            wide,
            pl.BlockSpec((PAGE, NB), lambda i: (i, 0)),
            pl.BlockSpec((NB, PAGE), lambda i: (0, i)),
            pl.BlockSpec((1, PAIRS, PAGE, 2 * PAGE), lambda i: (i, 0, 0, 0)),
        ],
        out_specs=(
            pl.BlockSpec((PAGE, 3 * width), lambda i: (i, 0)),
            pl.BlockSpec((HEADS, 2 * PAGE), lambda i: (0, 0)),
            pl.BlockSpec((2, HEADS, NB), lambda i: (0, 0, 0)),
        ),
        out_shape=(
            jax.ShapeDtypeStruct((PAGES * PAGE, 3 * width), BF),
            jax.ShapeDtypeStruct((HEADS, 2 * PAGE), F32),
            jax.ShapeDtypeStruct((2, HEADS, NB), F32),
        ),
        scratch_shapes=[
            pltpu.VMEM((PAIRS, PAGE, 2 * PAGE), F32),
            pltpu.VMEM((NB, HEADS * NB), F32),
            pltpu.VMEM((PAIRS, PAGE, 2 * PAGE), F32),
            pltpu.VMEM((PAIRS, PAGE, 2 * PAGE), BF),
            pltpu.VMEM((PAGE, HEADS * NB), BF),
        ],
        compiler_params=pltpu.CompilerParams(vmem_limit_bytes=VMEM_LIMIT),
        cost_estimate=BRIEF,
    )(queries, keys, values, d_context, boxes, flipped, prob)


def fold_sums(slide_sum, box_sum):
    spot = np.zeros((2 * PAGE, NB), np.float32)
    for c in range(2 * PAGE - 1):
        spot[c, min(max(PAGE - 1 - c, -64), 63) + 64] = 1.0
    position = lax.dot_general(
        slide_sum,
        jnp.asarray(spot),
        (((1,), (0,)), ((), ())),
        precision=lax.Precision.HIGHEST,
        preferred_element_type=F32,
    )
    box = jnp.roll(box_sum, 65, axis=2)
    return jnp.concatenate([position[None], box], axis=0).transpose(0, 2, 1)


ROWS_AT_ONCE = 32
Q_BIAS, V_BIAS, O_BIAS, GAIN1, SHIFT1, I_BIAS, U_BIAS, GAIN2, SHIFT2 = range(9)
SPOTS = (0, 1, 2, 3, 4, 5, 9, 10, 11)
TABLE_SPOT = 12


def lanes(order_ref, k, size):
    return pl.ds(pl.multiple_of(order_ref[k] * size, size), size)


def fetch(blocks, held, sem):
    copies = [
        pltpu.make_async_copy(blocks[k], held.at[k], sem.at[k]) for k in range(len(blocks))
    ]
    for copy in copies:
        copy.start()
    return copies


def norm_parts(values):
    center = jnp.mean(values, axis=-1, keepdims=True)
    centered = values - center
    spread = lax.rsqrt(jnp.mean(centered * centered, axis=-1, keepdims=True) + EPSILON)
    return centered * spread, spread


def norm_back(normed, spread, pulled):
    level = jnp.mean(pulled, axis=-1, keepdims=True)
    slope = jnp.mean(pulled * normed, axis=-1, keepdims=True)
    return spread * (pulled - level - normed * slope)


def fold_rows(values):
    return jnp.sum(values.reshape(-1, 8, values.shape[-1]), axis=0)


def run(kernel, shapes, order, ins, blocks, scratch):
    return pl.pallas_call(
        kernel,
        out_shape=tuple(jax.ShapeDtypeStruct(shape, kind) for shape, kind in shapes),
        in_specs=[pl.BlockSpec(memory_space=pltpu.SMEM)]
        + [pl.BlockSpec(memory_space=pltpu.VMEM)] * len(ins)
        + [pl.BlockSpec(memory_space=pltpu.HBM)] * len(blocks),
        out_specs=(pl.BlockSpec(memory_space=pltpu.VMEM),) * len(shapes),
        scratch_shapes=scratch,
        compiler_params=pltpu.CompilerParams(vmem_limit_bytes=VMEM_LIMIT),
        cost_estimate=BRIEF,
    )(order, *ins, *blocks)


def project_kernel(order_ref, x_ref, *refs):
    blocks = refs[:8]
    q_ref, k_ref, v_ref, vector_ref, table_ref, held, sem = refs[8:]
    copies = fetch(blocks, held, sem)
    x = jnp.concatenate([x_ref[:, lanes(order_ref, k, 128)] for k in range(8)], axis=1)
    for copy in copies:
        copy.wait()
    rows = (held.shape[1] - 16) // 3

    def piece(k, spot):
        return held[k, pl.ds(3 * rows, 16), pl.ds(spot % 8 * 128, 128)].astype(F32)[
            spot // 8 : spot // 8 + 1
        ]

    for k in range(8):
        for i, spot in enumerate(SPOTS):
            if i == I_BIAS:
                for part in range(4):
                    at = pl.multiple_of(order_ref[k] * 512 + part * 128, 128)
                    vector_ref[i : i + 1, pl.ds(at, 128)] = piece(k, spot + part)
            else:
                vector_ref[i : i + 1, lanes(order_ref, k, 128)] = piece(k, spot)
        for part in range(6):
            table_ref[order_ref[k], :, part * 128 : (part + 1) * 128] = piece(
                k, TABLE_SPOT + part
            )
    width = q_ref.shape[1]
    half = width // 2
    for j, out_ref in enumerate((k_ref, q_ref, v_ref)):
        j = (1, 0, 2)[j]
        for part in range(2):
            at = slice(part * half, (part + 1) * half)
            weight = jnp.concatenate(
                [held[k, j * rows : (j + 1) * rows, at] for k in range(8)], axis=0
            )
            found = dot(x, weight)
            if j == 0:
                found = (found + vector_ref[Q_BIAS : Q_BIAS + 1, at]) * HEAD_DIM ** (-0.5)
            if j == 2:
                found = found + vector_ref[V_BIAS : V_BIAS + 1, at]
            out_ref[:, at] = found.astype(BF)


def project(order, x, blocks):
    count, width = x.shape
    return run(
        project_kernel,
        [((count, width), BF)] * 3 + [((16, 4 * width), F32), ((8, 1, 768), F32)],
        order,
        [x],
        blocks,
        [pltpu.VMEM((8,) + blocks[0].shape, BF), pltpu.SemaphoreType.DMA((8,))],
    )


def output_kernel(order_ref, c_ref, spread_ref, hidden_ref, vector_ref, *refs):
    blocks = refs[:8]
    context_ref, normed_ref, deviation_ref, low_ref, held, sem = refs[8:]
    copies = fetch(blocks, held, sem)
    context_ref[...] = dot(spread_ref[...], c_ref[...]).astype(BF)
    x = jnp.concatenate([context_ref[:, lanes(order_ref, k, 128)] for k in range(8)], axis=1)
    for copy in copies:
        copy.wait()
    width = hidden_ref.shape[1]
    normed_ref[...] = dot(x, held[...].reshape(-1, width))
    bias = vector_ref[O_BIAS : O_BIAS + 1, :width]
    gain = vector_ref[GAIN1 : GAIN1 + 1, :width]
    offset = vector_ref[SHIFT1 : SHIFT1 + 1, :width]
    for c in range(hidden_ref.shape[0] // ROWS_AT_ONCE):
        at = slice(c * ROWS_AT_ONCE, (c + 1) * ROWS_AT_ONCE)
        normed, deviation = norm_parts(hidden_ref[at].astype(F32) + (normed_ref[at] + bias))
        normed_ref[at] = normed
        deviation_ref[at] = deviation
        low_ref[at] = (normed * gain + offset).astype(BF)


def output_block(order, context, spread, hidden, vectors, blocks):
    count, width = hidden.shape
    return run(
        output_kernel,
        [((count, width), BF), ((count, width), F32), ((count, 1), F32), ((count, width), BF)],
        order,
        [context, spread, hidden, vectors],
        blocks,
        [pltpu.VMEM((8,) + blocks[0].shape, BF), pltpu.SemaphoreType.DMA((8,))],
    )


def inner_kernel(tiles, order_ref, x_ref, vector_ref, *refs):
    blocks = refs[:8]
    active_ref, steep_ref, held, first, second, sem = refs[8:]
    rows = blocks[0].shape[0]
    size = active_ref.shape[1] // tiles
    copies = []
    for t in range(tiles):
        at = slice(t * size, (t + 1) * size)
        copies.append(
            [
                pltpu.make_async_copy(
                    blocks[k].at[:, at], held.at[pl.ds(k * rows, rows), at], sem.at[t, k]
                )
                for k in range(8)
            ]
        )
        for copy in copies[-1]:
            copy.start()
    x = jnp.concatenate([x_ref[:, lanes(order_ref, k, 128)] for k in range(8)], axis=1)
    halves = (first, second)

    def bend(t):
        source = halves[t % 2]
        at = slice(t * size, (t + 1) * size)
        bias = vector_ref[I_BIAS : I_BIAS + 1, at]
        for c in range(x_ref.shape[0] // ROWS_AT_ONCE):
            row = slice(c * ROWS_AT_ONCE, (c + 1) * ROWS_AT_ONCE)
            inner = source[row] + bias
            share = 0.5 + 0.5 * lax.erf(inner * 0.5**0.5)
            active_ref[row, at] = (inner * share).astype(BF)
            steep_ref[row, at] = (
                share + inner * jnp.exp(-0.5 * inner * inner) * (2 * np.pi) ** -0.5
            ).astype(BF)

    for t in range(tiles):
        for copy in copies[t]:
            copy.wait()
        halves[t % 2][...] = dot(x, held[:, t * size : (t + 1) * size])
        if t > 0:
            bend(t - 1)
    bend(tiles - 1)


def inner_block(order, x, vectors, blocks, tiles=8):
    count, width = x.shape
    wide = blocks[0].shape[1]
    return run(
        partial(inner_kernel, tiles),
        [((count, wide), BF), ((count, wide), BF)],
        order,
        [x, vectors],
        blocks,
        [
            pltpu.VMEM((width, wide), BF),
            pltpu.VMEM((count, wide // tiles), F32),
            pltpu.VMEM((count, wide // tiles), F32),
            pltpu.SemaphoreType.DMA((tiles, 8)),
        ],
    )


def outer_kernel(order_ref, a_ref, normed_ref, upstream_ref, vector_ref, *refs):
    blocks = refs[:8]
    out_ref, second_ref, d_outer_ref, sum_ref, held, sem = refs[8:]
    copies = fetch(blocks, held, sem)
    width = out_ref.shape[1]
    rows = blocks[0].shape[0]
    for k in range(8):
        copies[k].wait()
        part = dot(a_ref[:, lanes(order_ref, k, rows)], held[k])
        if k == 0:
            second_ref[...] = part
        else:
            second_ref[...] += part
    gain1 = vector_ref[GAIN1 : GAIN1 + 1, :width]
    shift1 = vector_ref[SHIFT1 : SHIFT1 + 1, :width]
    gain2 = vector_ref[GAIN2 : GAIN2 + 1, :width]
    shift2 = vector_ref[SHIFT2 : SHIFT2 + 1, :width]
    bias = vector_ref[U_BIAS : U_BIAS + 1, :width]
    sums = [jnp.zeros((8, width), F32)] * 3
    for c in range(out_ref.shape[0] // ROWS_AT_ONCE):
        at = slice(c * ROWS_AT_ONCE, (c + 1) * ROWS_AT_ONCE)
        first_out = normed_ref[at] * gain1 + shift1
        normed, deviation = norm_parts(first_out + (second_ref[at] + bias))
        out_ref[at] = (normed * gain2 + shift2).astype(BF)
        upstream = upstream_ref[at].astype(F32)
        d_second = norm_back(normed, deviation, upstream * gain2)
        second_ref[at] = d_second
        low = d_second.astype(BF)
        d_outer_ref[at] = low
        sums[0] = sums[0] + fold_rows(upstream * normed)
        sums[1] = sums[1] + fold_rows(upstream)
        sums[2] = sums[2] + fold_rows(low.astype(F32))
    for i in range(3):
        sum_ref[i : i + 1, :] = jnp.sum(sums[i], axis=0, keepdims=True)


def outer_block(order, active, normed, upstream, vectors, blocks):
    count, width = normed.shape
    return run(
        outer_kernel,
        [((count, width), BF), ((count, width), F32), ((count, width), BF), ((8, width), F32)],
        order,
        [active, normed, upstream, vectors],
        blocks,
        [pltpu.VMEM((8,) + blocks[0].shape, BF), pltpu.SemaphoreType.DMA((8,))],
    )


def inner_back_kernel(order_ref, d_ref, steep_ref, *refs):
    blocks = refs[:8]
    out_ref, sum_ref, held, sem = refs[8:]
    copies = fetch(blocks, held, sem)
    rows = blocks[0].shape[0]
    for k in range(8):
        copies[k].wait()
        at = lanes(order_ref, k, rows)
        low = (dot(d_ref[...], held[k], NT) * steep_ref[:, at].astype(F32)).astype(BF)
        out_ref[:, at] = low
        sum_ref[:, at] = fold_rows(low.astype(F32))


def inner_back(order, d_outer, steep, blocks):
    count, wide = steep.shape
    return run(
        inner_back_kernel,
        [((count, wide), BF), ((8, wide), F32)],
        order,
        [d_outer, steep],
        blocks,
        [pltpu.VMEM((8,) + blocks[0].shape, BF), pltpu.SemaphoreType.DMA((8,))],
    )


def first_back_kernel(
    order_ref, d_ref, second_ref, normed_ref, deviation_ref, vector_ref, *refs
):
    blocks = refs[:8]
    summed_ref, low_ref, sum_ref, held, sem = refs[8:]
    copies = fetch(blocks, held, sem)
    width = summed_ref.shape[1]
    for k in range(0, 8, 2):
        copies[k].wait()
        copies[k + 1].wait()
        weight = jnp.concatenate([held[k], held[k + 1]], axis=0)
        part = dot(d_ref[...], weight, NT)
        rows = part.shape[1] // 2
        summed_ref[:, lanes(order_ref, k, rows)] = part[:, :rows]
        summed_ref[:, lanes(order_ref, k + 1, rows)] = part[:, rows:]
    gain = vector_ref[GAIN1 : GAIN1 + 1, :width]
    sums = [jnp.zeros((8, width), F32)] * 3
    for c in range(summed_ref.shape[0] // ROWS_AT_ONCE):
        at = slice(c * ROWS_AT_ONCE, (c + 1) * ROWS_AT_ONCE)
        d_first = second_ref[at] + summed_ref[at]
        normed = normed_ref[at]
        d_summed = norm_back(normed, deviation_ref[at], d_first * gain)
        summed_ref[at] = d_summed
        low = d_summed.astype(BF)
        low_ref[at] = low
        sums[0] = sums[0] + fold_rows(d_first * normed)
        sums[1] = sums[1] + fold_rows(d_first)
        sums[2] = sums[2] + fold_rows(low.astype(F32))
    for i in range(3):
        sum_ref[i : i + 1, :] = jnp.sum(sums[i], axis=0, keepdims=True)


def first_back(order, d_inner, d_second, normed, deviation, vectors, blocks):
    count, width = normed.shape
    return run(
        first_back_kernel,
        [((count, width), F32), ((count, width), BF), ((8, width), F32)],
        order,
        [d_inner, d_second, normed, deviation, vectors],
        blocks,
        [pltpu.VMEM((8,) + blocks[0].shape, BF), pltpu.SemaphoreType.DMA((8,))],
    )


def context_back_kernel(order_ref, d_ref, spread_ref, *refs):
    blocks = refs[:8]
    out_ref, held, kept, sem = refs[8:]
    copies = fetch(blocks, held, sem)
    rows = blocks[0].shape[0]
    for copy in copies:
        copy.wait()
    for k in range(0, 8, 2):
        weight = jnp.concatenate([held[k], held[k + 1]], axis=0)
        part = dot(d_ref[...], weight, NT).astype(BF)
        kept[:, lanes(order_ref, k, rows)] = part[:, :rows]
        kept[:, lanes(order_ref, k + 1, rows)] = part[:, rows:]
    out_ref[...] = dot(spread_ref[...], kept[...]).astype(BF)


def context_back(order, d_attn, spread, blocks):
    count, width = d_attn.shape
    return run(
        context_back_kernel,
        [((spread.shape[0], width), BF)],
        order,
        [d_attn, spread],
        blocks,
        [
            pltpu.VMEM((8,) + blocks[0].shape, BF),
            pltpu.VMEM((count, width), BF),
            pltpu.SemaphoreType.DMA((8,)),
        ],
    )[0]


def input_back_kernel(order_ref, d_ref, spread_ref, summed_ref, *refs):
    blocks = refs[:8]
    out_ref, sum_ref, held, kept, sem = refs[8:]
    copies = fetch(blocks, held, sem)
    rows = (blocks[0].shape[0] - 16) // 3
    width = out_ref.shape[1]
    for j in range(6):
        at = slice(j * width // 2, (j + 1) * width // 2)
        part = dot(spread_ref[...], d_ref[:, at])
        kept[:, at] = part.astype(BF)
        sum_ref[:, at] = fold_rows(part)
    for copy in copies:
        copy.wait()
    for k in range(0, 8, 2):
        weight = jnp.concatenate(
            [
                jnp.concatenate(
                    [held[k, j * rows : (j + 1) * rows], held[k + 1, j * rows : (j + 1) * rows]],
                    axis=0,
                )
                for j in range(3)
            ],
            axis=1,
        )
        part = dot(kept[...], weight, NT)
        for i in range(2):
            at = lanes(order_ref, k + i, rows)
            out_ref[:, at] = summed_ref[:, at] + part[:, i * rows : (i + 1) * rows]


def input_back(order, d_mixed, spread, d_summed, blocks):
    count, width = d_summed.shape
    return run(
        input_back_kernel,
        [((count, width), F32), ((8, 3 * width), F32)],
        order,
        [d_mixed, spread, d_summed],
        blocks,
        [
            pltpu.VMEM((8,) + blocks[0].shape, BF),
            pltpu.VMEM((count, 3 * width), BF),
            pltpu.SemaphoreType.DMA((8,)),
        ],
    )


def on_device(line, *args):
    (
        hidden_in,
        cotangent,
        segment_ids,
        box_left,
        box_top,
        query_weight,
        query_bias,
        key_weight,
        value_weight,
        value_bias,
        output_weight,
        output_bias,
        first_gain,
        first_shift,
        inner_weight,
        inner_bias,
        outer_weight,
        outer_bias,
        second_gain,
        second_shift,
        bucket_table,
    ) = args
    slot_count = segment_ids.shape[1]
    width = hidden_in.shape[1]
    vectors = (
        query_bias,
        value_bias,
        output_bias,
        first_gain,
        first_shift,
        inner_bias,
        outer_bias,
        second_gain,
        second_shift,
        bucket_table,
    )
    phase = lax.optimization_barrier
    if line:
        order = block_order(lax.axis_index("fsdp"))
        put = (order[None, :] == jnp.arange(8)[:, None]).astype(F32)
        packed = pack((query_weight, key_weight, value_weight), vectors)
        in_blocks = first_hops(packed)
    else:
        order = jnp.arange(8, dtype=jnp.int32)

        def whole(shard):
            return lax.all_gather(shard, "fsdp", axis=0, tiled=True)

        def blocks_of(shard):
            full = whole(shard)
            return list(full.reshape(8, full.shape[0] // 8, full.shape[1]))

        small = jnp.concatenate([whole(item).reshape(8, -1) for item in vectors], axis=1)
        small = jnp.pad(small, ((0, 0), (0, 16 * width - small.shape[1])))
        in_blocks = jnp.concatenate(
            [whole(item).reshape(8, -1, width) for item in (query_weight, key_weight, value_weight)]
            + [small.reshape(8, 16, width)],
            axis=1,
        )
        in_blocks = list(in_blocks)
        output_blocks = blocks_of(output_weight)
        inner_blocks = blocks_of(inner_weight)
        outer_blocks = blocks_of(outer_weight)

    slot = lax.iota(jnp.int32, slot_count)
    pages = lax.iota(jnp.int32, PAGES)
    segments = segment_ids[0]
    member = segments[None, :] == pages[:, None]
    lengths = jnp.sum(member, axis=1, dtype=jnp.int32)
    starts = jnp.sum(segments[None, :] < pages[:, None], axis=1, dtype=jnp.int32)
    start_of = jnp.sum(jnp.where(member, starts[:, None], 0), axis=0)
    target = segments * PAGE + slot - start_of
    padded = lax.iota(jnp.int32, PAGES * PAGE)
    spread = (padded[:, None] == target[None, :]).astype(BF)
    gather = (padded[None, :] == target[:, None]).astype(BF)
    coords = lax.iota(jnp.int32, NB) % 64
    sides = jnp.where(padded[None, :NB] < 64, box_left[0][:, None], box_top[0][:, None])
    boxes = dot(spread, (sides == coords[None, :]).astype(BF)).astype(BF)
    turned = jnp.where(padded[:NB, None] < 64, box_top[0][None, :], box_left[0][None, :])
    turned = (turned == 63 - coords[:, None]).astype(BF)
    flipped = dot(turned, spread, NT).astype(BF)
    hidden = dot(spread, hidden_in).astype(BF)

    if line:
        in_blocks, hidden, boxes, flipped, gather, spread, output_weight = phase(
            (in_blocks, hidden, boxes, flipped, gather, spread, output_weight)
        )
        own, near, far = in_blocks
        both = hop(near, FAR)
        twins = [hop(item, TWIN) for item in (own, near, far)]
        output_blocks = first_hops(output_weight)
        both, twins, output_blocks, inner_weight = phase(
            (both, twins, output_blocks, inner_weight)
        )
        inner_blocks = first_hops(inner_weight)
        output_blocks = last_hops(*output_blocks)
        in_blocks = [own, near, far, both] + twins + [hop(both, TWIN)]
    queries, keys, values, vector, table = project(order, hidden, in_blocks)
    lookup, slide = make_tables(table.reshape(3, NB, HEADS).astype(BF))
    if line:
        queries, keys, values, lookup, slide, inner_blocks, output_blocks, outer_weight = phase(
            (queries, keys, values, lookup, slide, inner_blocks, output_blocks, outer_weight)
        )
        outer_blocks = first_hops(outer_weight)
        inner_both = hop(inner_blocks[1], FAR)
        inner_twins = [hop(item, TWIN) for item in inner_blocks]
    context, prob = attend(lengths, queries, keys, values, boxes, lookup, slide)
    if line:
        context, inner_both, inner_twins, outer_blocks = phase(
            (context, inner_both, inner_twins, outer_blocks)
        )
        inner_blocks = list(inner_blocks) + [inner_both] + inner_twins
        inner_blocks.append(hop(inner_both, TWIN))
        outer_blocks = last_hops(*outer_blocks)
    context, normed, deviation, first_low = output_block(
        order, context, gather, hidden_in, vector, output_blocks
    )
    active, steep = inner_block(order, first_low, vector, inner_blocks)
    layer_out, d_second, d_outer, second_sums = outer_block(
        order, active, normed, cotangent, vector, outer_blocks
    )

    if line:
        send = turned_blocks(order, 4, active, d_outer)
        d_outer, send = phase((d_outer, send))
        keep = turned_blocks(order, 0, active, d_outer)
        stay2, away2 = fold_twin(keep, hop(send, TWIN))
        d_outer, stay2, away2 = phase((d_outer, stay2, away2))
        other2 = hop(away2, FAR)
    d_inner, inner_sums = inner_back(order, d_outer, steep, outer_blocks)
    if line:
        send = grad_blocks(order, 4, first_low, d_inner, 1024)
        d_inner, send, other2 = phase((d_inner, send, other2))
        other1 = hop(send, TWIN)
        stay2, away2 = fold_far(stay2, other2)
        other2 = hop(away2, NEAR)
        keep = grad_blocks(order, 0, first_low, d_inner, 1024)
        stay1, away1 = fold_twin(keep, other1)
        d_inner, stay1, away1, stay2, other2 = phase((d_inner, stay1, away1, stay2, other2))
        other1 = hop(away1, FAR)
        kept2, sent = cut(stay2 + other2, 1)
        other2 = trade(sent, 1)
    d_summed, d_attn, first_sums = first_back(
        order, d_inner, d_second, normed, deviation, vector, inner_blocks
    )
    if line:
        other0 = hop(grad_blocks(order, 4, context, d_attn, 512), TWIN)
        stay0, away0 = fold_twin(grad_blocks(order, 0, context, d_attn, 512), other0)
    d_context = context_back(order, d_attn, spread, output_blocks)
    if line:
        d_context, stay0, away0, stay1, other1, kept2, other2 = phase(
            (d_context, stay0, away0, stay1, other1, kept2, other2)
        )
        stay1, away1 = fold_far(stay1, other1)
        other1 = hop(away1, NEAR)
        other0 = hop(away0, FAR)
        kept2, sent = cut(kept2 + other2, 2)
        other2 = trade(sent, 2)
    d_mixed, slide_sum, box_sum = attend_back(
        queries, keys, values, d_context, boxes, flipped, prob
    )
    if line:
        d_mixed, stay0, other0, stay1, other1, kept2, other2 = phase(
            (d_mixed, stay0, other0, stay1, other1, kept2, other2)
        )
        stay0, away0 = fold_far(stay0, other0)
        other0 = hop(away0, NEAR)
        kept1, sent = cut(stay1 + other1, 1)
        other1 = trade(sent, 1)
        kept2 = kept2 + other2
        other2 = trade(kept2, 2)
        send = grad_blocks(order, 4, hidden, d_mixed, 1024)
        d_mixed, send, stay0, other0, kept1, other1, kept2, other2 = phase(
            (d_mixed, send, stay0, other0, kept1, other1, kept2, other2)
        )
        kept1, sent = cut(kept1 + other1, 2)
        other1 = trade(sent, 2)
        kept2 = paste(kept2, other2, 2)
        other2 = trade(kept2, 1)
        keep = grad_blocks(order, 0, hidden, d_mixed, 1024)
        stay, away = fold_twin(keep, hop(send, TWIN))
        d_mixed, stay, away, stay0, other0, kept1, other1, kept2, other2 = phase(
            (d_mixed, stay, away, stay0, other0, kept1, other1, kept2, other2)
        )
        other = hop(away, FAR)
        kept1 = kept1 + other1
        other1 = trade(kept1, 2)
        pieces = line_pieces(stay0 + other0)
        outer_own = paste(kept2, other2, 1).T.astype(F32)
    input_grad, in_sums = input_back(order, d_mixed, gather, d_summed, in_blocks)
    table_grad = fold_sums(slide_sum, box_sum)
    in_bias_grad = jnp.sum(in_sums, axis=0)
    grads = (
        in_bias_grad[:width],
        in_bias_grad[2 * width :],
        first_sums[2],
        first_sums[0],
        first_sums[1],
        jnp.sum(inner_sums, axis=0),
        second_sums[2],
        second_sums[0],
        second_sums[1],
        table_grad,
    )
    if line:
        small = jnp.concatenate([item.reshape(8, -1) for item in grads], axis=1)
        picked = jnp.einsum("bk,bn->kn", put, small, precision=lax.Precision.HIGHEST)
        picked = picked.reshape(8, -1, 128)
        small_stay, small_away = fold_twin(picked[:4], hop(picked[4:], TWIN))
        small_other = hop(small_away, FAR)
        stay, other, input_grad, small_stay, small_other, kept1, other1, pieces, outer_own = phase(
            (stay, other, input_grad, small_stay, small_other, kept1, other1, pieces, outer_own)
        )
        stay, away = fold_far(stay, other)
        other = hop(away, NEAR)
        small_stay, small_away = fold_far(small_stay, small_other)
        small_other = hop(small_away, NEAR)
        kept1 = paste(kept1, other1, 2)
        other1 = trade(kept1, 1)
        found = line_share(*pieces)
        stay, other, small_stay, small_other, kept1, other1, found = phase(
            (stay, other, small_stay, small_other, kept1, other1, found)
        )
        small = small_stay + small_other
        small_other = trade(small, 1)
        pieces = line_pieces(stay + other)
        inner_own = paste(kept1, other1, 1).astype(F32)
        output_own = line_join(found)
        small, small_other, pieces, inner_own, output_own = phase(
            (small, small_other, pieces, inner_own, output_own)
        )
        in_own = line_join(line_share(*pieces))
        small = small + small_other
        small = (small + trade(small, 2)).reshape(-1)
        cuts = np.cumsum([0] + [item.shape[0] for item in vectors])
        owned = [small[cuts[i] : cuts[i + 1]] for i in range(len(vectors))]
    else:

        def reduce(value):
            value = lax.psum_scatter(value, "fsdp", scatter_dimension=0, tiled=True)
            return lax.psum(value, "dp")

        owned = [reduce(item.reshape(-1)) for item in grads]
        outer_own = reduce(dot(active, d_outer, TN).astype(BF))
        inner_own = reduce(dot(first_low, d_inner, TN).astype(BF))
        output_own = reduce(dot(context, d_attn, TN).astype(BF))
        in_own = reduce(dot(hidden, d_mixed, TN).astype(BF))
    in_own = in_own.astype(F32)
    return (
        layer_out,
        input_grad,
        in_own[:, :width],
        owned[0],
        in_own[:, width : 2 * width],
        in_own[:, 2 * width :],
        owned[1],
        output_own.astype(F32),
        owned[2],
        owned[3],
        owned[4],
        inner_own.astype(F32),
        owned[5],
        outer_own.astype(F32),
        owned[6],
        owned[7],
        owned[8],
        owned[9],
    )


def solution(mesh):
    line = mesh.shape["fsdp"] == 8 and mesh.shape["dp"] == 4
    both, across, flat = P(("fsdp", "dp"), None), P("fsdp", None), P("fsdp")
    return jax.shard_map(
        partial(on_device, line),
        mesh=mesh,
        in_specs=(both,) * 5
        + (across, flat, across, across, flat, across, flat, flat, flat)
        + (across, flat, across, flat, flat, flat, flat),
        out_specs=(both, both)
        + (across, flat, across, across, flat, across, flat, flat, flat)
        + (across, flat, across, flat, flat, flat, flat),
        check_vma=False,
    )
```

```python
from functools import partial

import jax
import jax.numpy as jnp
import numpy as np
from jax import lax
from jax.experimental import pallas as pl
from jax.experimental.pallas import tpu as pltpu
from jax.sharding import PartitionSpec as P

HEADS = 16
HEAD_DIM = 64
PAIRS = HEADS // 2
NB = 128
PAGE = 128
PAGES = 8
EPSILON = 1e-05
BLOCKED = -1e30
BF = jnp.bfloat16
F32 = jnp.float32
VMEM_LIMIT = 62 * 1024 * 1024
SCALE = 0.0


def cost(microseconds):
    return pl.CostEstimate(
        flops=1, bytes_accessed=1 + int(microseconds * SCALE * 3e6), transcendentals=0
    )


NT = (((1,), (1,)), ((), ()))
TN = (((0,), (0,)), ((), ()))


def dot(left_side, right_side, dims=(((1,), (0,)), ((), ()))):
    return lax.dot_general(left_side, right_side, dims, preferred_element_type=F32)


def flips(bit_of):
    return [(i, i ^ bit_of(i & 1)) for i in range(8)]


NEAR = flips(lambda c: 2 if c else 4)
FAR = flips(lambda c: 4 if c else 2)
TWIN = flips(lambda c: 1)


def block_order(me):
    rel0 = np.array([0, 4, 2, 6, 1, 3, 5, 7], np.int32)
    rel1 = np.array([0, 2, 4, 6, 1, 5, 3, 7], np.int32)
    rel = jnp.where((me & 1) == 0, rel0, rel1)
    return jnp.bitwise_xor(me, rel).astype(jnp.int32)


def hop(value, pairs):
    return lax.ppermute(value, "fsdp", pairs)


def after(value, *others):
    return lax.optimization_barrier((value,) + others)[0]


def fold_far(stay, other):
    return stay[0] + other[0], stay[1] + other[1]


def trade(value, bit):
    return lax.ppermute(value, "dp", [(i, i ^ bit) for i in range(4)])


def cut(value, bit):
    high = (lax.axis_index("dp") & bit) // bit
    halves = value.reshape((2, value.shape[0] // 2) + value.shape[1:])
    return (
        lax.dynamic_index_in_dim(halves, high, 0, keepdims=False),
        lax.dynamic_index_in_dim(halves, 1 - high, 0, keepdims=False),
    )


def paste(mine, other, bit):
    high = (lax.axis_index("dp") & bit) != 0
    return jnp.concatenate([jnp.where(high, other, mine), jnp.where(high, mine, other)], axis=0)


def pack_kernel(shapes, *refs):
    items, out_ref, sem = refs[: len(shapes) + 3], refs[-2], refs[-1]
    rows = items[0].shape[0]
    copies = [
        pltpu.make_async_copy(items[j], out_ref.at[pl.ds(j * rows, rows), :], sem.at[j])
        for j in range(3)
    ]
    for copy in copies:
        copy.start()
    spot = 0
    out_ref[3 * rows :, :] = jnp.zeros((16, out_ref.shape[1]), BF)
    for item, count in zip(items[3:], shapes):
        for i in range(count):
            row, lane = 3 * rows + spot // 8, spot % 8 * 128
            out_ref[row : row + 1, lane : lane + 128] = item[i : i + 1, :]
            spot += 1
    for copy in copies:
        copy.wait()


def pack(weights, vectors):
    rows, columns = weights[0].shape
    vectors = [item.reshape(-1, 128) for item in vectors]
    return pl.pallas_call(
        partial(pack_kernel, tuple(item.shape[0] for item in vectors)),
        out_shape=jax.ShapeDtypeStruct((3 * rows + 16, columns), BF),
        in_specs=[pl.BlockSpec(memory_space=pltpu.HBM)] * 3
        + [pl.BlockSpec(memory_space=pltpu.VMEM)] * len(vectors),
        out_specs=pl.BlockSpec(memory_space=pltpu.VMEM),
        scratch_shapes=[pltpu.SemaphoreType.DMA((3,))],
        cost_estimate=cost(3),
    )(*weights, *vectors)


def emit(found, k, others, outs):
    if others:
        outs[k // 2][k % 2] = (found + others[k][...].astype(F32)).astype(BF)
    else:
        outs[k][...] = found.astype(BF)


def turned_kernel(fold, order_ref, left_ref, right_ref, *refs):
    others, outs, turned = refs[: 4 * fold], refs[4 * fold : -1], refs[-1]
    i = pl.program_id(0)

    @pl.when(i == 0)
    def _():
        turned[...] = right_ref[...].T

    found = dot(turned[...], left_ref[...])
    for k in range(4):

        @pl.when(i == k)
        def _():
            emit(found, k, others, outs)


def turned_blocks(order, first, left, right, others=()):
    depth, rows, columns = left.shape[0], left.shape[1] // 8, right.shape[1]
    fold = int(bool(others))
    whole = pl.BlockSpec((columns, rows), lambda i, n: (0, 0))
    if fold:
        out_specs = (pl.BlockSpec((2, columns, rows), lambda i, n: (0, 0, 0)),) * 2
        shapes = (jax.ShapeDtypeStruct((2, columns, rows), BF),) * 2
    else:
        out_specs = (whole,) * 4
        shapes = (jax.ShapeDtypeStruct((columns, rows), BF),) * 4
    return pl.pallas_call(
        partial(turned_kernel, fold),
        grid_spec=pltpu.PrefetchScalarGridSpec(
            num_scalar_prefetch=1,
            grid=(4,),
            in_specs=[
                pl.BlockSpec((depth, rows), lambda i, n: (0, n[first + i])),
                pl.BlockSpec((depth, columns), lambda i, n: (0, 0)),
            ]
            + [whole] * (4 * fold),
            out_specs=out_specs,
            scratch_shapes=[pltpu.VMEM((columns, depth), left.dtype)],
        ),
        out_shape=shapes,
        compiler_params=pltpu.CompilerParams(vmem_limit_bytes=VMEM_LIMIT),
        cost_estimate=cost(7),
    )(order, left, right, *others)


def grad_kernel(first, counts, fold, order_ref, *refs):
    pieces = len(counts)
    lefts, rights = refs[:pieces], refs[pieces : 2 * pieces]
    others = refs[2 * pieces : 2 * pieces + 4 * fold]
    outs, turned = refs[2 * pieces + 4 * fold : -pieces], refs[-pieces:]
    i = pl.program_id(0)
    rows = turned[0].shape[0] // 4
    start = 0
    for left_ref, right_ref, kept, count in zip(lefts, rights, turned, counts):

        @pl.when(i == start)
        def _():
            for k in range(4):
                kept[k * rows : (k + 1) * rows, :] = left_ref[
                    :, lanes(order_ref, first + k, rows)
                ].T

        @pl.when((i >= start) & (i < start + count))
        def _():
            found = dot(kept[...], right_ref[...])
            for k in range(4):
                emit(found[k * rows : (k + 1) * rows], k, others, outs)

        start += count


def grad_blocks(order, first, pairs, tile, others=()):
    rows = pairs[0][0].shape[1] // 8
    counts = [right.shape[1] // tile for _, right in pairs]
    total = sum(counts)
    fold = int(bool(others))
    in_specs = [pl.BlockSpec(left.shape, lambda i, n: (0, 0)) for left, _ in pairs]
    start = 0
    for (_, right), count in zip(pairs, counts):

        def at(i, n, start=start, count=count):
            return 0, jnp.clip(i - start, 0, count - 1)

        in_specs.append(pl.BlockSpec((right.shape[0], tile), at))
        start += count
    one = pl.BlockSpec((rows, tile), lambda i, n: (0, i))
    if fold:
        out_specs = (pl.BlockSpec((2, rows, tile), lambda i, n: (0, 0, i)),) * 2
        shapes = (jax.ShapeDtypeStruct((2, rows, total * tile), BF),) * 2
    else:
        out_specs = (one,) * 4
        shapes = (jax.ShapeDtypeStruct((rows, total * tile), BF),) * 4
    return pl.pallas_call(
        partial(grad_kernel, first, tuple(counts), fold),
        grid_spec=pltpu.PrefetchScalarGridSpec(
            num_scalar_prefetch=1,
            grid=(total,),
            in_specs=in_specs + [one] * (4 * fold),
            out_specs=out_specs,
            scratch_shapes=[pltpu.VMEM((4 * rows, left.shape[0]), BF) for left, _ in pairs],
        ),
        out_shape=shapes,
        compiler_params=pltpu.CompilerParams(vmem_limit_bytes=VMEM_LIMIT),
        cost_estimate=cost(2 * total),
    )(
        order,
        *[left for left, _ in pairs],
        *[right for _, right in pairs],
        *others,
    )


def to_twin(blocks):
    return [hop(block, TWIN) for block in blocks]


def lanes(order_ref, k, size):
    return pl.ds(pl.multiple_of(order_ref[k] * size, size), size)


def one_hot(shape, test):
    row = lax.broadcasted_iota(jnp.int32, shape, 0)
    lane = lax.broadcasted_iota(jnp.int32, shape, 1)
    return test(row, lane)


def precise(left_side, right_side, dims=(((1,), (0,)), ((), ()))):
    return lax.dot_general(
        left_side, right_side, dims, precision=lax.Precision.HIGHEST, preferred_element_type=F32
    )


def tables_kernel(table_ref, lookup_ref, slide_ref, flat):
    for i in range(48):
        flat[i : i + 1, :] = table_ref[i]
    wide = one_hot((NB, 16), lambda r, c: r // 8 == c).astype(F32)
    mine = one_hot((NB, NB), lambda r, c: c // 16 == r % 8)
    heads = one_hot((HEADS, NB), lambda r, c: c % 16 == r).astype(F32)
    by_head = []
    for kind in range(3):
        rows = jnp.where(mine, precise(wide, flat[16 * kind : 16 * (kind + 1), :]), 0.0)
        by_head.append(precise(heads, rows, NT))
    spot = one_hot(
        (2 * PAGE, NB),
        lambda m, bucket: jnp.clip(jnp.where(m <= PAGE, -m, 2 * PAGE - m), -64, 63) + 64 == bucket,
    ).astype(F32)
    position = precise(by_head[0], spot, NT)
    left_all = pltpu.roll(by_head[1], 64, 1)
    top_all = pltpu.roll(by_head[2], 64, 1)
    same = one_hot((NB, NB), lambda r, c: (r < 64) == (c < 64))
    for head in range(HEADS):
        base = jnp.broadcast_to(position[head : head + 1, :], (PAGE, 2 * PAGE))
        slid = pltpu.roll(base, 0, 1, stride=1, stride_axis=0)
        half = (head % 2) * PAGE
        slide_ref[head // 2, :, half : half + PAGE] = slid[:, :PAGE]
        left = jnp.broadcast_to(left_all[head : head + 1, :], (64, NB))
        top = jnp.broadcast_to(top_all[head : head + 1, :], (64, NB))
        slid = pltpu.roll(
            jnp.concatenate([left, top], axis=0), 0, 1, stride=1, stride_axis=0
        )
        lookup_ref[:, head * NB : (head + 1) * NB] = jnp.where(same, slid, 0.0).astype(BF)


def make_tables(table):
    return pl.pallas_call(
        tables_kernel,
        out_shape=(
            jax.ShapeDtypeStruct((NB, HEADS * NB), BF),
            jax.ShapeDtypeStruct((PAIRS, PAGE, 2 * PAGE), F32),
        ),
        scratch_shapes=[pltpu.VMEM((48, NB), F32)],
        compiler_params=pltpu.CompilerParams(vmem_limit_bytes=VMEM_LIMIT),
        cost_estimate=cost(3),
    )(table)


def split_heads(tile):
    lane = lax.broadcasted_iota(jnp.int32, tile.shape, 1)
    zero = jnp.zeros_like(tile)
    return jnp.concatenate(
        [jnp.where(lane < HEAD_DIM, tile, zero), jnp.where(lane >= HEAD_DIM, tile, zero)],
        axis=0,
    )


def join_heads(tall):
    lane = lax.broadcasted_iota(jnp.int32, (PAGE, NB), 1)
    return jnp.where(lane < HEAD_DIM, tall[:PAGE, :NB], tall[PAGE:, :NB])


def attend_kernel(
    length_ref, q_ref, k_ref, v_ref, box_ref, lookup_ref, slide_ref, context_ref, prob_ref, logit
):
    length = length_ref[pl.program_id(0)]
    inside = lax.broadcasted_iota(jnp.int32, (PAGE, 2 * PAGE), 0) < length
    boxes = box_ref[...]
    for pair in range(PAIRS):
        at = slice(pair * NB, (pair + 1) * NB)
        looked = dot(boxes, lookup_ref[:, 2 * pair * NB : 2 * (pair + 1) * NB]).astype(BF)
        looked = jnp.concatenate([looked[:, :NB], looked[:, NB:]], axis=0)
        asked = jnp.concatenate([split_heads(q_ref[:, at]), looked], axis=1)
        offered = jnp.concatenate([k_ref[:, at], boxes], axis=1)
        logit[pair] = dot(offered, asked, NT)
    for pair in range(PAIRS):
        logits = jnp.where(inside, logit[pair] + slide_ref[pair], BLOCKED)
        peak = jnp.max(logits, axis=0, keepdims=True)
        grown = jnp.exp(logits - peak)
        total = jnp.sum(grown, axis=0, keepdims=True)
        prob_ref[0, pair] = (grown * (1.0 / total)).astype(BF)
    for pair in range(PAIRS):
        at = slice(pair * NB, (pair + 1) * NB)
        context_ref[:, at] = join_heads(dot(prob_ref[0, pair], v_ref[:, at], TN)).astype(BF)


def attend(lengths, queries, keys, values, boxes, lookup, slide):
    wide = pl.BlockSpec((PAGE, HEADS * HEAD_DIM), lambda i, n: (i, 0))
    return pl.pallas_call(
        attend_kernel,
        grid_spec=pltpu.PrefetchScalarGridSpec(
            num_scalar_prefetch=1,
            grid=(PAGES,),
            in_specs=[
                wide,
                wide,
                wide,
                pl.BlockSpec((PAGE, NB), lambda i, n: (i, 0)),
                pl.BlockSpec((NB, HEADS * NB), lambda i, n: (0, 0)),
                pl.BlockSpec((PAIRS, PAGE, 2 * PAGE), lambda i, n: (0, 0, 0)),
            ],
            out_specs=(
                wide,
                pl.BlockSpec((1, PAIRS, PAGE, 2 * PAGE), lambda i, n: (i, 0, 0, 0)),
            ),
            scratch_shapes=[pltpu.VMEM((PAIRS, PAGE, 2 * PAGE), F32)],
        ),
        out_shape=(
            jax.ShapeDtypeStruct((PAGES * PAGE, HEADS * HEAD_DIM), BF),
            jax.ShapeDtypeStruct((PAGES, PAIRS, PAGE, 2 * PAGE), BF),
        ),
        compiler_params=pltpu.CompilerParams(vmem_limit_bytes=VMEM_LIMIT),
        cost_estimate=cost(13.5),
    )(lengths, queries, keys, values, boxes, lookup, slide)


def attend_back_kernel(
    q_ref,
    k_ref,
    v_ref,
    g_ref,
    box_ref,
    flip_ref,
    prob_ref,
    grad_ref,
    slide_sum_ref,
    box_sum_ref,
    bias_sum_ref,
    slide_acc,
    box_acc,
    d_prob,
    d_logit,
    boxed,
):
    page = pl.program_id(0)

    @pl.when(page == 0)
    def _():
        slide_acc[...] = jnp.zeros_like(slide_acc)
        box_acc[...] = jnp.zeros_like(box_acc)
        bias_sum_ref[...] = jnp.zeros_like(bias_sum_ref)

    boxes = box_ref[...]
    width = HEADS * HEAD_DIM
    scale = HEAD_DIM ** (-0.5)
    for pair in range(PAIRS):
        at = slice(pair * NB, (pair + 1) * NB)
        pulled = split_heads(g_ref[:, at])
        d_prob[pair] = dot(v_ref[:, at], pulled, NT)
        grad_ref[:, 2 * width + pair * NB : 2 * width + (pair + 1) * NB] = dot(
            prob_ref[0, pair], pulled
        ).astype(BF)
    for pair in range(PAIRS):
        prob = prob_ref[0, pair].astype(F32)
        inner = jnp.sum(prob * d_prob[pair], axis=0, keepdims=True)
        found = prob * (d_prob[pair] - inner)
        slide_acc[pair] += found
        d_logit[pair] = found.astype(BF)
    for pair in range(PAIRS):
        at = slice(pair * NB, (pair + 1) * NB)
        offered = jnp.concatenate([k_ref[:, at], boxes], axis=1)
        back = dot(d_logit[pair], offered, TN)
        grad_ref[:, at] = (join_heads(back) * scale).astype(BF)
        grad_ref[:, width + pair * NB : width + (pair + 1) * NB] = dot(
            d_logit[pair], split_heads(q_ref[:, at])
        ).astype(BF)
        tall = back[:, NB:].astype(BF)
        boxed[:, 2 * pair * NB : 2 * (pair + 1) * NB] = jnp.concatenate(
            [tall[:PAGE], tall[PAGE:]], axis=1
        )
    box_acc[...] += dot(flip_ref[...], boxed[...])
    for part in range(3 * width // 512):
        at = slice(part * 512, (part + 1) * 512)
        bias_sum_ref[:, at] += fold_rows(grad_ref[:, at].astype(F32))

    @pl.when(page == PAGES - 1)
    def _():
        row = lax.broadcasted_iota(jnp.int32, (NB, NB), 0)
        lane = lax.broadcasted_iota(jnp.int32, (NB, NB), 1)
        mirror = (row + lane == NB - 1).astype(BF)
        same = (row < 64) == (lane >= 64)
        for head in range(HEADS):
            half = (head % 2) * PAGE
            block = slide_acc[head // 2, :, half : half + PAGE]
            high = block.astype(BF)
            low = (block - high.astype(F32)).astype(BF)
            block = dot(mirror, high) + dot(mirror, low)
            block = jnp.concatenate([block, jnp.zeros_like(block)], axis=1)
            slid = pltpu.roll(block, 0, 1, stride=1, stride_axis=0)
            slide_sum_ref[head : head + 1, :] = jnp.sum(slid, axis=0, keepdims=True)
            block = jnp.where(same, box_acc[:, head * NB : (head + 1) * NB], 0.0)
            slid = pltpu.roll(block, 0, 1, stride=1, stride_axis=0)
            box_sum_ref[1, head : head + 1, :] = jnp.sum(slid[:64], axis=0, keepdims=True)
            box_sum_ref[0, head : head + 1, :] = jnp.sum(slid[64:], axis=0, keepdims=True)


def attend_back(queries, keys, values, d_context, boxes, flipped, prob):
    width = HEADS * HEAD_DIM
    wide = pl.BlockSpec((PAGE, width), lambda i: (i, 0))
    return pl.pallas_call(
        attend_back_kernel,
        grid=(PAGES,),
        in_specs=[
            wide,
            wide,
            wide,
            wide,
            pl.BlockSpec((PAGE, NB), lambda i: (i, 0)),
            pl.BlockSpec((NB, PAGE), lambda i: (0, i)),
            pl.BlockSpec((1, PAIRS, PAGE, 2 * PAGE), lambda i: (i, 0, 0, 0)),
        ],
        out_specs=(
            pl.BlockSpec((PAGE, 3 * width), lambda i: (i, 0)),
            pl.BlockSpec((HEADS, 2 * PAGE), lambda i: (0, 0)),
            pl.BlockSpec((2, HEADS, NB), lambda i: (0, 0, 0)),
            pl.BlockSpec((8, 3 * width), lambda i: (0, 0)),
        ),
        out_shape=(
            jax.ShapeDtypeStruct((PAGES * PAGE, 3 * width), BF),
            jax.ShapeDtypeStruct((HEADS, 2 * PAGE), F32),
            jax.ShapeDtypeStruct((2, HEADS, NB), F32),
            jax.ShapeDtypeStruct((8, 3 * width), F32),
        ),
        scratch_shapes=[
            pltpu.VMEM((PAIRS, PAGE, 2 * PAGE), F32),
            pltpu.VMEM((NB, HEADS * NB), F32),
            pltpu.VMEM((PAIRS, PAGE, 2 * PAGE), F32),
            pltpu.VMEM((PAIRS, PAGE, 2 * PAGE), BF),
            pltpu.VMEM((PAGE, HEADS * NB), BF),
        ],
        compiler_params=pltpu.CompilerParams(vmem_limit_bytes=VMEM_LIMIT),
        cost_estimate=cost(14),
    )(queries, keys, values, d_context, boxes, flipped, prob)


ROWS_AT_ONCE = 32
Q_BIAS, V_BIAS, O_BIAS, GAIN1, SHIFT1, I_BIAS, U_BIAS, GAIN2, SHIFT2 = range(9)
SPOTS = (0, 1, 2, 3, 4, 5, 9, 10, 11)
TABLE_SPOT = 12


def fetch(blocks, held, sem):
    copies = [
        pltpu.make_async_copy(blocks[k], held.at[k], sem.at[k]) for k in range(len(blocks))
    ]
    for copy in copies:
        copy.start()
    return copies


def norm_parts(values):
    center = jnp.mean(values, axis=-1, keepdims=True)
    centered = values - center
    spread = lax.rsqrt(jnp.mean(centered * centered, axis=-1, keepdims=True) + EPSILON)
    return centered * spread, spread


def norm_back(normed, spread, pulled):
    level = jnp.mean(pulled, axis=-1, keepdims=True)
    slope = jnp.mean(pulled * normed, axis=-1, keepdims=True)
    return spread * (pulled - level - normed * slope)


def fold_rows(values):
    return jnp.sum(values.reshape(-1, 8, values.shape[-1]), axis=0)


def run(length, kernel, shapes, order, ins, blocks, scratch, far=()):
    near_spec = pl.BlockSpec(memory_space=pltpu.VMEM)
    far_spec = pl.BlockSpec(memory_space=pltpu.HBM)
    return pl.pallas_call(
        kernel,
        out_shape=tuple(jax.ShapeDtypeStruct(item[0], item[1]) for item in shapes),
        in_specs=[pl.BlockSpec(memory_space=pltpu.SMEM)]
        + [near_spec] * len(ins)
        + [far_spec] * (len(far) + len(blocks)),
        out_specs=tuple(far_spec if len(item) > 2 else near_spec for item in shapes),
        scratch_shapes=scratch,
        compiler_params=pltpu.CompilerParams(vmem_limit_bytes=VMEM_LIMIT),
        cost_estimate=cost(length),
    )(order, *ins, *far, *blocks)


def begin(source, target, sem):
    copy = pltpu.make_async_copy(source, target, sem)
    copy.start()
    return copy


def finish(copies):
    for copy in copies:
        copy.wait()


def row_groups(count):
    chunks = count // ROWS_AT_ONCE
    edges = sorted({chunks * i // 4 for i in range(5)})
    return [range(low, high) for low, high in zip(edges, edges[1:])]


def project_kernel(order_ref, x_ref, *refs):
    blocks = refs[:8]
    q_ref, k_ref, v_ref, vector_ref, table_ref, held, sem = refs[8:]
    copies = fetch(blocks, held, sem)
    x = jnp.concatenate([x_ref[:, lanes(order_ref, k, 128)] for k in range(8)], axis=1)
    for copy in copies:
        copy.wait()
    rows = (held.shape[1] - 16) // 3

    def piece(k, spot):
        return held[k, pl.ds(3 * rows, 16), pl.ds(spot % 8 * 128, 128)].astype(F32)[
            spot // 8 : spot // 8 + 1
        ]

    for k in range(8):
        for i, spot in enumerate(SPOTS):
            if i == I_BIAS:
                for part in range(4):
                    at = pl.multiple_of(order_ref[k] * 512 + part * 128, 128)
                    vector_ref[i : i + 1, pl.ds(at, 128)] = piece(k, spot + part)
            else:
                vector_ref[i : i + 1, lanes(order_ref, k, 128)] = piece(k, spot)
        for part in range(6):
            table_ref[order_ref[k] * 6 + part] = piece(k, TABLE_SPOT + part)
    width = q_ref.shape[1]
    half = width // 2
    for j, out_ref in enumerate((k_ref, q_ref, v_ref)):
        j = (1, 0, 2)[j]
        for part in range(2):
            at = slice(part * half, (part + 1) * half)
            weight = jnp.concatenate(
                [held[k, j * rows : (j + 1) * rows, at] for k in range(8)], axis=0
            )
            found = dot(x, weight)
            if j == 0:
                found = (found + vector_ref[Q_BIAS : Q_BIAS + 1, at]) * HEAD_DIM ** (-0.5)
            if j == 2:
                found = found + vector_ref[V_BIAS : V_BIAS + 1, at]
            out_ref[:, at] = found.astype(BF)


def project(order, x, blocks):
    count, width = x.shape
    return run(
        12,
        project_kernel,
        [((count, width), BF)] * 3 + [((16, 4 * width), F32), ((48, 1, 128), F32)],
        order,
        [x],
        blocks,
        [pltpu.VMEM((8,) + blocks[0].shape, BF), pltpu.SemaphoreType.DMA((8,))],
    )


def output_kernel(order_ref, c_ref, spread_ref, hidden_ref, vector_ref, *refs):
    blocks = refs[:8]
    context_ref, normed_ref, deviation_ref, low_ref, held, sem = refs[8:]
    copies = fetch(blocks, held, sem)
    context_ref[...] = dot(spread_ref[...], c_ref[...]).astype(BF)
    x = jnp.concatenate([context_ref[:, lanes(order_ref, k, 128)] for k in range(8)], axis=1)
    for copy in copies:
        copy.wait()
    width = hidden_ref.shape[1]
    normed_ref[...] = dot(x, held[...].reshape(-1, width))
    bias = vector_ref[O_BIAS : O_BIAS + 1, :width]
    gain = vector_ref[GAIN1 : GAIN1 + 1, :width]
    offset = vector_ref[SHIFT1 : SHIFT1 + 1, :width]
    for c in range(hidden_ref.shape[0] // ROWS_AT_ONCE):
        at = slice(c * ROWS_AT_ONCE, (c + 1) * ROWS_AT_ONCE)
        normed, deviation = norm_parts(hidden_ref[at].astype(F32) + (normed_ref[at] + bias))
        normed_ref[at] = normed
        deviation_ref[at] = deviation
        low_ref[at] = (normed * gain + offset).astype(BF)


def output_block(order, context, spread, hidden, vectors, blocks):
    count, width = hidden.shape
    return run(
        7,
        output_kernel,
        [((count, width), BF), ((count, width), F32), ((count, 1), F32), ((count, width), BF)],
        order,
        [context, spread, hidden, vectors],
        blocks,
        [pltpu.VMEM((8,) + blocks[0].shape, BF), pltpu.SemaphoreType.DMA((8,))],
    )


def inner_kernel(tiles, order_ref, x_ref, vector_ref, *refs):
    blocks = refs[:8]
    active_out, steep_out, held, first, second, active_ref, steep_ref, sem, out_sem = refs[8:]
    leaving = []
    rows = blocks[0].shape[0]
    size = active_out.shape[1] // tiles
    copies = []
    for t in range(tiles):
        at = slice(t * size, (t + 1) * size)
        copies.append(
            [
                pltpu.make_async_copy(
                    blocks[k].at[:, at], held.at[pl.ds(k * rows, rows), at], sem.at[t, k]
                )
                for k in range(8)
            ]
        )
        for copy in copies[-1]:
            copy.start()
    x = jnp.concatenate([x_ref[:, lanes(order_ref, k, 128)] for k in range(8)], axis=1)
    halves = (first, second)

    def bend(t):
        source = halves[t % 2]
        at = slice(t * size, (t + 1) * size)
        bias = vector_ref[I_BIAS : I_BIAS + 1, at]
        for c in range(x_ref.shape[0] // ROWS_AT_ONCE):
            row = slice(c * ROWS_AT_ONCE, (c + 1) * ROWS_AT_ONCE)
            inner = source[row] + bias
            share = 0.5 + 0.5 * lax.erf(inner * 0.5**0.5)
            active_ref[row, at] = (inner * share).astype(BF)
            steep_ref[row, at] = (
                share + inner * jnp.exp(-0.5 * inner * inner) * (2 * np.pi) ** -0.5
            ).astype(BF)

        leaving.append(begin(active_ref.at[:, at], active_out.at[:, at], out_sem.at[0, t]))
        leaving.append(begin(steep_ref.at[:, at], steep_out.at[:, at], out_sem.at[1, t]))

    for t in range(tiles):
        finish(copies[t])
        halves[t % 2][...] = dot(x, held[:, t * size : (t + 1) * size])
        if t > 0:
            bend(t - 1)
    bend(tiles - 1)
    finish(leaving)


def inner_block(order, x, vectors, blocks, tiles=8):
    count, width = x.shape
    wide = blocks[0].shape[1]
    return run(
        14,
        partial(inner_kernel, tiles),
        [((count, wide), BF, 1), ((count, wide), BF, 1)],
        order,
        [x, vectors],
        blocks,
        [
            pltpu.VMEM((width, wide), BF),
            pltpu.VMEM((count, wide // tiles), F32),
            pltpu.VMEM((count, wide // tiles), F32),
            pltpu.VMEM((count, wide), BF),
            pltpu.VMEM((count, wide), BF),
            pltpu.SemaphoreType.DMA((tiles, 8)),
            pltpu.SemaphoreType.DMA((2, tiles)),
        ],
    )


def outer_kernel(order_ref, vector_ref, a_far, normed_far, upstream_far, *refs):
    blocks = refs[:8]
    (
        out_far,
        second_far,
        d_outer_far,
        sum_ref,
        held,
        a_ref,
        normed_ref,
        upstream_ref,
        out_ref,
        second_ref,
        d_outer_ref,
        sem,
        in_sem,
        out_sem,
    ) = refs[8:]
    width = out_ref.shape[1]
    rows = blocks[0].shape[0]
    weights, lefts = [], []
    for k in range(8):
        at = lanes(order_ref, k, rows)
        lefts.append(begin(a_far.at[:, at], a_ref.at[k], in_sem.at[k]))
        weights.append(begin(blocks[k], held.at[k], sem.at[k]))
    late = [
        begin(normed_far, normed_ref, in_sem.at[8]),
        begin(upstream_far, upstream_ref, in_sem.at[9]),
    ]
    for k in range(8):
        finish([lefts[k], weights[k]])
        part = dot(a_ref[k], held[k])
        if k == 0:
            second_ref[...] = part
        else:
            second_ref[...] += part
    finish(late)
    gain1 = vector_ref[GAIN1 : GAIN1 + 1, :width]
    shift1 = vector_ref[SHIFT1 : SHIFT1 + 1, :width]
    gain2 = vector_ref[GAIN2 : GAIN2 + 1, :width]
    shift2 = vector_ref[SHIFT2 : SHIFT2 + 1, :width]
    bias = vector_ref[U_BIAS : U_BIAS + 1, :width]
    sums = [jnp.zeros((8, width), F32)] * 3
    leaving = []
    for g, group in enumerate(row_groups(out_ref.shape[0])):
        for c in group:
            at = slice(c * ROWS_AT_ONCE, (c + 1) * ROWS_AT_ONCE)
            first_out = normed_ref[at] * gain1 + shift1
            normed, deviation = norm_parts(first_out + (second_ref[at] + bias))
            out_ref[at] = (normed * gain2 + shift2).astype(BF)
            upstream = upstream_ref[at].astype(F32)
            d_second = norm_back(normed, deviation, upstream * gain2)
            second_ref[at] = d_second
            low = d_second.astype(BF)
            d_outer_ref[at] = low
            sums[0] = sums[0] + fold_rows(upstream * normed)
            sums[1] = sums[1] + fold_rows(upstream)
            sums[2] = sums[2] + fold_rows(low.astype(F32))
        at = pl.ds(group[0] * ROWS_AT_ONCE, len(group) * ROWS_AT_ONCE)
        for i, (source, target) in enumerate(
            ((out_ref, out_far), (second_ref, second_far), (d_outer_ref, d_outer_far))
        ):
            leaving.append(begin(source.at[at], target.at[at], out_sem.at[i, g]))
    for i in range(3):
        sum_ref[i : i + 1, :] = jnp.sum(sums[i], axis=0, keepdims=True)
    finish(leaving)


def outer_block(order, active, normed, upstream, vectors, blocks):
    count, width = normed.shape
    return run(
        11.5,
        outer_kernel,
        [
            ((count, width), BF, 1),
            ((count, width), F32, 1),
            ((count, width), BF, 1),
            ((8, width), F32),
        ],
        order,
        [vectors],
        blocks,
        [
            pltpu.VMEM((8,) + blocks[0].shape, BF),
            pltpu.VMEM((8, count, active.shape[1] // 8), BF),
            pltpu.VMEM((count, width), F32),
            pltpu.VMEM((count, width), BF),
            pltpu.VMEM((count, width), BF),
            pltpu.VMEM((count, width), F32),
            pltpu.VMEM((count, width), BF),
            pltpu.SemaphoreType.DMA((8,)),
            pltpu.SemaphoreType.DMA((10,)),
            pltpu.SemaphoreType.DMA((3, 4)),
        ],
        [active, normed, upstream],
    )


def inner_back_kernel(order_ref, d_ref, steep_far, *refs):
    blocks = refs[:8]
    out_far, sum_ref, held, steep_ref, out_ref, sem, in_sem, out_sem = refs[8:]
    rows = blocks[0].shape[0]
    copies = []
    for k in range(8):
        at = lanes(order_ref, k, rows)
        copies.append(
            [
                begin(blocks[k], held.at[k], sem.at[k]),
                begin(steep_far.at[:, at], steep_ref.at[k], in_sem.at[k]),
            ]
        )
    leaving = []
    for k in range(8):
        finish(copies[k])
        at = lanes(order_ref, k, rows)
        low = (dot(d_ref[...], held[k], NT) * steep_ref[k].astype(F32)).astype(BF)
        out_ref[k] = low
        sum_ref[:, at] = fold_rows(low.astype(F32))
        leaving.append(begin(out_ref.at[k], out_far.at[:, at], out_sem.at[k]))
    finish(leaving)


def inner_back(order, d_outer, steep, blocks):
    count, wide = steep.shape
    return run(
        10,
        inner_back_kernel,
        [((count, wide), BF, 1), ((8, wide), F32)],
        order,
        [d_outer],
        blocks,
        [
            pltpu.VMEM((8,) + blocks[0].shape, BF),
            pltpu.VMEM((8, count, wide // 8), BF),
            pltpu.VMEM((8, count, wide // 8), BF),
            pltpu.SemaphoreType.DMA((8,)),
            pltpu.SemaphoreType.DMA((8,)),
            pltpu.SemaphoreType.DMA((8,)),
        ],
        [steep],
    )


def first_back_kernel(
    order_ref, d_ref, deviation_ref, vector_ref, second_far, normed_far, *refs
):
    blocks = refs[:8]
    (
        summed_far,
        low_far,
        sum_ref,
        held,
        second_ref,
        normed_ref,
        summed_ref,
        low_ref,
        sem,
        in_sem,
        out_sem,
    ) = refs[8:]
    copies = fetch(blocks, held, sem)
    late = [
        begin(second_far, second_ref, in_sem.at[0]),
        begin(normed_far, normed_ref, in_sem.at[1]),
    ]
    width = summed_ref.shape[1]
    for k in range(0, 8, 2):
        finish(copies[k : k + 2])
        weight = jnp.concatenate([held[k], held[k + 1]], axis=0)
        part = dot(d_ref[...], weight, NT)
        rows = part.shape[1] // 2
        summed_ref[:, lanes(order_ref, k, rows)] = part[:, :rows]
        summed_ref[:, lanes(order_ref, k + 1, rows)] = part[:, rows:]
    finish(late)
    gain = vector_ref[GAIN1 : GAIN1 + 1, :width]
    sums = [jnp.zeros((8, width), F32)] * 3
    leaving = []
    for g, group in enumerate(row_groups(summed_ref.shape[0])):
        for c in group:
            at = slice(c * ROWS_AT_ONCE, (c + 1) * ROWS_AT_ONCE)
            d_first = second_ref[at] + summed_ref[at]
            normed = normed_ref[at]
            d_summed = norm_back(normed, deviation_ref[at], d_first * gain)
            summed_ref[at] = d_summed
            low = d_summed.astype(BF)
            low_ref[at] = low
            sums[0] = sums[0] + fold_rows(d_first * normed)
            sums[1] = sums[1] + fold_rows(d_first)
            sums[2] = sums[2] + fold_rows(low.astype(F32))
        at = pl.ds(group[0] * ROWS_AT_ONCE, len(group) * ROWS_AT_ONCE)
        leaving.append(begin(summed_ref.at[at], summed_far.at[at], out_sem.at[0, g]))
        leaving.append(begin(low_ref.at[at], low_far.at[at], out_sem.at[1, g]))
    for i in range(3):
        sum_ref[i : i + 1, :] = jnp.sum(sums[i], axis=0, keepdims=True)
    finish(leaving)


def first_back(order, d_inner, d_second, normed, deviation, vectors, blocks):
    count, width = normed.shape
    return run(
        16,
        first_back_kernel,
        [((count, width), F32, 1), ((count, width), BF, 1), ((8, width), F32)],
        order,
        [d_inner, deviation, vectors],
        blocks,
        [
            pltpu.VMEM((8,) + blocks[0].shape, BF),
            pltpu.VMEM((count, width), F32),
            pltpu.VMEM((count, width), F32),
            pltpu.VMEM((count, width), F32),
            pltpu.VMEM((count, width), BF),
            pltpu.SemaphoreType.DMA((8,)),
            pltpu.SemaphoreType.DMA((2,)),
            pltpu.SemaphoreType.DMA((2, 4)),
        ],
        [d_second, normed],
    )


def context_back_kernel(order_ref, d_ref, spread_ref, *refs):
    blocks = refs[:8]
    out_ref, held, kept, sem = refs[8:]
    copies = fetch(blocks, held, sem)
    rows = blocks[0].shape[0]
    for copy in copies:
        copy.wait()
    for k in range(0, 8, 2):
        weight = jnp.concatenate([held[k], held[k + 1]], axis=0)
        part = dot(d_ref[...], weight, NT).astype(BF)
        kept[:, lanes(order_ref, k, rows)] = part[:, :rows]
        kept[:, lanes(order_ref, k + 1, rows)] = part[:, rows:]
    out_ref[...] = dot(spread_ref[...], kept[...]).astype(BF)


def context_back(order, d_attn, spread, blocks):
    count, width = d_attn.shape
    return run(
        6.5,
        context_back_kernel,
        [((spread.shape[0], width), BF)],
        order,
        [d_attn, spread],
        blocks,
        [
            pltpu.VMEM((8,) + blocks[0].shape, BF),
            pltpu.VMEM((count, width), BF),
            pltpu.SemaphoreType.DMA((8,)),
        ],
    )[0]


def input_back_kernel(order_ref, d_ref, spread_ref, summed_far, *refs):
    blocks = refs[:8]
    out_far, held, kept, summed_ref, out_ref, sem, in_sem, out_sem = refs[8:]
    copies = fetch(blocks, held, sem)
    late = begin(summed_far, summed_ref, in_sem.at[0])
    rows = (blocks[0].shape[0] - 16) // 3
    width = summed_ref.shape[1]
    for j in range(6):
        at = slice(j * width // 2, (j + 1) * width // 2)
        kept[:, at] = dot(spread_ref[...], d_ref[:, at]).astype(BF)
    finish(copies)
    late.wait()
    leaving = []
    for k in range(0, 8, 2):
        weight = jnp.concatenate(
            [
                jnp.concatenate(
                    [held[k, j * rows : (j + 1) * rows], held[k + 1, j * rows : (j + 1) * rows]],
                    axis=0,
                )
                for j in range(3)
            ],
            axis=1,
        )
        part = dot(kept[...], weight, NT)
        for i in range(2):
            at = lanes(order_ref, k + i, rows)
            out_ref[k + i] = summed_ref[:, at] + part[:, i * rows : (i + 1) * rows]
            leaving.append(begin(out_ref.at[k + i], out_far.at[:, at], out_sem.at[k + i]))
    finish(leaving)


def input_back(order, d_mixed, spread, d_summed, blocks):
    count, width = d_summed.shape
    return run(
        12.5,
        input_back_kernel,
        [((count, width), F32, 1)],
        order,
        [d_mixed, spread],
        blocks,
        [
            pltpu.VMEM((8,) + blocks[0].shape, BF),
            pltpu.VMEM((count, 3 * width), BF),
            pltpu.VMEM((count, width), F32),
            pltpu.VMEM((8, count, width // 8), F32),
            pltpu.SemaphoreType.DMA((8,)),
            pltpu.SemaphoreType.DMA((1,)),
            pltpu.SemaphoreType.DMA((8,)),
        ],
        [d_summed],
    )[0]


def small_kernel(
    order_ref,
    slide_ref,
    box_ref,
    bias_ref,
    first_ref,
    inner_ref,
    second_ref,
    *refs,
):
    outs, flat = refs[:8], refs[8]
    spot = one_hot(
        (2 * PAGE, NB),
        lambda c, bucket: (jnp.clip(PAGE - 1 - c, -64, 63) + 64 == bucket) & (c < 2 * PAGE - 1),
    ).astype(F32)
    by_head = [precise(slide_ref[...], spot)]
    by_head += [pltpu.roll(box_ref[i], 65, 1) for i in range(2)]
    heads = one_hot((NB, HEADS), lambda r, c: r % 16 == c).astype(F32)
    mine = one_hot((NB, NB), lambda r, c: r // 16 == c % 8)
    rows = one_hot((16, NB), lambda r, c: c // 8 == r).astype(F32)
    for kind in range(3):
        spread = jnp.where(mine, precise(heads, by_head[kind]), 0.0)
        found = precise(rows, spread, NT)
        for i in range(16):
            flat[16 * kind + i] = found[i : i + 1]
    width = first_ref.shape[1]
    bias = jnp.sum(bias_ref[...], axis=0, keepdims=True)
    inner = jnp.sum(inner_ref[...], axis=0, keepdims=True)
    bias_ref[0:1, :] = bias
    inner_ref[0:1, :] = inner
    for k in range(8):
        out_ref = outs[k]
        at = lanes(order_ref, k, 128)
        out_ref[0:1, :] = bias_ref[0:1, at]
        out_ref[1:2, :] = bias_ref[
            0:1, pl.ds(pl.multiple_of(2 * width + order_ref[k] * 128, 128), 128)
        ]
        out_ref[2:3, :] = first_ref[2:3, at]
        out_ref[3:5, :] = first_ref[0:2, at]
        for part in range(4):
            piece = pl.ds(pl.multiple_of(order_ref[k] * 512 + part * 128, 128), 128)
            out_ref[5 + part : 6 + part, :] = inner_ref[0:1, piece]
        out_ref[9:10, :] = second_ref[2:3, at]
        out_ref[10:12, :] = second_ref[0:2, at]
        for part in range(6):
            out_ref[12 + part : 13 + part, :] = flat[order_ref[k] * 6 + part]
        out_ref[18:, :] = jnp.zeros((6, 128), F32)


def small_blocks(order, sums):
    return pl.pallas_call(
        small_kernel,
        out_shape=(jax.ShapeDtypeStruct((24, 128), F32),) * 8,
        in_specs=[pl.BlockSpec(memory_space=pltpu.SMEM)]
        + [pl.BlockSpec(memory_space=pltpu.VMEM)] * 6,
        out_specs=(pl.BlockSpec(memory_space=pltpu.VMEM),) * 8,
        scratch_shapes=[pltpu.VMEM((48, 1, 128), F32)],
        compiler_params=pltpu.CompilerParams(vmem_limit_bytes=VMEM_LIMIT),
        cost_estimate=cost(3),
    )(order, *sums)


def on_device(line, mesh_size, *args):
    (
        hidden_in,
        cotangent,
        segment_ids,
        box_left,
        box_top,
        query_weight,
        query_bias,
        key_weight,
        value_weight,
        value_bias,
        output_weight,
        output_bias,
        first_gain,
        first_shift,
        inner_weight,
        inner_bias,
        outer_weight,
        outer_bias,
        second_gain,
        second_shift,
        bucket_table,
    ) = args
    slot_count = segment_ids.shape[1]
    width = hidden_in.shape[1]
    vectors = (
        query_bias,
        value_bias,
        output_bias,
        first_gain,
        first_shift,
        inner_bias,
        outer_bias,
        second_gain,
        second_shift,
        bucket_table,
    )
    phase = lax.optimization_barrier
    if line:
        order = block_order(lax.axis_index("fsdp"))
        packed = pack((query_weight, key_weight, value_weight), vectors)
        in_blocks = [packed, hop(packed, NEAR), hop(packed, FAR)]
    else:
        order = jnp.arange(8, dtype=jnp.int32)

        def whole(shard):
            return lax.all_gather(shard, "fsdp", axis=0, tiled=True)

        def blocks_of(shard):
            full = whole(shard)
            return list(full.reshape(8, full.shape[0] // 8, full.shape[1]))

        small = jnp.concatenate([whole(item).reshape(8, -1) for item in vectors], axis=1)
        small = jnp.pad(small, ((0, 0), (0, 16 * width - small.shape[1])))
        in_blocks = jnp.concatenate(
            [whole(item).reshape(8, -1, width) for item in (query_weight, key_weight, value_weight)]
            + [small.reshape(8, 16, width)],
            axis=1,
        )
        in_blocks = list(in_blocks)
        output_blocks = blocks_of(output_weight)
        inner_blocks = blocks_of(inner_weight)
        outer_blocks = blocks_of(outer_weight)

    slot = lax.iota(jnp.int32, slot_count)
    pages = lax.iota(jnp.int32, PAGES)
    segments = segment_ids[0]
    member = segments[None, :] == pages[:, None]
    lengths = jnp.sum(member, axis=1, dtype=jnp.int32)
    starts = jnp.sum(segments[None, :] < pages[:, None], axis=1, dtype=jnp.int32)
    start_of = jnp.sum(jnp.where(member, starts[:, None], 0), axis=0)
    target = segments * PAGE + slot - start_of
    padded = lax.iota(jnp.int32, PAGES * PAGE)
    spread = (padded[:, None] == target[None, :]).astype(BF)
    gather = (padded[None, :] == target[:, None]).astype(BF)
    coords = lax.iota(jnp.int32, NB) % 64
    sides = jnp.where(padded[None, :NB] < 64, box_left[0][:, None], box_top[0][:, None])
    boxes = dot(spread, (sides == coords[None, :]).astype(BF)).astype(BF)
    turned = jnp.where(padded[:NB, None] < 64, box_top[0][None, :], box_left[0][None, :])
    turned = (turned == 63 - coords[:, None]).astype(BF)
    flipped = dot(turned, spread, NT).astype(BF)
    hidden = dot(spread, hidden_in).astype(BF)

    if line:
        in_blocks, hidden, boxes, flipped, gather, spread, inner_weight = phase(
            (in_blocks, hidden, boxes, flipped, gather, spread, inner_weight)
        )
        own, near, far = in_blocks
        both = hop(near, FAR)
        twins = [hop(item, TWIN) for item in (own, near, far)]
        inner_near = hop(inner_weight, NEAR)
        both, twins, inner_near, inner_weight, output_weight = phase(
            (both, twins, inner_near, inner_weight, output_weight)
        )
        in_blocks = [own, near, far, both] + twins + [hop(both, TWIN)]
        inner_far = hop(inner_weight, FAR)
        output_near, output_far = hop(output_weight, NEAR), hop(output_weight, FAR)
    queries, keys, values, vector, table = project(order, hidden, in_blocks)
    lookup, slide = make_tables(table)
    if line:
        (
            queries,
            keys,
            values,
            lookup,
            slide,
            inner_near,
            inner_far,
            output_near,
            output_far,
            outer_weight,
        ) = phase(
            (
                queries,
                keys,
                values,
                lookup,
                slide,
                inner_near,
                inner_far,
                output_near,
                output_far,
                outer_weight,
            )
        )
        outer_near = hop(outer_weight, NEAR)
        output_blocks = [output_weight, output_near, output_far, hop(output_near, FAR)]
    context, prob = attend(lengths, queries, keys, values, boxes, lookup, slide)
    if line:
        context, outer_near, output_blocks, inner_near, inner_far = phase(
            (context, outer_near, output_blocks, inner_near, inner_far)
        )
        inner_blocks = [inner_weight, inner_near, inner_far, hop(inner_near, FAR)]
        outer_far = hop(outer_weight, FAR)
        output_blocks = output_blocks + [hop(item, TWIN) for item in output_blocks]
        inner_twins = [hop(item, TWIN) for item in inner_blocks[:3]]
    context, normed, deviation, first_low = output_block(
        order, context, gather, hidden_in, vector, output_blocks
    )
    if line:
        first_low, inner_blocks, inner_twins, outer_near, outer_far = phase(
            (first_low, inner_blocks, inner_twins, outer_near, outer_far)
        )
        outer_blocks = [outer_weight, outer_near, outer_far, hop(outer_near, FAR)]
        inner_blocks = inner_blocks + inner_twins + [hop(inner_blocks[3], TWIN)]
        outer_twins = [hop(item, TWIN) for item in outer_blocks[:3]]
    active, steep = inner_block(order, first_low, vector, inner_blocks)
    if line:
        active, outer_blocks, outer_twins = phase((active, outer_blocks, outer_twins))
        outer_blocks = outer_blocks + outer_twins + [hop(outer_blocks[3], TWIN)]
    layer_out, d_second, d_outer, second_sums = outer_block(
        order, active, normed, cotangent, vector, outer_blocks
    )

    if line:
        send = turned_blocks(order, 4, active, d_outer)
        d_outer, send = phase((d_outer, send))
        other2 = to_twin(send)
    d_inner, inner_sums = inner_back(order, d_outer, steep, outer_blocks)
    if line:
        d_inner, other2 = phase((d_inner, other2))
        stay2, away2 = turned_blocks(order, 0, active, d_outer, other2)
        d_inner, stay2, away2 = phase((d_inner, stay2, away2))
        other2 = hop(away2, FAR)
        d_inner, stay2 = phase((d_inner, stay2))
    d_summed, d_attn, first_sums = first_back(
        order, d_inner, d_second, normed, deviation, vector, inner_blocks
    )
    if line:
        pairs1 = ((first_low, d_inner), (context, d_attn))
        send = grad_blocks(order, 4, pairs1, 1024)
        d_attn, send, stay2, other2 = phase((d_attn, send, stay2, other2))
        other1 = to_twin(send)
        stay2, away2 = fold_far(stay2, other2)
        other2 = hop(away2, NEAR)
    d_context = context_back(order, d_attn, spread, output_blocks)
    if line:
        d_context, other1, stay2 = phase((d_context, other1, stay2))
        stay1, away1 = grad_blocks(order, 0, pairs1, 1024, other1)
        d_context, stay1, away1, stay2, other2 = phase(
            (d_context, stay1, away1, stay2, other2)
        )
        other1 = hop(away1, FAR)
        kept2, sent2 = cut(stay2 + other2, 1)
        other2 = trade(sent2, 1)
    d_mixed, slide_sum, box_sum, bias_sum = attend_back(
        queries, keys, values, d_context, boxes, flipped, prob
    )
    sums = (slide_sum, box_sum, bias_sum, first_sums, inner_sums, second_sums)
    if line:
        pairs = ((hidden, d_mixed),)
        d_mixed, kept2, other2, stay1, sums = phase((d_mixed, kept2, other2, stay1, sums))
        kept2, sent2 = cut(kept2 + other2, 2)
        other2 = trade(sent2, 2)
        send = grad_blocks(order, 4, pairs, 1024)
        d_mixed, send, kept2, other2, stay1, other1, sums = phase(
            (d_mixed, send, kept2, other2, stay1, other1, sums)
        )
        other = to_twin(send)
        stay1, away1 = fold_far(stay1, other1)
        other1 = hop(away1, NEAR)
        kept2 = kept2 + other2
        other2 = trade(kept2, 2)
    small = small_blocks(order, sums)
    if line:
        d_mixed, other, small, stay1, kept2 = phase((d_mixed, other, small, stay1, kept2))
        stay, away = grad_blocks(order, 0, pairs, 1024, other)
        d_mixed, stay, away, stay1, other1, kept2, other2, small = phase(
            (d_mixed, stay, away, stay1, other1, kept2, other2, small)
        )
        other = hop(away, FAR)
        small_other = to_twin(small[4:])
        kept1, sent1 = cut(stay1 + other1, 1)
        other1 = trade(sent1, 1)
    input_grad = input_back(order, d_mixed, gather, d_summed, in_blocks)
    if line:
        stay, other, input_grad, small, small_other, kept1, other1, kept2, other2 = phase(
            (stay, other, input_grad, small, small_other, kept1, other1, kept2, other2)
        )
        stay, away = fold_far(stay, other)
        other = hop(away, NEAR)
        kept1, sent1 = cut(kept1 + other1, 2)
        other1 = trade(sent1, 2)
        kept2 = paste(kept2, other2, 2)
        other2 = trade(kept2, 1)
        small = [small[i] + small_other[i] for i in range(4)]
        small_other = hop(jnp.stack(small[2:]), FAR)
        stay, other, small, small_other, kept1, other1, kept2, other2 = phase(
            (stay, other, small, small_other, kept1, other1, kept2, other2)
        )
        kept, sent = cut(stay + other, 1)
        other = trade(sent, 1)
        kept1 = kept1 + other1
        other1 = trade(kept1, 2)
        small = small[0] + small_other[0], small[1] + small_other[1]
        small_other = hop(small[1], NEAR)
        kept, other, kept1, other1, small, small_other, kept2, other2 = phase(
            (kept, other, kept1, other1, small, small_other, kept2, other2)
        )
        kept, sent = cut(kept + other, 2)
        other = trade(sent, 2)
        kept1 = paste(kept1, other1, 2)
        other1 = trade(kept1, 1)
        small = small[0] + small_other
        small_other = trade(small, 1)
        outer_own = paste(kept2, other2, 1).T.astype(F32)
        kept, other, kept1, other1, small, small_other, outer_own = phase(
            (kept, other, kept1, other1, small, small_other, outer_own)
        )
        kept = kept + other
        other = trade(kept, 2)
        small = small + small_other
        small_other = trade(small, 2)
        inner_own = paste(kept1, other1, 1).astype(F32)
        kept, other, small, small_other, inner_own = phase(
            (kept, other, small, small_other, inner_own)
        )
        kept = paste(kept, other, 2)
        other = trade(kept, 1)
        small = (small + small_other).reshape(-1)
        kept, other, small = phase((kept, other, small))
        in_own = paste(kept, other, 1)
        inner_own, output_own = inner_own[:, : 4 * width], inner_own[:, 4 * width :]
        cuts = np.cumsum([0] + [item.shape[0] for item in vectors])
        owned = [small[cuts[i] : cuts[i + 1]] for i in range(len(vectors))]
    else:

        def reduce(value):
            value = lax.psum_scatter(value, "fsdp", scatter_dimension=0, tiled=True)
            return lax.psum(value, "dp")

        small = jnp.stack(small)[:, :18].reshape(8, -1)
        edges = np.cumsum([0] + [item.shape[0] * mesh_size // 8 for item in vectors])
        owned = [
            reduce(small[:, edges[i] : edges[i + 1]].reshape(-1)) for i in range(len(vectors))
        ]
        outer_own = reduce(dot(active, d_outer, TN).astype(BF))
        inner_own = reduce(dot(first_low, d_inner, TN).astype(BF))
        output_own = reduce(dot(context, d_attn, TN).astype(BF))
        in_own = reduce(dot(hidden, d_mixed, TN).astype(BF))
    in_own = in_own.astype(F32)
    return (
        layer_out,
        input_grad,
        in_own[:, :width],
        owned[0],
        in_own[:, width : 2 * width],
        in_own[:, 2 * width :],
        owned[1],
        output_own.astype(F32),
        owned[2],
        owned[3],
        owned[4],
        inner_own.astype(F32),
        owned[5],
        outer_own.astype(F32),
        owned[6],
        owned[7],
        owned[8],
        owned[9],
    )


def solution(mesh):
    line = mesh.shape["fsdp"] == 8 and mesh.shape["dp"] == 4
    both, across, flat = P(("fsdp", "dp"), None), P("fsdp", None), P("fsdp")
    return jax.shard_map(
        partial(on_device, line, mesh.shape["fsdp"]),
        mesh=mesh,
        in_specs=(both,) * 5
        + (across, flat, across, across, flat, across, flat, flat, flat)
        + (across, flat, across, flat, flat, flat, flat),
        out_specs=(both, both)
        + (across, flat, across, across, flat, across, flat, flat, flat)
        + (across, flat, across, flat, flat, flat, flat),
        check_vma=False,
    )
```

```python
from functools import partial

import jax
import jax.numpy as jnp
import numpy as np
from jax import lax
from jax.experimental import pallas as pl
from jax.experimental.pallas import tpu as pltpu
from jax.sharding import PartitionSpec as P

HEADS = 16
HEAD_DIM = 64
PAIRS = HEADS // 2
NB = 128
PAGE = 128
PAGES = 8
EPSILON = 1e-05
BLOCKED = -1e30
BF = jnp.bfloat16
F32 = jnp.float32
VMEM_LIMIT = 62 * 1024 * 1024
SCALE = 0.3


def cost(microseconds):
    return pl.CostEstimate(
        flops=1 + int(microseconds * SCALE * 1e9), bytes_accessed=1, transcendentals=0
    )


NT = (((1,), (1,)), ((), ()))
TN = (((0,), (0,)), ((), ()))


def dot(left_side, right_side, dims=(((1,), (0,)), ((), ()))):
    return lax.dot_general(left_side, right_side, dims, preferred_element_type=F32)


def flips(bit_of):
    return [(i, i ^ bit_of(i & 1)) for i in range(8)]


NEAR = flips(lambda c: 2 if c else 4)
FAR = flips(lambda c: 4 if c else 2)
TWIN = flips(lambda c: 1)


def block_order(me):
    rel0 = np.array([0, 4, 2, 6, 1, 3, 5, 7], np.int32)
    rel1 = np.array([0, 2, 4, 6, 1, 5, 3, 7], np.int32)
    rel = jnp.where((me & 1) == 0, rel0, rel1)
    return jnp.bitwise_xor(me, rel).astype(jnp.int32)


def hop(value, pairs):
    return lax.ppermute(value, "fsdp", pairs)


def after(value, *others):
    return lax.optimization_barrier((value,) + others)[0]


def fold_far(stay, other):
    return stay[0] + other[0], stay[1] + other[1]


def trade(value, bit):
    return lax.ppermute(value, "dp", [(i, i ^ bit) for i in range(4)])


def cut(value, bit):
    high = (lax.axis_index("dp") & bit) // bit
    halves = value.reshape((2, value.shape[0] // 2) + value.shape[1:])
    return (
        lax.dynamic_index_in_dim(halves, high, 0, keepdims=False),
        lax.dynamic_index_in_dim(halves, 1 - high, 0, keepdims=False),
    )


def paste(mine, other, bit):
    high = (lax.axis_index("dp") & bit) != 0
    return jnp.concatenate([jnp.where(high, other, mine), jnp.where(high, mine, other)], axis=0)


def pack_kernel(shapes, *refs):
    items, out_ref, sem = refs[: len(shapes) + 3], refs[-2], refs[-1]
    rows = items[0].shape[0]
    copies = [
        pltpu.make_async_copy(items[j], out_ref.at[pl.ds(j * rows, rows), :], sem.at[j])
        for j in range(3)
    ]
    for copy in copies:
        copy.start()
    spot = 0
    out_ref[3 * rows :, :] = jnp.zeros((16, out_ref.shape[1]), BF)
    for item, count in zip(items[3:], shapes):
        for i in range(count):
            row, lane = 3 * rows + spot // 8, spot % 8 * 128
            out_ref[row : row + 1, lane : lane + 128] = item[i : i + 1, :]
            spot += 1
    for copy in copies:
        copy.wait()


def pack(weights, vectors):
    rows, columns = weights[0].shape
    vectors = [item.reshape(-1, 128) for item in vectors]
    return pl.pallas_call(
        partial(pack_kernel, tuple(item.shape[0] for item in vectors)),
        out_shape=jax.ShapeDtypeStruct((3 * rows + 16, columns), BF),
        in_specs=[pl.BlockSpec(memory_space=pltpu.HBM)] * 3
        + [pl.BlockSpec(memory_space=pltpu.VMEM)] * len(vectors),
        out_specs=pl.BlockSpec(memory_space=pltpu.VMEM),
        scratch_shapes=[pltpu.SemaphoreType.DMA((3,))],
        cost_estimate=cost(3),
    )(*weights, *vectors)


def emit(found, k, others, outs):
    if others:
        outs[k // 2][k % 2] = (found + others[k][...].astype(F32)).astype(BF)
    else:
        outs[k][...] = found.astype(BF)


def turned_kernel(fold, order_ref, left_ref, right_ref, *refs):
    others, outs, turned = refs[: 4 * fold], refs[4 * fold : -1], refs[-1]
    i = pl.program_id(0)

    @pl.when(i == 0)
    def _():
        turned[...] = right_ref[...].T

    found = dot(turned[...], left_ref[...])
    for k in range(4):

        @pl.when(i == k)
        def _():
            emit(found, k, others, outs)


def turned_blocks(order, first, left, right, others=()):
    depth, rows, columns = left.shape[0], left.shape[1] // 8, right.shape[1]
    fold = int(bool(others))
    whole = pl.BlockSpec((columns, rows), lambda i, n: (0, 0))
    if fold:
        out_specs = (pl.BlockSpec((2, columns, rows), lambda i, n: (0, 0, 0)),) * 2
        shapes = (jax.ShapeDtypeStruct((2, columns, rows), BF),) * 2
    else:
        out_specs = (whole,) * 4
        shapes = (jax.ShapeDtypeStruct((columns, rows), BF),) * 4
    return pl.pallas_call(
        partial(turned_kernel, fold),
        grid_spec=pltpu.PrefetchScalarGridSpec(
            num_scalar_prefetch=1,
            grid=(4,),
            in_specs=[
                pl.BlockSpec((depth, rows), lambda i, n: (0, n[first + i])),
                pl.BlockSpec((depth, columns), lambda i, n: (0, 0)),
            ]
            + [whole] * (4 * fold),
            out_specs=out_specs,
            scratch_shapes=[pltpu.VMEM((columns, depth), left.dtype)],
        ),
        out_shape=shapes,
        compiler_params=pltpu.CompilerParams(vmem_limit_bytes=VMEM_LIMIT),
        cost_estimate=cost(7),
    )(order, left, right, *others)


def grad_kernel(first, counts, fold, order_ref, *refs):
    pieces = len(counts)
    lefts, rights = refs[:pieces], refs[pieces : 2 * pieces]
    others = refs[2 * pieces : 2 * pieces + 4 * fold]
    outs, turned = refs[2 * pieces + 4 * fold : -pieces], refs[-pieces:]
    i = pl.program_id(0)
    rows = turned[0].shape[0] // 4
    start = 0
    for left_ref, right_ref, kept, count in zip(lefts, rights, turned, counts):

        @pl.when(i == start)
        def _():
            for k in range(4):
                kept[k * rows : (k + 1) * rows, :] = left_ref[
                    :, lanes(order_ref, first + k, rows)
                ].T

        @pl.when((i >= start) & (i < start + count))
        def _():
            found = dot(kept[...], right_ref[...])
            for k in range(4):
                emit(found[k * rows : (k + 1) * rows], k, others, outs)

        start += count


def grad_blocks(order, first, pairs, tile, others=()):
    rows = pairs[0][0].shape[1] // 8
    counts = [right.shape[1] // tile for _, right in pairs]
    total = sum(counts)
    fold = int(bool(others))
    in_specs = [pl.BlockSpec(left.shape, lambda i, n: (0, 0)) for left, _ in pairs]
    start = 0
    for (_, right), count in zip(pairs, counts):

        def at(i, n, start=start, count=count):
            return 0, jnp.clip(i - start, 0, count - 1)

        in_specs.append(pl.BlockSpec((right.shape[0], tile), at))
        start += count
    one = pl.BlockSpec((rows, tile), lambda i, n: (0, i))
    if fold:
        out_specs = (pl.BlockSpec((2, rows, tile), lambda i, n: (0, 0, i)),) * 2
        shapes = (jax.ShapeDtypeStruct((2, rows, total * tile), BF),) * 2
    else:
        out_specs = (one,) * 4
        shapes = (jax.ShapeDtypeStruct((rows, total * tile), BF),) * 4
    return pl.pallas_call(
        partial(grad_kernel, first, tuple(counts), fold),
        grid_spec=pltpu.PrefetchScalarGridSpec(
            num_scalar_prefetch=1,
            grid=(total,),
            in_specs=in_specs + [one] * (4 * fold),
            out_specs=out_specs,
            scratch_shapes=[pltpu.VMEM((4 * rows, left.shape[0]), BF) for left, _ in pairs],
        ),
        out_shape=shapes,
        compiler_params=pltpu.CompilerParams(vmem_limit_bytes=VMEM_LIMIT),
        cost_estimate=cost(2 * total),
    )(
        order,
        *[left for left, _ in pairs],
        *[right for _, right in pairs],
        *others,
    )


def to_twin(blocks):
    return [hop(block, TWIN) for block in blocks]


def lanes(order_ref, k, size):
    return pl.ds(pl.multiple_of(order_ref[k] * size, size), size)


def one_hot(shape, test):
    row = lax.broadcasted_iota(jnp.int32, shape, 0)
    lane = lax.broadcasted_iota(jnp.int32, shape, 1)
    return test(row, lane)


def precise(left_side, right_side, dims=(((1,), (0,)), ((), ()))):
    return lax.dot_general(
        left_side, right_side, dims, precision=lax.Precision.HIGHEST, preferred_element_type=F32
    )


def tables_kernel(table_ref, lookup_ref, slide_ref, flat):
    for i in range(48):
        flat[i : i + 1, :] = table_ref[i]
    wide = one_hot((NB, 16), lambda r, c: r // 8 == c).astype(F32)
    mine = one_hot((NB, NB), lambda r, c: c // 16 == r % 8)
    heads = one_hot((HEADS, NB), lambda r, c: c % 16 == r).astype(F32)
    by_head = []
    for kind in range(3):
        rows = jnp.where(mine, precise(wide, flat[16 * kind : 16 * (kind + 1), :]), 0.0)
        by_head.append(precise(heads, rows, NT))
    spot = one_hot(
        (2 * PAGE, NB),
        lambda m, bucket: jnp.clip(jnp.where(m <= PAGE, -m, 2 * PAGE - m), -64, 63) + 64 == bucket,
    ).astype(F32)
    position = precise(by_head[0], spot, NT)
    left_all = pltpu.roll(by_head[1], 64, 1)
    top_all = pltpu.roll(by_head[2], 64, 1)
    same = one_hot((NB, NB), lambda r, c: (r < 64) == (c < 64))
    for head in range(HEADS):
        base = jnp.broadcast_to(position[head : head + 1, :], (PAGE, 2 * PAGE))
        slid = pltpu.roll(base, 0, 1, stride=1, stride_axis=0)
        half = (head % 2) * PAGE
        slide_ref[head // 2, :, half : half + PAGE] = slid[:, :PAGE]
        left = jnp.broadcast_to(left_all[head : head + 1, :], (64, NB))
        top = jnp.broadcast_to(top_all[head : head + 1, :], (64, NB))
        slid = pltpu.roll(
            jnp.concatenate([left, top], axis=0), 0, 1, stride=1, stride_axis=0
        )
        lookup_ref[:, head * NB : (head + 1) * NB] = jnp.where(same, slid, 0.0).astype(BF)


def make_tables(table):
    return pl.pallas_call(
        tables_kernel,
        out_shape=(
            jax.ShapeDtypeStruct((NB, HEADS * NB), BF),
            jax.ShapeDtypeStruct((PAIRS, PAGE, 2 * PAGE), F32),
        ),
        scratch_shapes=[pltpu.VMEM((48, NB), F32)],
        compiler_params=pltpu.CompilerParams(vmem_limit_bytes=VMEM_LIMIT),
        cost_estimate=cost(3),
    )(table)


def split_heads(tile):
    lane = lax.broadcasted_iota(jnp.int32, tile.shape, 1)
    zero = jnp.zeros_like(tile)
    return jnp.concatenate(
        [jnp.where(lane < HEAD_DIM, tile, zero), jnp.where(lane >= HEAD_DIM, tile, zero)],
        axis=0,
    )


def join_heads(tall):
    lane = lax.broadcasted_iota(jnp.int32, (PAGE, NB), 1)
    return jnp.where(lane < HEAD_DIM, tall[:PAGE, :NB], tall[PAGE:, :NB])


def attend_kernel(
    length_ref, q_ref, k_ref, v_ref, box_ref, lookup_ref, slide_ref, context_ref, prob_ref, logit
):
    length = length_ref[pl.program_id(0)]
    inside = lax.broadcasted_iota(jnp.int32, (PAGE, 2 * PAGE), 0) < length
    boxes = box_ref[...]
    for pair in range(PAIRS):
        at = slice(pair * NB, (pair + 1) * NB)
        looked = dot(boxes, lookup_ref[:, 2 * pair * NB : 2 * (pair + 1) * NB]).astype(BF)
        looked = jnp.concatenate([looked[:, :NB], looked[:, NB:]], axis=0)
        asked = jnp.concatenate([split_heads(q_ref[:, at]), looked], axis=1)
        offered = jnp.concatenate([k_ref[:, at], boxes], axis=1)
        logit[pair] = dot(offered, asked, NT)
    for pair in range(PAIRS):
        logits = jnp.where(inside, logit[pair] + slide_ref[pair], BLOCKED)
        peak = jnp.max(logits, axis=0, keepdims=True)
        grown = jnp.exp(logits - peak)
        total = jnp.sum(grown, axis=0, keepdims=True)
        prob_ref[0, pair] = (grown * (1.0 / total)).astype(BF)
    for pair in range(PAIRS):
        at = slice(pair * NB, (pair + 1) * NB)
        context_ref[:, at] = join_heads(dot(prob_ref[0, pair], v_ref[:, at], TN)).astype(BF)


def attend(lengths, queries, keys, values, boxes, lookup, slide):
    wide = pl.BlockSpec((PAGE, HEADS * HEAD_DIM), lambda i, n: (i, 0))
    return pl.pallas_call(
        attend_kernel,
        grid_spec=pltpu.PrefetchScalarGridSpec(
            num_scalar_prefetch=1,
            grid=(PAGES,),
            in_specs=[
                wide,
                wide,
                wide,
                pl.BlockSpec((PAGE, NB), lambda i, n: (i, 0)),
                pl.BlockSpec((NB, HEADS * NB), lambda i, n: (0, 0)),
                pl.BlockSpec((PAIRS, PAGE, 2 * PAGE), lambda i, n: (0, 0, 0)),
            ],
            out_specs=(
                wide,
                pl.BlockSpec((1, PAIRS, PAGE, 2 * PAGE), lambda i, n: (i, 0, 0, 0)),
            ),
            scratch_shapes=[pltpu.VMEM((PAIRS, PAGE, 2 * PAGE), F32)],
        ),
        out_shape=(
            jax.ShapeDtypeStruct((PAGES * PAGE, HEADS * HEAD_DIM), BF),
            jax.ShapeDtypeStruct((PAGES, PAIRS, PAGE, 2 * PAGE), BF),
        ),
        compiler_params=pltpu.CompilerParams(vmem_limit_bytes=VMEM_LIMIT),
        cost_estimate=cost(13.5),
    )(lengths, queries, keys, values, boxes, lookup, slide)


def attend_back_kernel(
    q_ref,
    k_ref,
    v_ref,
    g_ref,
    box_ref,
    flip_ref,
    prob_ref,
    grad_ref,
    slide_sum_ref,
    box_sum_ref,
    bias_sum_ref,
    slide_acc,
    box_acc,
    d_prob,
    d_logit,
    boxed,
):
    page = pl.program_id(0)

    @pl.when(page == 0)
    def _():
        slide_acc[...] = jnp.zeros_like(slide_acc)
        box_acc[...] = jnp.zeros_like(box_acc)
        bias_sum_ref[...] = jnp.zeros_like(bias_sum_ref)

    boxes = box_ref[...]
    width = HEADS * HEAD_DIM
    scale = HEAD_DIM ** (-0.5)
    for pair in range(PAIRS):
        at = slice(pair * NB, (pair + 1) * NB)
        pulled = split_heads(g_ref[:, at])
        d_prob[pair] = dot(v_ref[:, at], pulled, NT)
        grad_ref[:, 2 * width + pair * NB : 2 * width + (pair + 1) * NB] = dot(
            prob_ref[0, pair], pulled
        ).astype(BF)
    for pair in range(PAIRS):
        prob = prob_ref[0, pair].astype(F32)
        inner = jnp.sum(prob * d_prob[pair], axis=0, keepdims=True)
        found = prob * (d_prob[pair] - inner)
        slide_acc[pair] += found
        d_logit[pair] = found.astype(BF)
    for pair in range(PAIRS):
        at = slice(pair * NB, (pair + 1) * NB)
        offered = jnp.concatenate([k_ref[:, at], boxes], axis=1)
        back = dot(d_logit[pair], offered, TN)
        grad_ref[:, at] = (join_heads(back) * scale).astype(BF)
        grad_ref[:, width + pair * NB : width + (pair + 1) * NB] = dot(
            d_logit[pair], split_heads(q_ref[:, at])
        ).astype(BF)
        tall = back[:, NB:].astype(BF)
        boxed[:, 2 * pair * NB : 2 * (pair + 1) * NB] = jnp.concatenate(
            [tall[:PAGE], tall[PAGE:]], axis=1
        )
    box_acc[...] += dot(flip_ref[...], boxed[...])
    for part in range(3 * width // 512):
        at = slice(part * 512, (part + 1) * 512)
        bias_sum_ref[:, at] += fold_rows(grad_ref[:, at].astype(F32))

    @pl.when(page == PAGES - 1)
    def _():
        row = lax.broadcasted_iota(jnp.int32, (NB, NB), 0)
        lane = lax.broadcasted_iota(jnp.int32, (NB, NB), 1)
        mirror = (row + lane == NB - 1).astype(BF)
        same = (row < 64) == (lane >= 64)
        for head in range(HEADS):
            half = (head % 2) * PAGE
            block = slide_acc[head // 2, :, half : half + PAGE]
            high = block.astype(BF)
            low = (block - high.astype(F32)).astype(BF)
            block = dot(mirror, high) + dot(mirror, low)
            block = jnp.concatenate([block, jnp.zeros_like(block)], axis=1)
            slid = pltpu.roll(block, 0, 1, stride=1, stride_axis=0)
            slide_sum_ref[head : head + 1, :] = jnp.sum(slid, axis=0, keepdims=True)
            block = jnp.where(same, box_acc[:, head * NB : (head + 1) * NB], 0.0)
            slid = pltpu.roll(block, 0, 1, stride=1, stride_axis=0)
            box_sum_ref[1, head : head + 1, :] = jnp.sum(slid[:64], axis=0, keepdims=True)
            box_sum_ref[0, head : head + 1, :] = jnp.sum(slid[64:], axis=0, keepdims=True)


def attend_back(queries, keys, values, d_context, boxes, flipped, prob):
    width = HEADS * HEAD_DIM
    wide = pl.BlockSpec((PAGE, width), lambda i: (i, 0))
    return pl.pallas_call(
        attend_back_kernel,
        grid=(PAGES,),
        in_specs=[
            wide,
            wide,
            wide,
            wide,
            pl.BlockSpec((PAGE, NB), lambda i: (i, 0)),
            pl.BlockSpec((NB, PAGE), lambda i: (0, i)),
            pl.BlockSpec((1, PAIRS, PAGE, 2 * PAGE), lambda i: (i, 0, 0, 0)),
        ],
        out_specs=(
            pl.BlockSpec((PAGE, 3 * width), lambda i: (i, 0)),
            pl.BlockSpec((HEADS, 2 * PAGE), lambda i: (0, 0)),
            pl.BlockSpec((2, HEADS, NB), lambda i: (0, 0, 0)),
            pl.BlockSpec((8, 3 * width), lambda i: (0, 0)),
        ),
        out_shape=(
            jax.ShapeDtypeStruct((PAGES * PAGE, 3 * width), BF),
            jax.ShapeDtypeStruct((HEADS, 2 * PAGE), F32),
            jax.ShapeDtypeStruct((2, HEADS, NB), F32),
            jax.ShapeDtypeStruct((8, 3 * width), F32),
        ),
        scratch_shapes=[
            pltpu.VMEM((PAIRS, PAGE, 2 * PAGE), F32),
            pltpu.VMEM((NB, HEADS * NB), F32),
            pltpu.VMEM((PAIRS, PAGE, 2 * PAGE), F32),
            pltpu.VMEM((PAIRS, PAGE, 2 * PAGE), BF),
            pltpu.VMEM((PAGE, HEADS * NB), BF),
        ],
        compiler_params=pltpu.CompilerParams(vmem_limit_bytes=VMEM_LIMIT),
        cost_estimate=cost(14),
    )(queries, keys, values, d_context, boxes, flipped, prob)


ROWS_AT_ONCE = 32
Q_BIAS, V_BIAS, O_BIAS, GAIN1, SHIFT1, I_BIAS, U_BIAS, GAIN2, SHIFT2 = range(9)
SPOTS = (0, 1, 2, 3, 4, 5, 9, 10, 11)
TABLE_SPOT = 12


def fetch(blocks, held, sem):
    copies = [
        pltpu.make_async_copy(blocks[k], held.at[k], sem.at[k]) for k in range(len(blocks))
    ]
    for copy in copies:
        copy.start()
    return copies


def norm_parts(values):
    center = jnp.mean(values, axis=-1, keepdims=True)
    centered = values - center
    spread = lax.rsqrt(jnp.mean(centered * centered, axis=-1, keepdims=True) + EPSILON)
    return centered * spread, spread


def norm_back(normed, spread, pulled):
    level = jnp.mean(pulled, axis=-1, keepdims=True)
    slope = jnp.mean(pulled * normed, axis=-1, keepdims=True)
    return spread * (pulled - level - normed * slope)


def fold_rows(values):
    return jnp.sum(values.reshape(-1, 8, values.shape[-1]), axis=0)


def run(length, kernel, shapes, order, ins, blocks, scratch, far=()):
    near_spec = pl.BlockSpec(memory_space=pltpu.VMEM)
    far_spec = pl.BlockSpec(memory_space=pltpu.HBM)
    return pl.pallas_call(
        kernel,
        out_shape=tuple(jax.ShapeDtypeStruct(item[0], item[1]) for item in shapes),
        in_specs=[pl.BlockSpec(memory_space=pltpu.SMEM)]
        + [near_spec] * len(ins)
        + [far_spec] * (len(far) + len(blocks)),
        out_specs=tuple(far_spec if len(item) > 2 else near_spec for item in shapes),
        scratch_shapes=scratch,
        compiler_params=pltpu.CompilerParams(vmem_limit_bytes=VMEM_LIMIT),
        cost_estimate=cost(length),
    )(order, *ins, *far, *blocks)


def begin(source, target, sem):
    copy = pltpu.make_async_copy(source, target, sem)
    copy.start()
    return copy


def finish(copies):
    for copy in copies:
        copy.wait()


def each_rows(group, body, carry):
    def step(c, carry):
        return body(pl.ds(pl.multiple_of(c * ROWS_AT_ONCE, ROWS_AT_ONCE), ROWS_AT_ONCE), carry)

    return lax.fori_loop(group[0], group[-1] + 1, step, carry)


def row_groups(count):
    chunks = count // ROWS_AT_ONCE
    edges = sorted({chunks * i // 4 for i in range(5)})
    return [range(low, high) for low, high in zip(edges, edges[1:])]


def project_kernel(order_ref, x_ref, *refs):
    blocks = refs[:8]
    q_ref, k_ref, v_ref, vector_ref, table_ref, held, sem = refs[8:]
    copies = fetch(blocks, held, sem)
    x = jnp.concatenate([x_ref[:, lanes(order_ref, k, 128)] for k in range(8)], axis=1)
    for copy in copies:
        copy.wait()
    rows = (held.shape[1] - 16) // 3

    def piece(k, spot):
        return held[k, pl.ds(3 * rows, 16), pl.ds(spot % 8 * 128, 128)].astype(F32)[
            spot // 8 : spot // 8 + 1
        ]

    for k in range(8):
        for i, spot in enumerate(SPOTS):
            if i == I_BIAS:
                for part in range(4):
                    at = pl.multiple_of(order_ref[k] * 512 + part * 128, 128)
                    vector_ref[i : i + 1, pl.ds(at, 128)] = piece(k, spot + part)
            else:
                vector_ref[i : i + 1, lanes(order_ref, k, 128)] = piece(k, spot)
        for part in range(6):
            table_ref[order_ref[k] * 6 + part] = piece(k, TABLE_SPOT + part)
    half = q_ref.shape[1] // 2

    @pl.loop(0, 2)
    def _(part):
        at = pl.ds(pl.multiple_of(part * half, half), half)
        for j, out_ref in ((1, k_ref), (0, q_ref), (2, v_ref)):
            weight = jnp.concatenate(
                [held[k, j * rows : (j + 1) * rows, at] for k in range(8)], axis=0
            )
            found = dot(x, weight)
            if j == 0:
                found = (found + vector_ref[Q_BIAS : Q_BIAS + 1, at]) * HEAD_DIM ** (-0.5)
            if j == 2:
                found = found + vector_ref[V_BIAS : V_BIAS + 1, at]
            out_ref[:, at] = found.astype(BF)


def project(order, x, blocks):
    count, width = x.shape
    return run(
        12,
        project_kernel,
        [((count, width), BF)] * 3 + [((16, 4 * width), F32), ((48, 1, 128), F32)],
        order,
        [x],
        blocks,
        [pltpu.VMEM((8,) + blocks[0].shape, BF), pltpu.SemaphoreType.DMA((8,))],
    )


def output_kernel(order_ref, c_ref, spread_ref, hidden_ref, vector_ref, *refs):
    blocks = refs[:8]
    context_ref, normed_ref, deviation_ref, low_ref, held, sem = refs[8:]
    copies = fetch(blocks, held, sem)
    context_ref[...] = dot(spread_ref[...], c_ref[...]).astype(BF)
    x = jnp.concatenate([context_ref[:, lanes(order_ref, k, 128)] for k in range(8)], axis=1)
    for copy in copies:
        copy.wait()
    width = hidden_ref.shape[1]
    normed_ref[...] = dot(x, held[...].reshape(-1, width))
    bias = vector_ref[O_BIAS : O_BIAS + 1, :width]
    gain = vector_ref[GAIN1 : GAIN1 + 1, :width]
    offset = vector_ref[SHIFT1 : SHIFT1 + 1, :width]

    def body(at, carry):
        normed, deviation = norm_parts(
            hidden_ref[at, :].astype(F32) + (normed_ref[at, :] + bias)
        )
        normed_ref[at, :] = normed
        deviation_ref[at, :] = deviation
        low_ref[at, :] = (normed * gain + offset).astype(BF)
        return carry

    each_rows(range(hidden_ref.shape[0] // ROWS_AT_ONCE), body, 0)


def output_block(order, context, spread, hidden, vectors, blocks):
    count, width = hidden.shape
    return run(
        7,
        output_kernel,
        [((count, width), BF), ((count, width), F32), ((count, 1), F32), ((count, width), BF)],
        order,
        [context, spread, hidden, vectors],
        blocks,
        [pltpu.VMEM((8,) + blocks[0].shape, BF), pltpu.SemaphoreType.DMA((8,))],
    )


def inner_kernel(tiles, order_ref, x_ref, vector_ref, *refs):
    blocks = refs[:8]
    active_out, steep_out, held, first, second, active_ref, steep_ref, sem, out_sem = refs[8:]
    rows = blocks[0].shape[0]
    size = active_out.shape[1] // tiles
    for t in range(tiles):
        at = slice(t * size, (t + 1) * size)
        for k in range(8):
            begin(blocks[k].at[:, at], held.at[t, pl.ds(k * rows, rows), :], sem.at[t])
    x = jnp.concatenate([x_ref[:, lanes(order_ref, k, 128)] for k in range(8)], axis=1)

    def place(t):
        return pl.ds(pl.multiple_of(t * size, size), size)

    def multiply(t, target):
        for k in range(8):
            pltpu.make_async_copy(
                blocks[k].at[:, :size], held.at[t, pl.ds(k * rows, rows), :], sem.at[t]
            ).wait()
        target[...] = dot(x, held[t])

    def bend(t, source):
        bias = vector_ref[I_BIAS : I_BIAS + 1, place(t)]
        for c in range(x_ref.shape[0] // ROWS_AT_ONCE):
            row = slice(c * ROWS_AT_ONCE, (c + 1) * ROWS_AT_ONCE)
            inner = source[row] + bias
            share = 0.5 + 0.5 * lax.erf(inner * 0.5**0.5)
            active_ref[row, place(t)] = (inner * share).astype(BF)
            steep_ref[row, place(t)] = (
                share + inner * jnp.exp(-0.5 * inner * inner) * (2 * np.pi) ** -0.5
            ).astype(BF)

    def leave(t):
        at = place(t)
        return (
            pltpu.make_async_copy(active_ref.at[:, at], active_out.at[:, at], out_sem.at[0, t]),
            pltpu.make_async_copy(steep_ref.at[:, at], steep_out.at[:, at], out_sem.at[1, t]),
        )

    second[...] = jnp.zeros_like(second)

    @pl.loop(0, tiles // 2)
    def _(half):
        t = 2 * half
        before = jnp.maximum(t - 1, 0)
        multiply(t, first)
        bend(before, second)
        multiply(t + 1, second)
        bend(t, first)

        @pl.when(half > 0)
        def _():
            for copy in leave(before):
                copy.start()

        for copy in leave(t):
            copy.start()

    bend(tiles - 1, second)
    for copy in leave(tiles - 1):
        copy.start()
    for t in range(tiles):
        finish(leave(t))


def inner_block(order, x, vectors, blocks, tiles=8):
    count, width = x.shape
    wide = blocks[0].shape[1]
    return run(
        14,
        partial(inner_kernel, tiles),
        [((count, wide), BF, 1), ((count, wide), BF, 1)],
        order,
        [x, vectors],
        blocks,
        [
            pltpu.VMEM((tiles, width, wide // tiles), BF),
            pltpu.VMEM((count, wide // tiles), F32),
            pltpu.VMEM((count, wide // tiles), F32),
            pltpu.VMEM((count, wide), BF),
            pltpu.VMEM((count, wide), BF),
            pltpu.SemaphoreType.DMA((tiles,)),
            pltpu.SemaphoreType.DMA((2, tiles)),
        ],
    )


def outer_kernel(order_ref, vector_ref, a_far, normed_far, upstream_far, *refs):
    blocks = refs[:8]
    (
        out_far,
        second_far,
        d_outer_far,
        sum_ref,
        held,
        a_ref,
        normed_ref,
        upstream_ref,
        out_ref,
        second_ref,
        d_outer_ref,
        sem,
        in_sem,
        out_sem,
    ) = refs[8:]
    width = out_ref.shape[1]
    rows = blocks[0].shape[0]
    weights, lefts = [], []
    for k in range(8):
        at = lanes(order_ref, k, rows)
        lefts.append(begin(a_far.at[:, at], a_ref.at[k], in_sem.at[k]))
        weights.append(begin(blocks[k], held.at[k], sem.at[k]))
    late = [
        begin(normed_far, normed_ref, in_sem.at[8]),
        begin(upstream_far, upstream_ref, in_sem.at[9]),
    ]
    finish([lefts[0], weights[0]])
    second_ref[...] = dot(a_ref[0], held[0])

    @pl.loop(1, 8)
    def _(k):
        pltpu.make_async_copy(
            a_far.at[:, lanes(order_ref, k, rows)], a_ref.at[k], in_sem.at[k]
        ).wait()
        pltpu.make_async_copy(blocks[1], held.at[k], sem.at[k]).wait()
        second_ref[...] += dot(a_ref[k], held[k])

    finish(late)
    gain1 = vector_ref[GAIN1 : GAIN1 + 1, :width]
    shift1 = vector_ref[SHIFT1 : SHIFT1 + 1, :width]
    gain2 = vector_ref[GAIN2 : GAIN2 + 1, :width]
    shift2 = vector_ref[SHIFT2 : SHIFT2 + 1, :width]
    bias = vector_ref[U_BIAS : U_BIAS + 1, :width]
    sums = (jnp.zeros((8, width), F32),) * 3
    leaving = []
    for g, group in enumerate(row_groups(out_ref.shape[0])):

        def body(at, sums):
            first_out = normed_ref[at, :] * gain1 + shift1
            normed, deviation = norm_parts(first_out + (second_ref[at, :] + bias))
            out_ref[at, :] = (normed * gain2 + shift2).astype(BF)
            upstream = upstream_ref[at, :].astype(F32)
            d_second = norm_back(normed, deviation, upstream * gain2)
            second_ref[at, :] = d_second
            low = d_second.astype(BF)
            d_outer_ref[at, :] = low
            return (
                sums[0] + fold_rows(upstream * normed),
                sums[1] + fold_rows(upstream),
                sums[2] + fold_rows(low.astype(F32)),
            )

        sums = each_rows(group, body, sums)
        at = pl.ds(group[0] * ROWS_AT_ONCE, len(group) * ROWS_AT_ONCE)
        for i, (source, target) in enumerate(
            ((out_ref, out_far), (second_ref, second_far), (d_outer_ref, d_outer_far))
        ):
            leaving.append(begin(source.at[at], target.at[at], out_sem.at[i, g]))
    for i in range(3):
        sum_ref[i : i + 1, :] = jnp.sum(sums[i], axis=0, keepdims=True)
    finish(leaving)


def outer_block(order, active, normed, upstream, vectors, blocks):
    count, width = normed.shape
    return run(
        11.5,
        outer_kernel,
        [
            ((count, width), BF, 1),
            ((count, width), F32, 1),
            ((count, width), BF, 1),
            ((8, width), F32),
        ],
        order,
        [vectors],
        blocks,
        [
            pltpu.VMEM((8,) + blocks[0].shape, BF),
            pltpu.VMEM((8, count, active.shape[1] // 8), BF),
            pltpu.VMEM((count, width), F32),
            pltpu.VMEM((count, width), BF),
            pltpu.VMEM((count, width), BF),
            pltpu.VMEM((count, width), F32),
            pltpu.VMEM((count, width), BF),
            pltpu.SemaphoreType.DMA((8,)),
            pltpu.SemaphoreType.DMA((10,)),
            pltpu.SemaphoreType.DMA((3, 4)),
        ],
        [active, normed, upstream],
    )


def inner_back_kernel(order_ref, d_ref, steep_far, *refs):
    blocks = refs[:8]
    out_far, sum_ref, held, steep_ref, out_ref, sem, in_sem, out_sem = refs[8:]
    rows = blocks[0].shape[0]
    copies = []
    for k in range(8):
        at = lanes(order_ref, k, rows)
        copies.append(
            [
                begin(blocks[k], held.at[k], sem.at[k]),
                begin(steep_far.at[:, at], steep_ref.at[k], in_sem.at[k]),
            ]
        )

    @pl.loop(0, 8)
    def _(k):
        at = lanes(order_ref, k, rows)
        pltpu.make_async_copy(blocks[0], held.at[k], sem.at[k]).wait()
        pltpu.make_async_copy(steep_far.at[:, at], steep_ref.at[k], in_sem.at[k]).wait()
        low = (dot(d_ref[...], held[k], NT) * steep_ref[k].astype(F32)).astype(BF)
        out_ref[k] = low
        sum_ref[:, at] = fold_rows(low.astype(F32))
        begin(out_ref.at[k], out_far.at[:, at], out_sem.at[k])

    for k in range(8):
        pltpu.make_async_copy(
            out_ref.at[k], out_far.at[:, lanes(order_ref, k, rows)], out_sem.at[k]
        ).wait()


def inner_back(order, d_outer, steep, blocks):
    count, wide = steep.shape
    return run(
        10,
        inner_back_kernel,
        [((count, wide), BF, 1), ((8, wide), F32)],
        order,
        [d_outer],
        blocks,
        [
            pltpu.VMEM((8,) + blocks[0].shape, BF),
            pltpu.VMEM((8, count, wide // 8), BF),
            pltpu.VMEM((8, count, wide // 8), BF),
            pltpu.SemaphoreType.DMA((8,)),
            pltpu.SemaphoreType.DMA((8,)),
            pltpu.SemaphoreType.DMA((8,)),
        ],
        [steep],
    )


def first_back_kernel(
    order_ref, d_ref, deviation_ref, vector_ref, second_far, normed_far, *refs
):
    blocks = refs[:8]
    (
        summed_far,
        low_far,
        sum_ref,
        held,
        second_ref,
        normed_ref,
        summed_ref,
        low_ref,
        sem,
        in_sem,
        out_sem,
    ) = refs[8:]
    copies = fetch(blocks, held, sem)
    late = [
        begin(second_far, second_ref, in_sem.at[0]),
        begin(normed_far, normed_ref, in_sem.at[1]),
    ]
    width = summed_ref.shape[1]
    rows = blocks[0].shape[0]

    @pl.loop(0, 4)
    def _(pair):
        k = 2 * pair
        pltpu.make_async_copy(blocks[0], held.at[k], sem.at[k]).wait()
        pltpu.make_async_copy(blocks[0], held.at[k + 1], sem.at[k + 1]).wait()
        weight = jnp.concatenate([held[k], held[k + 1]], axis=0)
        part = dot(d_ref[...], weight, NT)
        summed_ref[:, lanes(order_ref, k, rows)] = part[:, :rows]
        summed_ref[:, lanes(order_ref, k + 1, rows)] = part[:, rows:]

    finish(late)
    gain = vector_ref[GAIN1 : GAIN1 + 1, :width]
    sums = (jnp.zeros((8, width), F32),) * 3
    leaving = []
    for g, group in enumerate(row_groups(summed_ref.shape[0])):

        def body(at, sums):
            d_first = second_ref[at, :] + summed_ref[at, :]
            normed = normed_ref[at, :]
            d_summed = norm_back(normed, deviation_ref[at, :], d_first * gain)
            summed_ref[at, :] = d_summed
            low = d_summed.astype(BF)
            low_ref[at, :] = low
            return (
                sums[0] + fold_rows(d_first * normed),
                sums[1] + fold_rows(d_first),
                sums[2] + fold_rows(low.astype(F32)),
            )

        sums = each_rows(group, body, sums)
        at = pl.ds(group[0] * ROWS_AT_ONCE, len(group) * ROWS_AT_ONCE)
        leaving.append(begin(summed_ref.at[at], summed_far.at[at], out_sem.at[0, g]))
        leaving.append(begin(low_ref.at[at], low_far.at[at], out_sem.at[1, g]))
    for i in range(3):
        sum_ref[i : i + 1, :] = jnp.sum(sums[i], axis=0, keepdims=True)
    finish(leaving)


def first_back(order, d_inner, d_second, normed, deviation, vectors, blocks):
    count, width = normed.shape
    return run(
        16,
        first_back_kernel,
        [((count, width), F32, 1), ((count, width), BF, 1), ((8, width), F32)],
        order,
        [d_inner, deviation, vectors],
        blocks,
        [
            pltpu.VMEM((8,) + blocks[0].shape, BF),
            pltpu.VMEM((count, width), F32),
            pltpu.VMEM((count, width), F32),
            pltpu.VMEM((count, width), F32),
            pltpu.VMEM((count, width), BF),
            pltpu.SemaphoreType.DMA((8,)),
            pltpu.SemaphoreType.DMA((2,)),
            pltpu.SemaphoreType.DMA((2, 4)),
        ],
        [d_second, normed],
    )


def context_back_kernel(order_ref, d_ref, spread_ref, *refs):
    blocks = refs[:8]
    out_ref, held, kept, sem = refs[8:]
    copies = fetch(blocks, held, sem)
    rows = blocks[0].shape[0]
    for copy in copies:
        copy.wait()

    @pl.loop(0, 4)
    def _(pair):
        k = 2 * pair
        weight = jnp.concatenate([held[k], held[k + 1]], axis=0)
        part = dot(d_ref[...], weight, NT).astype(BF)
        kept[:, lanes(order_ref, k, rows)] = part[:, :rows]
        kept[:, lanes(order_ref, k + 1, rows)] = part[:, rows:]

    out_ref[...] = dot(spread_ref[...], kept[...]).astype(BF)


def context_back(order, d_attn, spread, blocks):
    count, width = d_attn.shape
    return run(
        6.5,
        context_back_kernel,
        [((spread.shape[0], width), BF)],
        order,
        [d_attn, spread],
        blocks,
        [
            pltpu.VMEM((8,) + blocks[0].shape, BF),
            pltpu.VMEM((count, width), BF),
            pltpu.SemaphoreType.DMA((8,)),
        ],
    )[0]


def input_back_kernel(order_ref, d_ref, spread_ref, summed_far, *refs):
    blocks = refs[:8]
    out_far, held, kept, summed_ref, out_ref, sem, in_sem, out_sem = refs[8:]
    copies = fetch(blocks, held, sem)
    late = begin(summed_far, summed_ref, in_sem.at[0])
    rows = (blocks[0].shape[0] - 16) // 3
    width = summed_ref.shape[1]

    @pl.loop(0, 3)
    def _(j):
        at = pl.ds(pl.multiple_of(j * width, width), width)
        kept[:, at] = dot(spread_ref[...], d_ref[:, at]).astype(BF)

    finish(copies)
    late.wait()

    @pl.loop(0, 4)
    def _(pair):
        k = 2 * pair
        weight = jnp.concatenate(
            [
                jnp.concatenate(
                    [held[k, j * rows : (j + 1) * rows], held[k + 1, j * rows : (j + 1) * rows]],
                    axis=0,
                )
                for j in range(3)
            ],
            axis=1,
        )
        part = dot(kept[...], weight, NT)
        for i in range(2):
            at = lanes(order_ref, k + i, rows)
            out_ref[k + i] = summed_ref[:, at] + part[:, i * rows : (i + 1) * rows]
            begin(out_ref.at[k + i], out_far.at[:, at], out_sem.at[k + i])

    for k in range(8):
        at = lanes(order_ref, k, rows)
        pltpu.make_async_copy(out_ref.at[k], out_far.at[:, at], out_sem.at[k]).wait()


def input_back(order, d_mixed, spread, d_summed, blocks):
    count, width = d_summed.shape
    return run(
        12.5,
        input_back_kernel,
        [((count, width), F32, 1)],
        order,
        [d_mixed, spread],
        blocks,
        [
            pltpu.VMEM((8,) + blocks[0].shape, BF),
            pltpu.VMEM((count, 3 * width), BF),
            pltpu.VMEM((count, width), F32),
            pltpu.VMEM((8, count, width // 8), F32),
            pltpu.SemaphoreType.DMA((8,)),
            pltpu.SemaphoreType.DMA((1,)),
            pltpu.SemaphoreType.DMA((8,)),
        ],
        [d_summed],
    )[0]


def small_kernel(
    order_ref,
    slide_ref,
    box_ref,
    bias_ref,
    first_ref,
    inner_ref,
    second_ref,
    *refs,
):
    outs, flat = refs[:8], refs[8]
    spot = one_hot(
        (2 * PAGE, NB),
        lambda c, bucket: (jnp.clip(PAGE - 1 - c, -64, 63) + 64 == bucket) & (c < 2 * PAGE - 1),
    ).astype(F32)
    by_head = [precise(slide_ref[...], spot)]
    by_head += [pltpu.roll(box_ref[i], 65, 1) for i in range(2)]
    heads = one_hot((NB, HEADS), lambda r, c: r % 16 == c).astype(F32)
    mine = one_hot((NB, NB), lambda r, c: r // 16 == c % 8)
    rows = one_hot((16, NB), lambda r, c: c // 8 == r).astype(F32)
    for kind in range(3):
        spread = jnp.where(mine, precise(heads, by_head[kind]), 0.0)
        found = precise(rows, spread, NT)
        for i in range(16):
            flat[16 * kind + i] = found[i : i + 1]
    width = first_ref.shape[1]
    bias = jnp.sum(bias_ref[...], axis=0, keepdims=True)
    inner = jnp.sum(inner_ref[...], axis=0, keepdims=True)
    bias_ref[0:1, :] = bias
    inner_ref[0:1, :] = inner
    for k in range(8):
        out_ref = outs[k]
        at = lanes(order_ref, k, 128)
        out_ref[0:1, :] = bias_ref[0:1, at]
        out_ref[1:2, :] = bias_ref[
            0:1, pl.ds(pl.multiple_of(2 * width + order_ref[k] * 128, 128), 128)
        ]
        out_ref[2:3, :] = first_ref[2:3, at]
        out_ref[3:5, :] = first_ref[0:2, at]
        for part in range(4):
            piece = pl.ds(pl.multiple_of(order_ref[k] * 512 + part * 128, 128), 128)
            out_ref[5 + part : 6 + part, :] = inner_ref[0:1, piece]
        out_ref[9:10, :] = second_ref[2:3, at]
        out_ref[10:12, :] = second_ref[0:2, at]
        for part in range(6):
            out_ref[12 + part : 13 + part, :] = flat[order_ref[k] * 6 + part]
        out_ref[18:, :] = jnp.zeros((6, 128), F32)


def small_blocks(order, sums):
    return pl.pallas_call(
        small_kernel,
        out_shape=(jax.ShapeDtypeStruct((24, 128), F32),) * 8,
        in_specs=[pl.BlockSpec(memory_space=pltpu.SMEM)]
        + [pl.BlockSpec(memory_space=pltpu.VMEM)] * 6,
        out_specs=(pl.BlockSpec(memory_space=pltpu.VMEM),) * 8,
        scratch_shapes=[pltpu.VMEM((48, 1, 128), F32)],
        compiler_params=pltpu.CompilerParams(vmem_limit_bytes=VMEM_LIMIT),
        cost_estimate=cost(3),
    )(order, *sums)


def on_device(line, mesh_size, *args):
    (
        hidden_in,
        cotangent,
        segment_ids,
        box_left,
        box_top,
        query_weight,
        query_bias,
        key_weight,
        value_weight,
        value_bias,
        output_weight,
        output_bias,
        first_gain,
        first_shift,
        inner_weight,
        inner_bias,
        outer_weight,
        outer_bias,
        second_gain,
        second_shift,
        bucket_table,
    ) = args
    slot_count = segment_ids.shape[1]
    width = hidden_in.shape[1]
    vectors = (
        query_bias,
        value_bias,
        output_bias,
        first_gain,
        first_shift,
        inner_bias,
        outer_bias,
        second_gain,
        second_shift,
        bucket_table,
    )
    phase = lax.optimization_barrier
    if line:
        order = block_order(lax.axis_index("fsdp"))
        packed = pack((query_weight, key_weight, value_weight), vectors)
        in_blocks = [packed, hop(packed, NEAR), hop(packed, FAR)]
    else:
        order = jnp.arange(8, dtype=jnp.int32)

        def whole(shard):
            return lax.all_gather(shard, "fsdp", axis=0, tiled=True)

        def blocks_of(shard):
            full = whole(shard)
            return list(full.reshape(8, full.shape[0] // 8, full.shape[1]))

        small = jnp.concatenate([whole(item).reshape(8, -1) for item in vectors], axis=1)
        small = jnp.pad(small, ((0, 0), (0, 16 * width - small.shape[1])))
        in_blocks = jnp.concatenate(
            [whole(item).reshape(8, -1, width) for item in (query_weight, key_weight, value_weight)]
            + [small.reshape(8, 16, width)],
            axis=1,
        )
        in_blocks = list(in_blocks)
        output_blocks = blocks_of(output_weight)
        inner_blocks = blocks_of(inner_weight)
        outer_blocks = blocks_of(outer_weight)

    slot = lax.iota(jnp.int32, slot_count)
    pages = lax.iota(jnp.int32, PAGES)
    segments = segment_ids[0]
    member = segments[None, :] == pages[:, None]
    lengths = jnp.sum(member, axis=1, dtype=jnp.int32)
    starts = jnp.sum(segments[None, :] < pages[:, None], axis=1, dtype=jnp.int32)
    start_of = jnp.sum(jnp.where(member, starts[:, None], 0), axis=0)
    target = segments * PAGE + slot - start_of
    padded = lax.iota(jnp.int32, PAGES * PAGE)
    spread = (padded[:, None] == target[None, :]).astype(BF)
    gather = (padded[None, :] == target[:, None]).astype(BF)
    coords = lax.iota(jnp.int32, NB) % 64
    sides = jnp.where(padded[None, :NB] < 64, box_left[0][:, None], box_top[0][:, None])
    boxes = dot(spread, (sides == coords[None, :]).astype(BF)).astype(BF)
    turned = jnp.where(padded[:NB, None] < 64, box_top[0][None, :], box_left[0][None, :])
    turned = (turned == 63 - coords[:, None]).astype(BF)
    flipped = dot(turned, spread, NT).astype(BF)
    hidden = dot(spread, hidden_in).astype(BF)

    if line:
        in_blocks, hidden, boxes, flipped, gather, spread, inner_weight = phase(
            (in_blocks, hidden, boxes, flipped, gather, spread, inner_weight)
        )
        own, near, far = in_blocks
        both = hop(near, FAR)
        twins = [hop(item, TWIN) for item in (own, near, far)]
        inner_near = hop(inner_weight, NEAR)
        both, twins, inner_near, inner_weight, output_weight = phase(
            (both, twins, inner_near, inner_weight, output_weight)
        )
        in_blocks = [own, near, far, both] + twins + [hop(both, TWIN)]
        inner_far = hop(inner_weight, FAR)
        output_near, output_far = hop(output_weight, NEAR), hop(output_weight, FAR)
    queries, keys, values, vector, table = project(order, hidden, in_blocks)
    lookup, slide = make_tables(table)
    if line:
        (
            queries,
            keys,
            values,
            lookup,
            slide,
            inner_near,
            inner_far,
            output_near,
            output_far,
            outer_weight,
        ) = phase(
            (
                queries,
                keys,
                values,
                lookup,
                slide,
                inner_near,
                inner_far,
                output_near,
                output_far,
                outer_weight,
            )
        )
        outer_near = hop(outer_weight, NEAR)
        output_blocks = [output_weight, output_near, output_far, hop(output_near, FAR)]
    context, prob = attend(lengths, queries, keys, values, boxes, lookup, slide)
    if line:
        context, outer_near, output_blocks, inner_near, inner_far = phase(
            (context, outer_near, output_blocks, inner_near, inner_far)
        )
        inner_blocks = [inner_weight, inner_near, inner_far, hop(inner_near, FAR)]
        outer_far = hop(outer_weight, FAR)
        output_blocks = output_blocks + [hop(item, TWIN) for item in output_blocks]
        inner_twins = [hop(item, TWIN) for item in inner_blocks[:3]]
    context, normed, deviation, first_low = output_block(
        order, context, gather, hidden_in, vector, output_blocks
    )
    if line:
        first_low, inner_blocks, inner_twins, outer_near, outer_far = phase(
            (first_low, inner_blocks, inner_twins, outer_near, outer_far)
        )
        outer_blocks = [outer_weight, outer_near, outer_far, hop(outer_near, FAR)]
        inner_blocks = inner_blocks + inner_twins + [hop(inner_blocks[3], TWIN)]
        outer_twins = [hop(item, TWIN) for item in outer_blocks[:3]]
    active, steep = inner_block(order, first_low, vector, inner_blocks)
    if line:
        active, outer_blocks, outer_twins = phase((active, outer_blocks, outer_twins))
        outer_blocks = outer_blocks + outer_twins + [hop(outer_blocks[3], TWIN)]
    layer_out, d_second, d_outer, second_sums = outer_block(
        order, active, normed, cotangent, vector, outer_blocks
    )

    if line:
        send = turned_blocks(order, 4, active, d_outer)
        d_outer, send = phase((d_outer, send))
        other2 = to_twin(send)
    d_inner, inner_sums = inner_back(order, d_outer, steep, outer_blocks)
    if line:
        d_inner, other2 = phase((d_inner, other2))
        stay2, away2 = turned_blocks(order, 0, active, d_outer, other2)
        d_inner, stay2, away2 = phase((d_inner, stay2, away2))
        other2 = hop(away2, FAR)
        d_inner, stay2 = phase((d_inner, stay2))
    d_summed, d_attn, first_sums = first_back(
        order, d_inner, d_second, normed, deviation, vector, inner_blocks
    )
    if line:
        pairs1 = ((first_low, d_inner), (context, d_attn))
        send = grad_blocks(order, 4, pairs1, 1024)
        d_attn, send, stay2, other2 = phase((d_attn, send, stay2, other2))
        other1 = to_twin(send)
        stay2, away2 = fold_far(stay2, other2)
        other2 = hop(away2, NEAR)
    d_context = context_back(order, d_attn, spread, output_blocks)
    if line:
        d_context, other1, stay2 = phase((d_context, other1, stay2))
        stay1, away1 = grad_blocks(order, 0, pairs1, 1024, other1)
        d_context, stay1, away1, stay2, other2 = phase(
            (d_context, stay1, away1, stay2, other2)
        )
        other1 = hop(away1, FAR)
        kept2, sent2 = cut(stay2 + other2, 1)
        other2 = trade(sent2, 1)
    d_mixed, slide_sum, box_sum, bias_sum = attend_back(
        queries, keys, values, d_context, boxes, flipped, prob
    )
    sums = (slide_sum, box_sum, bias_sum, first_sums, inner_sums, second_sums)
    if line:
        pairs = ((hidden, d_mixed),)
        d_mixed, kept2, other2, stay1, sums = phase((d_mixed, kept2, other2, stay1, sums))
        kept2, sent2 = cut(kept2 + other2, 2)
        other2 = trade(sent2, 2)
        send = grad_blocks(order, 4, pairs, 1024)
        d_mixed, send, kept2, other2, stay1, other1, sums = phase(
            (d_mixed, send, kept2, other2, stay1, other1, sums)
        )
        other = to_twin(send)
        stay1, away1 = fold_far(stay1, other1)
        other1 = hop(away1, NEAR)
        kept2 = kept2 + other2
        other2 = trade(kept2, 2)
    small = small_blocks(order, sums)
    if line:
        d_mixed, other, small, stay1, kept2 = phase((d_mixed, other, small, stay1, kept2))
        stay, away = grad_blocks(order, 0, pairs, 1024, other)
        d_mixed, stay, away, stay1, other1, kept2, other2, small = phase(
            (d_mixed, stay, away, stay1, other1, kept2, other2, small)
        )
        other = hop(away, FAR)
        small_other = to_twin(small[4:])
        kept1, sent1 = cut(stay1 + other1, 1)
        other1 = trade(sent1, 1)
    input_grad = input_back(order, d_mixed, gather, d_summed, in_blocks)
    if line:
        stay, other, input_grad, small, small_other, kept1, other1, kept2, other2 = phase(
            (stay, other, input_grad, small, small_other, kept1, other1, kept2, other2)
        )
        stay, away = fold_far(stay, other)
        other = hop(away, NEAR)
        kept1, sent1 = cut(kept1 + other1, 2)
        other1 = trade(sent1, 2)
        kept2 = paste(kept2, other2, 2)
        other2 = trade(kept2, 1)
        small = [small[i] + small_other[i] for i in range(4)]
        small_other = hop(jnp.stack(small[2:]), FAR)
        stay, other, small, small_other, kept1, other1, kept2, other2 = phase(
            (stay, other, small, small_other, kept1, other1, kept2, other2)
        )
        kept, sent = cut(stay + other, 1)
        other = trade(sent, 1)
        kept1 = kept1 + other1
        other1 = trade(kept1, 2)
        small = small[0] + small_other[0], small[1] + small_other[1]
        small_other = hop(small[1], NEAR)
        kept, other, kept1, other1, small, small_other, kept2, other2 = phase(
            (kept, other, kept1, other1, small, small_other, kept2, other2)
        )
        kept, sent = cut(kept + other, 2)
        other = trade(sent, 2)
        kept1 = paste(kept1, other1, 2)
        other1 = trade(kept1, 1)
        small = small[0] + small_other
        small_other = trade(small, 1)
        outer_own = paste(kept2, other2, 1).T.astype(F32)
        kept, other, kept1, other1, small, small_other, outer_own = phase(
            (kept, other, kept1, other1, small, small_other, outer_own)
        )
        kept = kept + other
        other = trade(kept, 2)
        small = small + small_other
        small_other = trade(small, 2)
        inner_own = paste(kept1, other1, 1).astype(F32)
        kept, other, small, small_other, inner_own = phase(
            (kept, other, small, small_other, inner_own)
        )
        kept = paste(kept, other, 2)
        other = trade(kept, 1)
        small = (small + small_other).reshape(-1)
        kept, other, small = phase((kept, other, small))
        in_own = paste(kept, other, 1)
        inner_own, output_own = inner_own[:, : 4 * width], inner_own[:, 4 * width :]
        cuts = np.cumsum([0] + [item.shape[0] for item in vectors])
        owned = [small[cuts[i] : cuts[i + 1]] for i in range(len(vectors))]
    else:

        def reduce(value):
            value = lax.psum_scatter(value, "fsdp", scatter_dimension=0, tiled=True)
            return lax.psum(value, "dp")

        small = jnp.stack(small)[:, :18].reshape(8, -1)
        edges = np.cumsum([0] + [item.shape[0] * mesh_size // 8 for item in vectors])
        owned = [
            reduce(small[:, edges[i] : edges[i + 1]].reshape(-1)) for i in range(len(vectors))
        ]
        outer_own = reduce(dot(active, d_outer, TN).astype(BF))
        inner_own = reduce(dot(first_low, d_inner, TN).astype(BF))
        output_own = reduce(dot(context, d_attn, TN).astype(BF))
        in_own = reduce(dot(hidden, d_mixed, TN).astype(BF))
    in_own = in_own.astype(F32)
    return (
        layer_out,
        input_grad,
        in_own[:, :width],
        owned[0],
        in_own[:, width : 2 * width],
        in_own[:, 2 * width :],
        owned[1],
        output_own.astype(F32),
        owned[2],
        owned[3],
        owned[4],
        inner_own.astype(F32),
        owned[5],
        outer_own.astype(F32),
        owned[6],
        owned[7],
        owned[8],
        owned[9],
    )


def solution(mesh):
    line = mesh.shape["fsdp"] == 8 and mesh.shape["dp"] == 4
    both, across, flat = P(("fsdp", "dp"), None), P("fsdp", None), P("fsdp")
    return jax.shard_map(
        partial(on_device, line, mesh.shape["fsdp"]),
        mesh=mesh,
        in_specs=(both,) * 5
        + (across, flat, across, across, flat, across, flat, flat, flat)
        + (across, flat, across, flat, flat, flat, flat),
        out_specs=(both, both)
        + (across, flat, across, across, flat, across, flat, flat, flat)
        + (across, flat, across, flat, flat, flat, flat),
        check_vma=False,
    )
```

```python
from functools import partial

import jax
import jax.numpy as jnp
import numpy as np
from jax import lax
from jax.experimental import pallas as pl
from jax.experimental.pallas import tpu as pltpu
from jax.sharding import PartitionSpec as P

HEADS = 16
HEAD_DIM = 64
PAIRS = HEADS // 2
NB = 128
PAGE = 128
PAGES = 8
EPSILON = 1e-05
BLOCKED = -1e30
BF = jnp.bfloat16
F32 = jnp.float32
VMEM_LIMIT = 62 * 1024 * 1024
SCALE = 0.3


def cost(microseconds):
    return pl.CostEstimate(
        flops=1 + int(microseconds * SCALE * 1e9), bytes_accessed=1, transcendentals=0
    )


NT = (((1,), (1,)), ((), ()))
TN = (((0,), (0,)), ((), ()))


def dot(left_side, right_side, dims=(((1,), (0,)), ((), ()))):
    return lax.dot_general(left_side, right_side, dims, preferred_element_type=F32)


def flips(bit_of):
    return [(i, i ^ bit_of(i & 1)) for i in range(8)]


NEAR = flips(lambda c: 2 if c else 4)
FAR = flips(lambda c: 4 if c else 2)
TWIN = flips(lambda c: 1)


def block_order(me):
    rel0 = np.array([0, 4, 2, 6, 1, 3, 5, 7], np.int32)
    rel1 = np.array([0, 2, 4, 6, 1, 5, 3, 7], np.int32)
    rel = jnp.where((me & 1) == 0, rel0, rel1)
    return jnp.bitwise_xor(me, rel).astype(jnp.int32)


def hop(value, pairs):
    return lax.ppermute(value, "fsdp", pairs)


def after(value, *others):
    return lax.optimization_barrier((value,) + others)[0]


def fold_far(stay, other):
    return stay[0] + other[0], stay[1] + other[1]


def trade(value, bit):
    return lax.ppermute(value, "dp", [(i, i ^ bit) for i in range(4)])


def cut(value, bit):
    high = (lax.axis_index("dp") & bit) // bit
    halves = value.reshape((2, value.shape[0] // 2) + value.shape[1:])
    return (
        lax.dynamic_index_in_dim(halves, high, 0, keepdims=False),
        lax.dynamic_index_in_dim(halves, 1 - high, 0, keepdims=False),
    )


def paste(mine, other, bit):
    high = (lax.axis_index("dp") & bit) != 0
    return jnp.concatenate([jnp.where(high, other, mine), jnp.where(high, mine, other)], axis=0)


def pack_kernel(shapes, *refs):
    items, out_ref, sem = refs[: len(shapes) + 3], refs[-2], refs[-1]
    rows = items[0].shape[0]
    copies = [
        pltpu.make_async_copy(items[j], out_ref.at[pl.ds(j * rows, rows), :], sem.at[j])
        for j in range(3)
    ]
    for copy in copies:
        copy.start()
    spot = 0
    out_ref[3 * rows :, :] = jnp.zeros((16, out_ref.shape[1]), BF)
    for item, count in zip(items[3:], shapes):
        for i in range(count):
            row, lane = 3 * rows + spot // 8, spot % 8 * 128
            out_ref[row : row + 1, lane : lane + 128] = item[i : i + 1, :]
            spot += 1
    for copy in copies:
        copy.wait()


def pack(weights, vectors):
    rows, columns = weights[0].shape
    vectors = [item.reshape(-1, 128) for item in vectors]
    return pl.pallas_call(
        partial(pack_kernel, tuple(item.shape[0] for item in vectors)),
        out_shape=jax.ShapeDtypeStruct((3 * rows + 16, columns), BF),
        in_specs=[pl.BlockSpec(memory_space=pltpu.HBM)] * 3
        + [pl.BlockSpec(memory_space=pltpu.VMEM)] * len(vectors),
        out_specs=pl.BlockSpec(memory_space=pltpu.VMEM),
        scratch_shapes=[pltpu.SemaphoreType.DMA((3,))],
        cost_estimate=cost(3),
    )(*weights, *vectors)


def emit(found, k, others, outs):
    if others:
        outs[k // 2][k % 2] = (found + others[k][...].astype(F32)).astype(BF)
    else:
        outs[k][...] = found.astype(BF)


def turned_kernel(first, fold, order_ref, right_ref, left_far, *refs):
    others, outs = refs[: 4 * fold], refs[4 * fold : -7]
    lefts, turned, came, left, in_sem, other_sem, out_sem = refs[-7:]
    rows = lefts.shape[2]
    copies = [
        begin(left_far.at[:, lanes(order_ref, first + k, rows)], lefts.at[k], in_sem.at[k])
        for k in range(4)
    ]
    arrivals = [begin(others[k], came.at[k], other_sem.at[k]) for k in range(4 * fold)]
    turned[...] = right_ref[...].T
    leaving = []
    for k in range(4):
        copies[k].wait()
        found = dot(turned[...], lefts[k])
        if fold:
            arrivals[k].wait()
            found = found + came[k].astype(F32)
        left[k] = found.astype(BF)
        target = outs[k // 2].at[k % 2] if fold else outs[k]
        leaving.append(begin(left.at[k], target, out_sem.at[k]))
    finish(leaving)


def turned_blocks(order, first, left, right, others=()):
    depth, rows, columns = left.shape[0], left.shape[1] // 8, right.shape[1]
    fold = int(bool(others))
    far = pl.BlockSpec(memory_space=pltpu.HBM)
    if fold:
        shapes = (jax.ShapeDtypeStruct((2, columns, rows), BF),) * 2
    else:
        shapes = (jax.ShapeDtypeStruct((columns, rows), BF),) * 4
    return pl.pallas_call(
        partial(turned_kernel, first, fold),
        out_shape=shapes,
        in_specs=[
            pl.BlockSpec(memory_space=pltpu.SMEM),
            pl.BlockSpec(memory_space=pltpu.VMEM),
            far,
        ]
        + [far] * (4 * fold),
        out_specs=(far,) * len(shapes),
        scratch_shapes=[
            pltpu.VMEM((4, depth, rows), BF),
            pltpu.VMEM((columns, depth), BF),
            pltpu.VMEM((4, columns, rows) if fold else (1, 16, 128), BF),
            pltpu.VMEM((4, columns, rows), BF),
            pltpu.SemaphoreType.DMA((4,)),
            pltpu.SemaphoreType.DMA((4,)),
            pltpu.SemaphoreType.DMA((4,)),
        ],
        compiler_params=pltpu.CompilerParams(vmem_limit_bytes=VMEM_LIMIT),
        cost_estimate=cost(7),
    )(order, right, left, *others)


def grad_kernel(first, counts, fold, order_ref, *refs):
    pieces = len(counts)
    lefts, rights = refs[:pieces], refs[pieces : 2 * pieces]
    others = refs[2 * pieces : 2 * pieces + 4 * fold]
    outs, turned = refs[2 * pieces + 4 * fold : -pieces], refs[-pieces:]
    i = pl.program_id(0)
    rows = turned[0].shape[0] // 4
    start = 0
    for left_ref, right_ref, kept, count in zip(lefts, rights, turned, counts):

        @pl.when(i == start)
        def _():
            for k in range(4):
                kept[k * rows : (k + 1) * rows, :] = left_ref[
                    :, lanes(order_ref, first + k, rows)
                ].T

        @pl.when((i >= start) & (i < start + count))
        def _():
            found = dot(kept[...], right_ref[...])
            for k in range(4):
                emit(found[k * rows : (k + 1) * rows], k, others, outs)

        start += count


def grad_blocks(order, first, pairs, tile, others=()):
    rows = pairs[0][0].shape[1] // 8
    counts = [right.shape[1] // tile for _, right in pairs]
    total = sum(counts)
    fold = int(bool(others))
    in_specs = [pl.BlockSpec(left.shape, lambda i, n: (0, 0)) for left, _ in pairs]
    start = 0
    for (_, right), count in zip(pairs, counts):

        def at(i, n, start=start, count=count):
            return 0, jnp.clip(i - start, 0, count - 1)

        in_specs.append(pl.BlockSpec((right.shape[0], tile), at))
        start += count
    one = pl.BlockSpec((rows, tile), lambda i, n: (0, i))
    if fold:
        out_specs = (pl.BlockSpec((2, rows, tile), lambda i, n: (0, 0, i)),) * 2
        shapes = (jax.ShapeDtypeStruct((2, rows, total * tile), BF),) * 2
    else:
        out_specs = (one,) * 4
        shapes = (jax.ShapeDtypeStruct((rows, total * tile), BF),) * 4
    return pl.pallas_call(
        partial(grad_kernel, first, tuple(counts), fold),
        grid_spec=pltpu.PrefetchScalarGridSpec(
            num_scalar_prefetch=1,
            grid=(total,),
            in_specs=in_specs + [one] * (4 * fold),
            out_specs=out_specs,
            scratch_shapes=[pltpu.VMEM((4 * rows, left.shape[0]), BF) for left, _ in pairs],
        ),
        out_shape=shapes,
        compiler_params=pltpu.CompilerParams(vmem_limit_bytes=VMEM_LIMIT),
        cost_estimate=cost(2 * total),
    )(
        order,
        *[left for left, _ in pairs],
        *[right for _, right in pairs],
        *others,
    )


def to_twin(blocks):
    return [hop(block, TWIN) for block in blocks]


def lanes(order_ref, k, size):
    return pl.ds(pl.multiple_of(order_ref[k] * size, size), size)


def one_hot(shape, test):
    row = lax.broadcasted_iota(jnp.int32, shape, 0)
    lane = lax.broadcasted_iota(jnp.int32, shape, 1)
    return test(row, lane)


def precise(left_side, right_side, dims=(((1,), (0,)), ((), ()))):
    return lax.dot_general(
        left_side, right_side, dims, precision=lax.Precision.HIGHEST, preferred_element_type=F32
    )


def tables_kernel(table_ref, lookup_ref, slide_ref, flat):
    for i in range(48):
        flat[i : i + 1, :] = table_ref[i]
    wide = one_hot((NB, 16), lambda r, c: r // 8 == c).astype(F32)
    mine = one_hot((NB, NB), lambda r, c: c // 16 == r % 8)
    heads = one_hot((HEADS, NB), lambda r, c: c % 16 == r).astype(F32)
    by_head = []
    for kind in range(3):
        rows = jnp.where(mine, precise(wide, flat[16 * kind : 16 * (kind + 1), :]), 0.0)
        by_head.append(precise(heads, rows, NT))
    spot = one_hot(
        (2 * PAGE, NB),
        lambda m, bucket: jnp.clip(jnp.where(m <= PAGE, -m, 2 * PAGE - m), -64, 63) + 64 == bucket,
    ).astype(F32)
    position = precise(by_head[0], spot, NT)
    left_all = pltpu.roll(by_head[1], 64, 1)
    top_all = pltpu.roll(by_head[2], 64, 1)
    same = one_hot((NB, NB), lambda r, c: (r < 64) == (c < 64))
    for head in range(HEADS):
        base = jnp.broadcast_to(position[head : head + 1, :], (PAGE, 2 * PAGE))
        slid = pltpu.roll(base, 0, 1, stride=1, stride_axis=0)
        half = (head % 2) * PAGE
        slide_ref[head // 2, :, half : half + PAGE] = slid[:, :PAGE]
        left = jnp.broadcast_to(left_all[head : head + 1, :], (64, NB))
        top = jnp.broadcast_to(top_all[head : head + 1, :], (64, NB))
        slid = pltpu.roll(
            jnp.concatenate([left, top], axis=0), 0, 1, stride=1, stride_axis=0
        )
        lookup_ref[:, head * NB : (head + 1) * NB] = jnp.where(same, slid, 0.0).astype(BF)


def make_tables(table):
    return pl.pallas_call(
        tables_kernel,
        out_shape=(
            jax.ShapeDtypeStruct((NB, HEADS * NB), BF),
            jax.ShapeDtypeStruct((PAIRS, PAGE, 2 * PAGE), F32),
        ),
        scratch_shapes=[pltpu.VMEM((48, NB), F32)],
        compiler_params=pltpu.CompilerParams(vmem_limit_bytes=VMEM_LIMIT),
        cost_estimate=cost(3),
    )(table)


def split_heads(tile):
    lane = lax.broadcasted_iota(jnp.int32, tile.shape, 1)
    zero = jnp.zeros_like(tile)
    return jnp.concatenate(
        [jnp.where(lane < HEAD_DIM, tile, zero), jnp.where(lane >= HEAD_DIM, tile, zero)],
        axis=0,
    )


def join_heads(tall):
    lane = lax.broadcasted_iota(jnp.int32, (PAGE, NB), 1)
    return jnp.where(lane < HEAD_DIM, tall[:PAGE, :NB], tall[PAGE:, :NB])


def attend_kernel(
    length_ref, q_ref, k_ref, v_ref, box_ref, lookup_ref, slide_ref, context_ref, prob_ref, logit
):
    length = length_ref[pl.program_id(0)]
    inside = lax.broadcasted_iota(jnp.int32, (PAGE, 2 * PAGE), 0) < length
    boxes = box_ref[...]
    for pair in range(PAIRS):
        at = slice(pair * NB, (pair + 1) * NB)
        looked = dot(boxes, lookup_ref[:, 2 * pair * NB : 2 * (pair + 1) * NB]).astype(BF)
        looked = jnp.concatenate([looked[:, :NB], looked[:, NB:]], axis=0)
        asked = jnp.concatenate([split_heads(q_ref[:, at]), looked], axis=1)
        offered = jnp.concatenate([k_ref[:, at], boxes], axis=1)
        logit[pair] = dot(offered, asked, NT)
    for pair in range(PAIRS):
        logits = jnp.where(inside, logit[pair] + slide_ref[pair], BLOCKED)
        peak = jnp.max(logits, axis=0, keepdims=True)
        grown = jnp.exp(logits - peak)
        total = jnp.sum(grown, axis=0, keepdims=True)
        prob_ref[0, pair] = (grown * (1.0 / total)).astype(BF)
    for pair in range(PAIRS):
        at = slice(pair * NB, (pair + 1) * NB)
        context_ref[:, at] = join_heads(dot(prob_ref[0, pair], v_ref[:, at], TN)).astype(BF)


def attend(lengths, queries, keys, values, boxes, lookup, slide):
    wide = pl.BlockSpec((PAGE, HEADS * HEAD_DIM), lambda i, n: (i, 0))
    return pl.pallas_call(
        attend_kernel,
        grid_spec=pltpu.PrefetchScalarGridSpec(
            num_scalar_prefetch=1,
            grid=(PAGES,),
            in_specs=[
                wide,
                wide,
                wide,
                pl.BlockSpec((PAGE, NB), lambda i, n: (i, 0)),
                pl.BlockSpec((NB, HEADS * NB), lambda i, n: (0, 0)),
                pl.BlockSpec((PAIRS, PAGE, 2 * PAGE), lambda i, n: (0, 0, 0)),
            ],
            out_specs=(
                wide,
                pl.BlockSpec((1, PAIRS, PAGE, 2 * PAGE), lambda i, n: (i, 0, 0, 0)),
            ),
            scratch_shapes=[pltpu.VMEM((PAIRS, PAGE, 2 * PAGE), F32)],
        ),
        out_shape=(
            jax.ShapeDtypeStruct((PAGES * PAGE, HEADS * HEAD_DIM), BF),
            jax.ShapeDtypeStruct((PAGES, PAIRS, PAGE, 2 * PAGE), BF),
        ),
        compiler_params=pltpu.CompilerParams(vmem_limit_bytes=VMEM_LIMIT),
        cost_estimate=cost(13.5),
    )(lengths, queries, keys, values, boxes, lookup, slide)


def attend_back_kernel(
    q_ref,
    k_ref,
    v_ref,
    g_ref,
    box_ref,
    flip_ref,
    prob_ref,
    grad_ref,
    slide_sum_ref,
    box_sum_ref,
    bias_sum_ref,
    slide_acc,
    box_acc,
    d_prob,
    d_logit,
    boxed,
):
    page = pl.program_id(0)

    @pl.when(page == 0)
    def _():
        slide_acc[...] = jnp.zeros_like(slide_acc)
        box_acc[...] = jnp.zeros_like(box_acc)
        bias_sum_ref[...] = jnp.zeros_like(bias_sum_ref)

    boxes = box_ref[...]
    width = HEADS * HEAD_DIM
    scale = HEAD_DIM ** (-0.5)
    for pair in range(PAIRS):
        at = slice(pair * NB, (pair + 1) * NB)
        pulled = split_heads(g_ref[:, at])
        d_prob[pair] = dot(v_ref[:, at], pulled, NT)
        grad_ref[:, 2 * width + pair * NB : 2 * width + (pair + 1) * NB] = dot(
            prob_ref[0, pair], pulled
        ).astype(BF)
    for pair in range(PAIRS):
        prob = prob_ref[0, pair].astype(F32)
        inner = jnp.sum(prob * d_prob[pair], axis=0, keepdims=True)
        found = prob * (d_prob[pair] - inner)
        slide_acc[pair] += found
        d_logit[pair] = found.astype(BF)
    for pair in range(PAIRS):
        at = slice(pair * NB, (pair + 1) * NB)
        offered = jnp.concatenate([k_ref[:, at], boxes], axis=1)
        back = dot(d_logit[pair], offered, TN)
        grad_ref[:, at] = (join_heads(back) * scale).astype(BF)
        grad_ref[:, width + pair * NB : width + (pair + 1) * NB] = dot(
            d_logit[pair], split_heads(q_ref[:, at])
        ).astype(BF)
        tall = back[:, NB:].astype(BF)
        boxed[:, 2 * pair * NB : 2 * (pair + 1) * NB] = jnp.concatenate(
            [tall[:PAGE], tall[PAGE:]], axis=1
        )
    box_acc[...] += dot(flip_ref[...], boxed[...])
    for part in range(3 * width // 512):
        at = slice(part * 512, (part + 1) * 512)
        bias_sum_ref[:, at] += fold_rows(grad_ref[:, at].astype(F32))

    @pl.when(page == PAGES - 1)
    def _():
        row = lax.broadcasted_iota(jnp.int32, (NB, NB), 0)
        lane = lax.broadcasted_iota(jnp.int32, (NB, NB), 1)
        mirror = (row + lane == NB - 1).astype(BF)
        same = (row < 64) == (lane >= 64)
        for head in range(HEADS):
            half = (head % 2) * PAGE
            block = slide_acc[head // 2, :, half : half + PAGE]
            high = block.astype(BF)
            low = (block - high.astype(F32)).astype(BF)
            block = dot(mirror, high) + dot(mirror, low)
            block = jnp.concatenate([block, jnp.zeros_like(block)], axis=1)
            slid = pltpu.roll(block, 0, 1, stride=1, stride_axis=0)
            slide_sum_ref[head : head + 1, :] = jnp.sum(slid, axis=0, keepdims=True)
            block = jnp.where(same, box_acc[:, head * NB : (head + 1) * NB], 0.0)
            slid = pltpu.roll(block, 0, 1, stride=1, stride_axis=0)
            box_sum_ref[1, head : head + 1, :] = jnp.sum(slid[:64], axis=0, keepdims=True)
            box_sum_ref[0, head : head + 1, :] = jnp.sum(slid[64:], axis=0, keepdims=True)


def attend_back(queries, keys, values, d_context, boxes, flipped, prob):
    width = HEADS * HEAD_DIM
    wide = pl.BlockSpec((PAGE, width), lambda i: (i, 0))
    return pl.pallas_call(
        attend_back_kernel,
        grid=(PAGES,),
        in_specs=[
            wide,
            wide,
            wide,
            wide,
            pl.BlockSpec((PAGE, NB), lambda i: (i, 0)),
            pl.BlockSpec((NB, PAGE), lambda i: (0, i)),
            pl.BlockSpec((1, PAIRS, PAGE, 2 * PAGE), lambda i: (i, 0, 0, 0)),
        ],
        out_specs=(
            pl.BlockSpec((PAGE, 3 * width), lambda i: (i, 0)),
            pl.BlockSpec((HEADS, 2 * PAGE), lambda i: (0, 0)),
            pl.BlockSpec((2, HEADS, NB), lambda i: (0, 0, 0)),
            pl.BlockSpec((8, 3 * width), lambda i: (0, 0)),
        ),
        out_shape=(
            jax.ShapeDtypeStruct((PAGES * PAGE, 3 * width), BF),
            jax.ShapeDtypeStruct((HEADS, 2 * PAGE), F32),
            jax.ShapeDtypeStruct((2, HEADS, NB), F32),
            jax.ShapeDtypeStruct((8, 3 * width), F32),
        ),
        scratch_shapes=[
            pltpu.VMEM((PAIRS, PAGE, 2 * PAGE), F32),
            pltpu.VMEM((NB, HEADS * NB), F32),
            pltpu.VMEM((PAIRS, PAGE, 2 * PAGE), F32),
            pltpu.VMEM((PAIRS, PAGE, 2 * PAGE), BF),
            pltpu.VMEM((PAGE, HEADS * NB), BF),
        ],
        compiler_params=pltpu.CompilerParams(vmem_limit_bytes=VMEM_LIMIT),
        cost_estimate=cost(14),
    )(queries, keys, values, d_context, boxes, flipped, prob)


ROWS_AT_ONCE = 32
Q_BIAS, V_BIAS, O_BIAS, GAIN1, SHIFT1, I_BIAS, U_BIAS, GAIN2, SHIFT2 = range(9)
SPOTS = (0, 1, 2, 3, 4, 5, 9, 10, 11)
TABLE_SPOT = 12


def fetch(blocks, held, sem):
    copies = [
        pltpu.make_async_copy(blocks[k], held.at[k], sem.at[k]) for k in range(len(blocks))
    ]
    for copy in copies:
        copy.start()
    return copies


def norm_parts(values):
    center = jnp.mean(values, axis=-1, keepdims=True)
    centered = values - center
    spread = lax.rsqrt(jnp.mean(centered * centered, axis=-1, keepdims=True) + EPSILON)
    return centered * spread, spread


def norm_back(normed, spread, pulled):
    level = jnp.mean(pulled, axis=-1, keepdims=True)
    slope = jnp.mean(pulled * normed, axis=-1, keepdims=True)
    return spread * (pulled - level - normed * slope)


def fold_rows(values):
    return jnp.sum(values.reshape(-1, 8, values.shape[-1]), axis=0)


def run(length, kernel, shapes, order, ins, blocks, scratch, far=()):
    near_spec = pl.BlockSpec(memory_space=pltpu.VMEM)
    far_spec = pl.BlockSpec(memory_space=pltpu.HBM)
    return pl.pallas_call(
        kernel,
        out_shape=tuple(jax.ShapeDtypeStruct(item[0], item[1]) for item in shapes),
        in_specs=[pl.BlockSpec(memory_space=pltpu.SMEM)]
        + [near_spec] * len(ins)
        + [far_spec] * (len(far) + len(blocks)),
        out_specs=tuple(far_spec if len(item) > 2 else near_spec for item in shapes),
        scratch_shapes=scratch,
        compiler_params=pltpu.CompilerParams(vmem_limit_bytes=VMEM_LIMIT),
        cost_estimate=cost(length),
    )(order, *ins, *far, *blocks)


def begin(source, target, sem):
    copy = pltpu.make_async_copy(source, target, sem)
    copy.start()
    return copy


def finish(copies):
    for copy in copies:
        copy.wait()


def each_rows(group, body, carry):
    for c in group:
        carry = body(pl.ds(c * ROWS_AT_ONCE, ROWS_AT_ONCE), carry)
    return carry


def row_groups(count):
    chunks = count // ROWS_AT_ONCE
    edges = sorted({chunks * i // 4 for i in range(5)})
    return [range(low, high) for low, high in zip(edges, edges[1:])]


def project_kernel(order_ref, x_ref, *refs):
    blocks = refs[:8]
    q_ref, k_ref, v_ref, vector_ref, table_ref, held, sem = refs[8:]
    copies = fetch(blocks, held, sem)
    x = jnp.concatenate([x_ref[:, lanes(order_ref, k, 128)] for k in range(8)], axis=1)
    for copy in copies:
        copy.wait()
    rows = (held.shape[1] - 16) // 3

    def piece(k, spot):
        return held[k, pl.ds(3 * rows, 16), pl.ds(spot % 8 * 128, 128)].astype(F32)[
            spot // 8 : spot // 8 + 1
        ]

    for k in range(8):
        for i, spot in enumerate(SPOTS):
            if i == I_BIAS:
                for part in range(4):
                    at = pl.multiple_of(order_ref[k] * 512 + part * 128, 128)
                    vector_ref[i : i + 1, pl.ds(at, 128)] = piece(k, spot + part)
            else:
                vector_ref[i : i + 1, lanes(order_ref, k, 128)] = piece(k, spot)
        for part in range(6):
            table_ref[order_ref[k] * 6 + part] = piece(k, TABLE_SPOT + part)
    half = q_ref.shape[1] // 2

    @pl.loop(0, 2)
    def _(part):
        at = pl.ds(pl.multiple_of(part * half, half), half)
        for j, out_ref in ((1, k_ref), (0, q_ref), (2, v_ref)):
            weight = jnp.concatenate(
                [held[k, j * rows : (j + 1) * rows, at] for k in range(8)], axis=0
            )
            found = dot(x, weight)
            if j == 0:
                found = (found + vector_ref[Q_BIAS : Q_BIAS + 1, at]) * HEAD_DIM ** (-0.5)
            if j == 2:
                found = found + vector_ref[V_BIAS : V_BIAS + 1, at]
            out_ref[:, at] = found.astype(BF)


def project(order, x, blocks):
    count, width = x.shape
    return run(
        12,
        project_kernel,
        [((count, width), BF)] * 3 + [((16, 4 * width), F32), ((48, 1, 128), F32)],
        order,
        [x],
        blocks,
        [pltpu.VMEM((8,) + blocks[0].shape, BF), pltpu.SemaphoreType.DMA((8,))],
    )


def output_kernel(order_ref, c_ref, spread_ref, hidden_ref, vector_ref, *refs):
    blocks = refs[:8]
    context_ref, normed_ref, deviation_ref, low_ref, held, sem = refs[8:]
    copies = fetch(blocks, held, sem)
    context_ref[...] = dot(spread_ref[...], c_ref[...]).astype(BF)
    x = jnp.concatenate([context_ref[:, lanes(order_ref, k, 128)] for k in range(8)], axis=1)
    for copy in copies:
        copy.wait()
    width = hidden_ref.shape[1]
    normed_ref[...] = dot(x, held[...].reshape(-1, width))
    bias = vector_ref[O_BIAS : O_BIAS + 1, :width]
    gain = vector_ref[GAIN1 : GAIN1 + 1, :width]
    offset = vector_ref[SHIFT1 : SHIFT1 + 1, :width]

    def body(at, carry):
        normed, deviation = norm_parts(
            hidden_ref[at, :].astype(F32) + (normed_ref[at, :] + bias)
        )
        normed_ref[at, :] = normed
        deviation_ref[at, :] = deviation
        low_ref[at, :] = (normed * gain + offset).astype(BF)
        return carry

    each_rows(range(hidden_ref.shape[0] // ROWS_AT_ONCE), body, 0)


def output_block(order, context, spread, hidden, vectors, blocks):
    count, width = hidden.shape
    return run(
        7,
        output_kernel,
        [((count, width), BF), ((count, width), F32), ((count, 1), F32), ((count, width), BF)],
        order,
        [context, spread, hidden, vectors],
        blocks,
        [pltpu.VMEM((8,) + blocks[0].shape, BF), pltpu.SemaphoreType.DMA((8,))],
    )


def inner_kernel(tiles, order_ref, x_ref, vector_ref, *refs):
    blocks = refs[:8]
    active_out, steep_out, held, first, second, active_ref, steep_ref, sem, out_sem = refs[8:]
    rows = blocks[0].shape[0]
    size = active_out.shape[1] // tiles
    for t in range(tiles):
        at = slice(t * size, (t + 1) * size)
        for k in range(8):
            begin(blocks[k].at[:, at], held.at[t, pl.ds(k * rows, rows), :], sem.at[t])
    x = jnp.concatenate([x_ref[:, lanes(order_ref, k, 128)] for k in range(8)], axis=1)

    def place(t):
        return pl.ds(pl.multiple_of(t * size, size), size)

    def multiply(t, target):
        for k in range(8):
            pltpu.make_async_copy(
                blocks[k].at[:, :size], held.at[t, pl.ds(k * rows, rows), :], sem.at[t]
            ).wait()
        target[...] = dot(x, held[t])

    def bend(t, source):
        bias = vector_ref[I_BIAS : I_BIAS + 1, place(t)]
        for c in range(x_ref.shape[0] // ROWS_AT_ONCE):
            row = slice(c * ROWS_AT_ONCE, (c + 1) * ROWS_AT_ONCE)
            inner = source[row] + bias
            share = 0.5 + 0.5 * lax.erf(inner * 0.5**0.5)
            active_ref[row, place(t)] = (inner * share).astype(BF)
            steep_ref[row, place(t)] = (
                share + inner * jnp.exp(-0.5 * inner * inner) * (2 * np.pi) ** -0.5
            ).astype(BF)

    def leave(t):
        at = place(t)
        return (
            pltpu.make_async_copy(active_ref.at[:, at], active_out.at[:, at], out_sem.at[0, t]),
            pltpu.make_async_copy(steep_ref.at[:, at], steep_out.at[:, at], out_sem.at[1, t]),
        )

    second[...] = jnp.zeros_like(second)

    @pl.loop(0, tiles // 2)
    def _(half):
        t = 2 * half
        before = jnp.maximum(t - 1, 0)
        multiply(t, first)
        bend(before, second)
        multiply(t + 1, second)
        bend(t, first)

        @pl.when(half > 0)
        def _():
            for copy in leave(before):
                copy.start()

        for copy in leave(t):
            copy.start()

    bend(tiles - 1, second)
    for copy in leave(tiles - 1):
        copy.start()
    for t in range(tiles):
        finish(leave(t))


def inner_block(order, x, vectors, blocks, tiles=8):
    count, width = x.shape
    wide = blocks[0].shape[1]
    return run(
        14,
        partial(inner_kernel, tiles),
        [((count, wide), BF, 1), ((count, wide), BF, 1)],
        order,
        [x, vectors],
        blocks,
        [
            pltpu.VMEM((tiles, width, wide // tiles), BF),
            pltpu.VMEM((count, wide // tiles), F32),
            pltpu.VMEM((count, wide // tiles), F32),
            pltpu.VMEM((count, wide), BF),
            pltpu.VMEM((count, wide), BF),
            pltpu.SemaphoreType.DMA((tiles,)),
            pltpu.SemaphoreType.DMA((2, tiles)),
        ],
    )


def outer_kernel(order_ref, vector_ref, a_far, normed_far, upstream_far, *refs):
    blocks = refs[:8]
    (
        out_far,
        second_far,
        d_outer_far,
        sum_ref,
        held,
        a_ref,
        normed_ref,
        upstream_ref,
        out_ref,
        second_ref,
        d_outer_ref,
        sem,
        in_sem,
        out_sem,
    ) = refs[8:]
    width = out_ref.shape[1]
    rows = blocks[0].shape[0]
    weights, lefts = [], []
    for k in range(8):
        at = lanes(order_ref, k, rows)
        lefts.append(begin(a_far.at[:, at], a_ref.at[k], in_sem.at[k]))
        weights.append(begin(blocks[k], held.at[k], sem.at[k]))
    late = [
        begin(normed_far, normed_ref, in_sem.at[8]),
        begin(upstream_far, upstream_ref, in_sem.at[9]),
    ]
    finish([lefts[0], weights[0]])
    second_ref[...] = dot(a_ref[0], held[0])

    @pl.loop(1, 8)
    def _(k):
        pltpu.make_async_copy(
            a_far.at[:, lanes(order_ref, k, rows)], a_ref.at[k], in_sem.at[k]
        ).wait()
        pltpu.make_async_copy(blocks[1], held.at[k], sem.at[k]).wait()
        second_ref[...] += dot(a_ref[k], held[k])

    finish(late)
    gain1 = vector_ref[GAIN1 : GAIN1 + 1, :width]
    shift1 = vector_ref[SHIFT1 : SHIFT1 + 1, :width]
    gain2 = vector_ref[GAIN2 : GAIN2 + 1, :width]
    shift2 = vector_ref[SHIFT2 : SHIFT2 + 1, :width]
    bias = vector_ref[U_BIAS : U_BIAS + 1, :width]
    sums = (jnp.zeros((8, width), F32),) * 3
    leaving = []
    for g, group in enumerate(row_groups(out_ref.shape[0])):

        def body(at, sums):
            first_out = normed_ref[at, :] * gain1 + shift1
            normed, deviation = norm_parts(first_out + (second_ref[at, :] + bias))
            out_ref[at, :] = (normed * gain2 + shift2).astype(BF)
            upstream = upstream_ref[at, :].astype(F32)
            d_second = norm_back(normed, deviation, upstream * gain2)
            second_ref[at, :] = d_second
            low = d_second.astype(BF)
            d_outer_ref[at, :] = low
            return (
                sums[0] + fold_rows(upstream * normed),
                sums[1] + fold_rows(upstream),
                sums[2] + fold_rows(low.astype(F32)),
            )

        sums = each_rows(group, body, sums)
        at = pl.ds(group[0] * ROWS_AT_ONCE, len(group) * ROWS_AT_ONCE)
        for i, (source, target) in enumerate(
            ((out_ref, out_far), (second_ref, second_far), (d_outer_ref, d_outer_far))
        ):
            leaving.append(begin(source.at[at], target.at[at], out_sem.at[i, g]))
    for i in range(3):
        sum_ref[i : i + 1, :] = jnp.sum(sums[i], axis=0, keepdims=True)
    finish(leaving)


def outer_block(order, active, normed, upstream, vectors, blocks):
    count, width = normed.shape
    return run(
        11.5,
        outer_kernel,
        [
            ((count, width), BF, 1),
            ((count, width), F32, 1),
            ((count, width), BF, 1),
            ((8, width), F32),
        ],
        order,
        [vectors],
        blocks,
        [
            pltpu.VMEM((8,) + blocks[0].shape, BF),
            pltpu.VMEM((8, count, active.shape[1] // 8), BF),
            pltpu.VMEM((count, width), F32),
            pltpu.VMEM((count, width), BF),
            pltpu.VMEM((count, width), BF),
            pltpu.VMEM((count, width), F32),
            pltpu.VMEM((count, width), BF),
            pltpu.SemaphoreType.DMA((8,)),
            pltpu.SemaphoreType.DMA((10,)),
            pltpu.SemaphoreType.DMA((3, 4)),
        ],
        [active, normed, upstream],
    )


def inner_back_kernel(order_ref, d_ref, steep_far, *refs):
    blocks = refs[:8]
    out_far, sum_ref, held, steep_ref, out_ref, sem, in_sem, out_sem = refs[8:]
    rows = blocks[0].shape[0]
    copies = []
    for k in range(8):
        at = lanes(order_ref, k, rows)
        copies.append(
            [
                begin(blocks[k], held.at[k], sem.at[k]),
                begin(steep_far.at[:, at], steep_ref.at[k], in_sem.at[k]),
            ]
        )

    @pl.loop(0, 8)
    def _(k):
        at = lanes(order_ref, k, rows)
        pltpu.make_async_copy(blocks[0], held.at[k], sem.at[k]).wait()
        pltpu.make_async_copy(steep_far.at[:, at], steep_ref.at[k], in_sem.at[k]).wait()
        low = (dot(d_ref[...], held[k], NT) * steep_ref[k].astype(F32)).astype(BF)
        out_ref[k] = low
        sum_ref[:, at] = fold_rows(low.astype(F32))
        begin(out_ref.at[k], out_far.at[:, at], out_sem.at[k])

    for k in range(8):
        pltpu.make_async_copy(
            out_ref.at[k], out_far.at[:, lanes(order_ref, k, rows)], out_sem.at[k]
        ).wait()


def inner_back(order, d_outer, steep, blocks):
    count, wide = steep.shape
    return run(
        10,
        inner_back_kernel,
        [((count, wide), BF, 1), ((8, wide), F32)],
        order,
        [d_outer],
        blocks,
        [
            pltpu.VMEM((8,) + blocks[0].shape, BF),
            pltpu.VMEM((8, count, wide // 8), BF),
            pltpu.VMEM((8, count, wide // 8), BF),
            pltpu.SemaphoreType.DMA((8,)),
            pltpu.SemaphoreType.DMA((8,)),
            pltpu.SemaphoreType.DMA((8,)),
        ],
        [steep],
    )


def first_back_kernel(
    order_ref, d_ref, deviation_ref, vector_ref, second_far, normed_far, *refs
):
    blocks = refs[:8]
    (
        summed_far,
        low_far,
        sum_ref,
        held,
        second_ref,
        normed_ref,
        summed_ref,
        low_ref,
        sem,
        in_sem,
        out_sem,
    ) = refs[8:]
    copies = fetch(blocks, held, sem)
    late = [
        begin(second_far, second_ref, in_sem.at[0]),
        begin(normed_far, normed_ref, in_sem.at[1]),
    ]
    width = summed_ref.shape[1]
    rows = blocks[0].shape[0]

    @pl.loop(0, 4)
    def _(pair):
        k = 2 * pair
        pltpu.make_async_copy(blocks[0], held.at[k], sem.at[k]).wait()
        pltpu.make_async_copy(blocks[0], held.at[k + 1], sem.at[k + 1]).wait()
        weight = jnp.concatenate([held[k], held[k + 1]], axis=0)
        part = dot(d_ref[...], weight, NT)
        summed_ref[:, lanes(order_ref, k, rows)] = part[:, :rows]
        summed_ref[:, lanes(order_ref, k + 1, rows)] = part[:, rows:]

    finish(late)
    gain = vector_ref[GAIN1 : GAIN1 + 1, :width]
    sums = (jnp.zeros((8, width), F32),) * 3
    leaving = []
    for g, group in enumerate(row_groups(summed_ref.shape[0])):

        def body(at, sums):
            d_first = second_ref[at, :] + summed_ref[at, :]
            normed = normed_ref[at, :]
            d_summed = norm_back(normed, deviation_ref[at, :], d_first * gain)
            summed_ref[at, :] = d_summed
            low = d_summed.astype(BF)
            low_ref[at, :] = low
            return (
                sums[0] + fold_rows(d_first * normed),
                sums[1] + fold_rows(d_first),
                sums[2] + fold_rows(low.astype(F32)),
            )

        sums = each_rows(group, body, sums)
        at = pl.ds(group[0] * ROWS_AT_ONCE, len(group) * ROWS_AT_ONCE)
        leaving.append(begin(summed_ref.at[at], summed_far.at[at], out_sem.at[0, g]))
        leaving.append(begin(low_ref.at[at], low_far.at[at], out_sem.at[1, g]))
    for i in range(3):
        sum_ref[i : i + 1, :] = jnp.sum(sums[i], axis=0, keepdims=True)
    finish(leaving)


def first_back(order, d_inner, d_second, normed, deviation, vectors, blocks):
    count, width = normed.shape
    return run(
        16,
        first_back_kernel,
        [((count, width), F32, 1), ((count, width), BF, 1), ((8, width), F32)],
        order,
        [d_inner, deviation, vectors],
        blocks,
        [
            pltpu.VMEM((8,) + blocks[0].shape, BF),
            pltpu.VMEM((count, width), F32),
            pltpu.VMEM((count, width), F32),
            pltpu.VMEM((count, width), F32),
            pltpu.VMEM((count, width), BF),
            pltpu.SemaphoreType.DMA((8,)),
            pltpu.SemaphoreType.DMA((2,)),
            pltpu.SemaphoreType.DMA((2, 4)),
        ],
        [d_second, normed],
    )


def context_back_kernel(order_ref, d_ref, spread_ref, *refs):
    blocks = refs[:8]
    out_ref, held, kept, sem = refs[8:]
    copies = fetch(blocks, held, sem)
    rows = blocks[0].shape[0]
    for copy in copies:
        copy.wait()

    @pl.loop(0, 4)
    def _(pair):
        k = 2 * pair
        weight = jnp.concatenate([held[k], held[k + 1]], axis=0)
        part = dot(d_ref[...], weight, NT).astype(BF)
        kept[:, lanes(order_ref, k, rows)] = part[:, :rows]
        kept[:, lanes(order_ref, k + 1, rows)] = part[:, rows:]

    out_ref[...] = dot(spread_ref[...], kept[...]).astype(BF)


def context_back(order, d_attn, spread, blocks):
    count, width = d_attn.shape
    return run(
        6.5,
        context_back_kernel,
        [((spread.shape[0], width), BF)],
        order,
        [d_attn, spread],
        blocks,
        [
            pltpu.VMEM((8,) + blocks[0].shape, BF),
            pltpu.VMEM((count, width), BF),
            pltpu.SemaphoreType.DMA((8,)),
        ],
    )[0]


def input_back_kernel(order_ref, d_ref, spread_ref, summed_far, *refs):
    blocks = refs[:8]
    out_far, held, kept, summed_ref, out_ref, sem, in_sem, out_sem = refs[8:]
    copies = fetch(blocks, held, sem)
    late = begin(summed_far, summed_ref, in_sem.at[0])
    rows = (blocks[0].shape[0] - 16) // 3
    width = summed_ref.shape[1]

    @pl.loop(0, 3)
    def _(j):
        at = pl.ds(pl.multiple_of(j * width, width), width)
        kept[:, at] = dot(spread_ref[...], d_ref[:, at]).astype(BF)

    finish(copies)
    late.wait()

    @pl.loop(0, 4)
    def _(pair):
        k = 2 * pair
        weight = jnp.concatenate(
            [
                jnp.concatenate(
                    [held[k, j * rows : (j + 1) * rows], held[k + 1, j * rows : (j + 1) * rows]],
                    axis=0,
                )
                for j in range(3)
            ],
            axis=1,
        )
        part = dot(kept[...], weight, NT)
        for i in range(2):
            at = lanes(order_ref, k + i, rows)
            out_ref[k + i] = summed_ref[:, at] + part[:, i * rows : (i + 1) * rows]
            begin(out_ref.at[k + i], out_far.at[:, at], out_sem.at[k + i])

    for k in range(8):
        at = lanes(order_ref, k, rows)
        pltpu.make_async_copy(out_ref.at[k], out_far.at[:, at], out_sem.at[k]).wait()


def input_back(order, d_mixed, spread, d_summed, blocks):
    count, width = d_summed.shape
    return run(
        12.5,
        input_back_kernel,
        [((count, width), F32, 1)],
        order,
        [d_mixed, spread],
        blocks,
        [
            pltpu.VMEM((8,) + blocks[0].shape, BF),
            pltpu.VMEM((count, 3 * width), BF),
            pltpu.VMEM((count, width), F32),
            pltpu.VMEM((8, count, width // 8), F32),
            pltpu.SemaphoreType.DMA((8,)),
            pltpu.SemaphoreType.DMA((1,)),
            pltpu.SemaphoreType.DMA((8,)),
        ],
        [d_summed],
    )[0]


def small_kernel(
    order_ref,
    slide_ref,
    box_ref,
    bias_ref,
    first_ref,
    inner_ref,
    second_ref,
    *refs,
):
    outs, flat = refs[:8], refs[8]
    spot = one_hot(
        (2 * PAGE, NB),
        lambda c, bucket: (jnp.clip(PAGE - 1 - c, -64, 63) + 64 == bucket) & (c < 2 * PAGE - 1),
    ).astype(F32)
    by_head = [precise(slide_ref[...], spot)]
    by_head += [pltpu.roll(box_ref[i], 65, 1) for i in range(2)]
    heads = one_hot((NB, HEADS), lambda r, c: r % 16 == c).astype(F32)
    mine = one_hot((NB, NB), lambda r, c: r // 16 == c % 8)
    rows = one_hot((16, NB), lambda r, c: c // 8 == r).astype(F32)
    for kind in range(3):
        spread = jnp.where(mine, precise(heads, by_head[kind]), 0.0)
        found = precise(rows, spread, NT)
        for i in range(16):
            flat[16 * kind + i] = found[i : i + 1]
    width = first_ref.shape[1]
    bias = jnp.sum(bias_ref[...], axis=0, keepdims=True)
    inner = jnp.sum(inner_ref[...], axis=0, keepdims=True)
    bias_ref[0:1, :] = bias
    inner_ref[0:1, :] = inner
    for k in range(8):
        out_ref = outs[k]
        at = lanes(order_ref, k, 128)
        out_ref[0:1, :] = bias_ref[0:1, at]
        out_ref[1:2, :] = bias_ref[
            0:1, pl.ds(pl.multiple_of(2 * width + order_ref[k] * 128, 128), 128)
        ]
        out_ref[2:3, :] = first_ref[2:3, at]
        out_ref[3:5, :] = first_ref[0:2, at]
        for part in range(4):
            piece = pl.ds(pl.multiple_of(order_ref[k] * 512 + part * 128, 128), 128)
            out_ref[5 + part : 6 + part, :] = inner_ref[0:1, piece]
        out_ref[9:10, :] = second_ref[2:3, at]
        out_ref[10:12, :] = second_ref[0:2, at]
        for part in range(6):
            out_ref[12 + part : 13 + part, :] = flat[order_ref[k] * 6 + part]
        out_ref[18:, :] = jnp.zeros((6, 128), F32)


def small_blocks(order, sums):
    return pl.pallas_call(
        small_kernel,
        out_shape=(jax.ShapeDtypeStruct((24, 128), F32),) * 8,
        in_specs=[pl.BlockSpec(memory_space=pltpu.SMEM)]
        + [pl.BlockSpec(memory_space=pltpu.VMEM)] * 6,
        out_specs=(pl.BlockSpec(memory_space=pltpu.VMEM),) * 8,
        scratch_shapes=[pltpu.VMEM((48, 1, 128), F32)],
        compiler_params=pltpu.CompilerParams(vmem_limit_bytes=VMEM_LIMIT),
        cost_estimate=cost(3),
    )(order, *sums)


def on_device(line, mesh_size, *args):
    (
        hidden_in,
        cotangent,
        segment_ids,
        box_left,
        box_top,
        query_weight,
        query_bias,
        key_weight,
        value_weight,
        value_bias,
        output_weight,
        output_bias,
        first_gain,
        first_shift,
        inner_weight,
        inner_bias,
        outer_weight,
        outer_bias,
        second_gain,
        second_shift,
        bucket_table,
    ) = args
    slot_count = segment_ids.shape[1]
    width = hidden_in.shape[1]
    vectors = (
        query_bias,
        value_bias,
        output_bias,
        first_gain,
        first_shift,
        inner_bias,
        outer_bias,
        second_gain,
        second_shift,
        bucket_table,
    )
    phase = lax.optimization_barrier
    if line:
        order = block_order(lax.axis_index("fsdp"))
        packed = pack((query_weight, key_weight, value_weight), vectors)
        in_blocks = [packed, hop(packed, NEAR), hop(packed, FAR)]
    else:
        order = jnp.arange(8, dtype=jnp.int32)

        def whole(shard):
            return lax.all_gather(shard, "fsdp", axis=0, tiled=True)

        def blocks_of(shard):
            full = whole(shard)
            return list(full.reshape(8, full.shape[0] // 8, full.shape[1]))

        small = jnp.concatenate([whole(item).reshape(8, -1) for item in vectors], axis=1)
        small = jnp.pad(small, ((0, 0), (0, 16 * width - small.shape[1])))
        in_blocks = jnp.concatenate(
            [whole(item).reshape(8, -1, width) for item in (query_weight, key_weight, value_weight)]
            + [small.reshape(8, 16, width)],
            axis=1,
        )
        in_blocks = list(in_blocks)
        output_blocks = blocks_of(output_weight)
        inner_blocks = blocks_of(inner_weight)
        outer_blocks = blocks_of(outer_weight)

    slot = lax.iota(jnp.int32, slot_count)
    pages = lax.iota(jnp.int32, PAGES)
    segments = segment_ids[0]
    member = segments[None, :] == pages[:, None]
    lengths = jnp.sum(member, axis=1, dtype=jnp.int32)
    starts = jnp.sum(segments[None, :] < pages[:, None], axis=1, dtype=jnp.int32)
    start_of = jnp.sum(jnp.where(member, starts[:, None], 0), axis=0)
    target = segments * PAGE + slot - start_of
    padded = lax.iota(jnp.int32, PAGES * PAGE)
    spread = (padded[:, None] == target[None, :]).astype(BF)
    gather = (padded[None, :] == target[:, None]).astype(BF)
    coords = lax.iota(jnp.int32, NB) % 64
    sides = jnp.where(padded[None, :NB] < 64, box_left[0][:, None], box_top[0][:, None])
    boxes = dot(spread, (sides == coords[None, :]).astype(BF)).astype(BF)
    turned = jnp.where(padded[:NB, None] < 64, box_top[0][None, :], box_left[0][None, :])
    turned = (turned == 63 - coords[:, None]).astype(BF)
    flipped = dot(turned, spread, NT).astype(BF)
    hidden = dot(spread, hidden_in).astype(BF)

    if line:
        in_blocks, hidden, boxes, flipped, gather, spread, inner_weight = phase(
            (in_blocks, hidden, boxes, flipped, gather, spread, inner_weight)
        )
        own, near, far = in_blocks
        both = hop(near, FAR)
        twins = [hop(item, TWIN) for item in (own, near, far)]
        inner_near = hop(inner_weight, NEAR)
        both, twins, inner_near, inner_weight, output_weight = phase(
            (both, twins, inner_near, inner_weight, output_weight)
        )
        in_blocks = [own, near, far, both] + twins + [hop(both, TWIN)]
        inner_far = hop(inner_weight, FAR)
        output_near, output_far = hop(output_weight, NEAR), hop(output_weight, FAR)
    queries, keys, values, vector, table = project(order, hidden, in_blocks)
    lookup, slide = make_tables(table)
    if line:
        (
            queries,
            keys,
            values,
            lookup,
            slide,
            inner_near,
            inner_far,
            output_near,
            output_far,
            outer_weight,
        ) = phase(
            (
                queries,
                keys,
                values,
                lookup,
                slide,
                inner_near,
                inner_far,
                output_near,
                output_far,
                outer_weight,
            )
        )
        outer_near = hop(outer_weight, NEAR)
        output_blocks = [output_weight, output_near, output_far, hop(output_near, FAR)]
    context, prob = attend(lengths, queries, keys, values, boxes, lookup, slide)
    if line:
        context, outer_near, output_blocks, inner_near, inner_far = phase(
            (context, outer_near, output_blocks, inner_near, inner_far)
        )
        inner_blocks = [inner_weight, inner_near, inner_far, hop(inner_near, FAR)]
        outer_far = hop(outer_weight, FAR)
        output_blocks = output_blocks + [hop(item, TWIN) for item in output_blocks]
        inner_twins = [hop(item, TWIN) for item in inner_blocks[:3]]
    context, normed, deviation, first_low = output_block(
        order, context, gather, hidden_in, vector, output_blocks
    )
    if line:
        first_low, inner_blocks, inner_twins, outer_near, outer_far = phase(
            (first_low, inner_blocks, inner_twins, outer_near, outer_far)
        )
        outer_blocks = [outer_weight, outer_near, outer_far, hop(outer_near, FAR)]
        inner_blocks = inner_blocks + inner_twins + [hop(inner_blocks[3], TWIN)]
        outer_twins = [hop(item, TWIN) for item in outer_blocks[:3]]
    active, steep = inner_block(order, first_low, vector, inner_blocks)
    if line:
        active, outer_blocks, outer_twins = phase((active, outer_blocks, outer_twins))
        outer_blocks = outer_blocks + outer_twins + [hop(outer_blocks[3], TWIN)]
    layer_out, d_second, d_outer, second_sums = outer_block(
        order, active, normed, cotangent, vector, outer_blocks
    )

    if line:
        send = turned_blocks(order, 4, active, d_outer)
        d_outer, send = phase((d_outer, send))
        other2 = to_twin(send)
    d_inner, inner_sums = inner_back(order, d_outer, steep, outer_blocks)
    if line:
        d_inner, other2 = phase((d_inner, other2))
        stay2, away2 = turned_blocks(order, 0, active, d_outer, other2)
        d_inner, stay2, away2 = phase((d_inner, stay2, away2))
        other2 = hop(away2, FAR)
        d_inner, stay2 = phase((d_inner, stay2))
    d_summed, d_attn, first_sums = first_back(
        order, d_inner, d_second, normed, deviation, vector, inner_blocks
    )
    if line:
        pairs1 = ((first_low, d_inner), (context, d_attn))
        send = grad_blocks(order, 4, pairs1, 1024)
        d_attn, send, stay2, other2 = phase((d_attn, send, stay2, other2))
        other1 = to_twin(send)
        stay2, away2 = fold_far(stay2, other2)
        other2 = hop(away2, NEAR)
    d_context = context_back(order, d_attn, spread, output_blocks)
    if line:
        d_context, other1, stay2 = phase((d_context, other1, stay2))
        stay1, away1 = grad_blocks(order, 0, pairs1, 1024, other1)
        d_context, stay1, away1, stay2, other2 = phase(
            (d_context, stay1, away1, stay2, other2)
        )
        other1 = hop(away1, FAR)
        kept2, sent2 = cut(stay2 + other2, 1)
        other2 = trade(sent2, 1)
    d_mixed, slide_sum, box_sum, bias_sum = attend_back(
        queries, keys, values, d_context, boxes, flipped, prob
    )
    sums = (slide_sum, box_sum, bias_sum, first_sums, inner_sums, second_sums)
    if line:
        pairs = ((hidden, d_mixed),)
        d_mixed, kept2, other2, stay1, sums = phase((d_mixed, kept2, other2, stay1, sums))
        kept2, sent2 = cut(kept2 + other2, 2)
        other2 = trade(sent2, 2)
        send = grad_blocks(order, 4, pairs, 1024)
        d_mixed, send, kept2, other2, stay1, other1, sums = phase(
            (d_mixed, send, kept2, other2, stay1, other1, sums)
        )
        other = to_twin(send)
        stay1, away1 = fold_far(stay1, other1)
        other1 = hop(away1, NEAR)
        kept2 = kept2 + other2
        other2 = trade(kept2, 2)
    small = small_blocks(order, sums)
    if line:
        d_mixed, other, small, stay1, kept2 = phase((d_mixed, other, small, stay1, kept2))
        stay, away = grad_blocks(order, 0, pairs, 1024, other)
        d_mixed, stay, away, stay1, other1, kept2, other2, small = phase(
            (d_mixed, stay, away, stay1, other1, kept2, other2, small)
        )
        other = hop(away, FAR)
        small_other = to_twin(small[4:])
        kept1, sent1 = cut(stay1 + other1, 1)
        other1 = trade(sent1, 1)
    input_grad = input_back(order, d_mixed, gather, d_summed, in_blocks)
    if line:
        stay, other, input_grad, small, small_other, kept1, other1, kept2, other2 = phase(
            (stay, other, input_grad, small, small_other, kept1, other1, kept2, other2)
        )
        stay, away = fold_far(stay, other)
        other = hop(away, NEAR)
        kept1, sent1 = cut(kept1 + other1, 2)
        other1 = trade(sent1, 2)
        kept2 = paste(kept2, other2, 2)
        other2 = trade(kept2, 1)
        small = [small[i] + small_other[i] for i in range(4)]
        small_other = hop(jnp.stack(small[2:]), FAR)
        stay, other, small, small_other, kept1, other1, kept2, other2 = phase(
            (stay, other, small, small_other, kept1, other1, kept2, other2)
        )
        kept, sent = cut(stay + other, 1)
        other = trade(sent, 1)
        kept1 = kept1 + other1
        other1 = trade(kept1, 2)
        small = small[0] + small_other[0], small[1] + small_other[1]
        small_other = hop(small[1], NEAR)
        kept, other, kept1, other1, small, small_other, kept2, other2 = phase(
            (kept, other, kept1, other1, small, small_other, kept2, other2)
        )
        kept, sent = cut(kept + other, 2)
        other = trade(sent, 2)
        kept1 = paste(kept1, other1, 2)
        other1 = trade(kept1, 1)
        small = small[0] + small_other
        small_other = trade(small, 1)
        outer_own = paste(kept2, other2, 1).T.astype(F32)
        kept, other, kept1, other1, small, small_other, outer_own = phase(
            (kept, other, kept1, other1, small, small_other, outer_own)
        )
        kept = kept + other
        other = trade(kept, 2)
        small = small + small_other
        small_other = trade(small, 2)
        inner_own = paste(kept1, other1, 1).astype(F32)
        kept, other, small, small_other, inner_own = phase(
            (kept, other, small, small_other, inner_own)
        )
        kept = paste(kept, other, 2)
        other = trade(kept, 1)
        small = (small + small_other).reshape(-1)
        kept, other, small = phase((kept, other, small))
        in_own = paste(kept, other, 1)
        inner_own, output_own = inner_own[:, : 4 * width], inner_own[:, 4 * width :]
        cuts = np.cumsum([0] + [item.shape[0] for item in vectors])
        owned = [small[cuts[i] : cuts[i + 1]] for i in range(len(vectors))]
    else:

        def reduce(value):
            value = lax.psum_scatter(value, "fsdp", scatter_dimension=0, tiled=True)
            return lax.psum(value, "dp")

        small = jnp.stack(small)[:, :18].reshape(8, -1)
        edges = np.cumsum([0] + [item.shape[0] * mesh_size // 8 for item in vectors])
        owned = [
            reduce(small[:, edges[i] : edges[i + 1]].reshape(-1)) for i in range(len(vectors))
        ]
        outer_own = reduce(dot(active, d_outer, TN).astype(BF))
        inner_own = reduce(dot(first_low, d_inner, TN).astype(BF))
        output_own = reduce(dot(context, d_attn, TN).astype(BF))
        in_own = reduce(dot(hidden, d_mixed, TN).astype(BF))
    in_own = in_own.astype(F32)
    return (
        layer_out,
        input_grad,
        in_own[:, :width],
        owned[0],
        in_own[:, width : 2 * width],
        in_own[:, 2 * width :],
        owned[1],
        output_own.astype(F32),
        owned[2],
        owned[3],
        owned[4],
        inner_own.astype(F32),
        owned[5],
        outer_own.astype(F32),
        owned[6],
        owned[7],
        owned[8],
        owned[9],
    )


def solution(mesh):
    line = mesh.shape["fsdp"] == 8 and mesh.shape["dp"] == 4
    both, across, flat = P(("fsdp", "dp"), None), P("fsdp", None), P("fsdp")
    return jax.shard_map(
        partial(on_device, line, mesh.shape["fsdp"]),
        mesh=mesh,
        in_specs=(both,) * 5
        + (across, flat, across, across, flat, across, flat, flat, flat)
        + (across, flat, across, flat, flat, flat, flat),
        out_specs=(both, both)
        + (across, flat, across, across, flat, across, flat, flat, flat)
        + (across, flat, across, flat, flat, flat, flat),
        check_vma=False,
    )
```

```python
from functools import partial

import jax
import jax.numpy as jnp
import numpy as np
from jax import lax
from jax.experimental import pallas as pl
from jax.experimental.pallas import tpu as pltpu
from jax.sharding import PartitionSpec as P

HEADS = 16
HEAD_DIM = 64
PAIRS = HEADS // 2
NB = 128
PAGE = 128
PAGES = 8
EPSILON = 1e-05
BLOCKED = -1e30
BF = jnp.bfloat16
F32 = jnp.float32
VMEM_LIMIT = 62 * 1024 * 1024
SCALE = 0.2


def cost(microseconds):
    return pl.CostEstimate(
        flops=1 + int(microseconds * SCALE * 1e9), bytes_accessed=1, transcendentals=0
    )


NT = (((1,), (1,)), ((), ()))
TN = (((0,), (0,)), ((), ()))


def dot(left_side, right_side, dims=(((1,), (0,)), ((), ()))):
    return lax.dot_general(left_side, right_side, dims, preferred_element_type=F32)


def flips(bit_of):
    return [(i, i ^ bit_of(i & 1)) for i in range(8)]


NEAR = flips(lambda c: 2 if c else 4)
FAR = flips(lambda c: 4 if c else 2)
TWIN = flips(lambda c: 1)


def block_order(me):
    rel0 = np.array([0, 4, 2, 6, 1, 3, 5, 7], np.int32)
    rel1 = np.array([0, 2, 4, 6, 1, 5, 3, 7], np.int32)
    rel = jnp.where((me & 1) == 0, rel0, rel1)
    return jnp.bitwise_xor(me, rel).astype(jnp.int32)


def hop(value, pairs):
    return lax.ppermute(value, "fsdp", pairs)


def after(value, *others):
    return lax.optimization_barrier((value,) + others)[0]


def fold_far(stay, other):
    return stay[0] + other[0], stay[1] + other[1]


def trade(value, bit):
    return lax.ppermute(value, "dp", [(i, i ^ bit) for i in range(4)])


def cut(value, bit):
    high = (lax.axis_index("dp") & bit) // bit
    halves = value.reshape((2, value.shape[0] // 2) + value.shape[1:])
    return (
        lax.dynamic_index_in_dim(halves, high, 0, keepdims=False),
        lax.dynamic_index_in_dim(halves, 1 - high, 0, keepdims=False),
    )


def paste(mine, other, bit):
    high = (lax.axis_index("dp") & bit) != 0
    return jnp.concatenate([jnp.where(high, other, mine), jnp.where(high, mine, other)], axis=0)


def pack_kernel(shapes, *refs):
    items, out_ref, sem = refs[: len(shapes) + 3], refs[-2], refs[-1]
    rows = items[0].shape[0]
    copies = [
        pltpu.make_async_copy(items[j], out_ref.at[pl.ds(j * rows, rows), :], sem.at[j])
        for j in range(3)
    ]
    for copy in copies:
        copy.start()
    spot = 0
    out_ref[3 * rows :, :] = jnp.zeros((16, out_ref.shape[1]), BF)
    for item, count in zip(items[3:], shapes):
        for i in range(count):
            row, lane = 3 * rows + spot // 8, spot % 8 * 128
            out_ref[row : row + 1, lane : lane + 128] = item[i : i + 1, :]
            spot += 1
    for copy in copies:
        copy.wait()


def pack(weights, vectors):
    rows, columns = weights[0].shape
    vectors = [item.reshape(-1, 128) for item in vectors]
    return pl.pallas_call(
        partial(pack_kernel, tuple(item.shape[0] for item in vectors)),
        out_shape=jax.ShapeDtypeStruct((3 * rows + 16, columns), BF),
        in_specs=[pl.BlockSpec(memory_space=pltpu.HBM)] * 3
        + [pl.BlockSpec(memory_space=pltpu.VMEM)] * len(vectors),
        out_specs=pl.BlockSpec(memory_space=pltpu.VMEM),
        scratch_shapes=[pltpu.SemaphoreType.DMA((3,))],
        cost_estimate=cost(3),
    )(*weights, *vectors)


def emit(found, k, others, outs):
    if others:
        outs[k // 2][k % 2] = (found + others[k][...].astype(F32)).astype(BF)
    else:
        outs[k][...] = found.astype(BF)


def turned_kernel(first, fold, order_ref, right_ref, left_far, *refs):
    others, outs = refs[: 4 * fold], refs[4 * fold : -7]
    lefts, turned, came, left, in_sem, other_sem, out_sem = refs[-7:]
    rows = lefts.shape[2]
    copies = [
        begin(left_far.at[:, lanes(order_ref, first + k, rows)], lefts.at[k], in_sem.at[k])
        for k in range(4)
    ]
    arrivals = [begin(others[k], came.at[k], other_sem.at[k]) for k in range(4 * fold)]
    turned[...] = right_ref[...].T
    leaving = []
    for k in range(4):
        copies[k].wait()
        found = dot(turned[...], lefts[k])
        if fold:
            arrivals[k].wait()
            found = found + came[k].astype(F32)
        left[k] = found.astype(BF)
        target = outs[k // 2].at[k % 2] if fold else outs[k]
        leaving.append(begin(left.at[k], target, out_sem.at[k]))
    finish(leaving)


def turned_blocks(order, first, left, right, others=()):
    depth, rows, columns = left.shape[0], left.shape[1] // 8, right.shape[1]
    fold = int(bool(others))
    far = pl.BlockSpec(memory_space=pltpu.HBM)
    if fold:
        shapes = (jax.ShapeDtypeStruct((2, columns, rows), BF),) * 2
    else:
        shapes = (jax.ShapeDtypeStruct((columns, rows), BF),) * 4
    return pl.pallas_call(
        partial(turned_kernel, first, fold),
        out_shape=shapes,
        in_specs=[
            pl.BlockSpec(memory_space=pltpu.SMEM),
            pl.BlockSpec(memory_space=pltpu.VMEM),
            far,
        ]
        + [far] * (4 * fold),
        out_specs=(far,) * len(shapes),
        scratch_shapes=[
            pltpu.VMEM((4, depth, rows), BF),
            pltpu.VMEM((columns, depth), BF),
            pltpu.VMEM((4, columns, rows) if fold else (1, 16, 128), BF),
            pltpu.VMEM((4, columns, rows), BF),
            pltpu.SemaphoreType.DMA((4,)),
            pltpu.SemaphoreType.DMA((4,)),
            pltpu.SemaphoreType.DMA((4,)),
        ],
        compiler_params=pltpu.CompilerParams(vmem_limit_bytes=VMEM_LIMIT),
        cost_estimate=cost(7),
    )(order, right, left, *others)


def grad_kernel(first, counts, fold, order_ref, *refs):
    pieces = len(counts)
    lefts, rights = refs[:pieces], refs[pieces : 2 * pieces]
    others = refs[2 * pieces : 2 * pieces + 4 * fold]
    outs, turned = refs[2 * pieces + 4 * fold : -pieces], refs[-pieces:]
    i = pl.program_id(0)
    rows = turned[0].shape[0] // 4
    start = 0
    for left_ref, right_ref, kept, count in zip(lefts, rights, turned, counts):

        @pl.when(i == start)
        def _():
            for k in range(4):
                kept[k * rows : (k + 1) * rows, :] = left_ref[
                    :, lanes(order_ref, first + k, rows)
                ].T

        @pl.when((i >= start) & (i < start + count))
        def _():
            found = dot(kept[...], right_ref[...])
            for k in range(4):
                emit(found[k * rows : (k + 1) * rows], k, others, outs)

        start += count


def grad_blocks(order, first, pairs, tile, others=()):
    rows = pairs[0][0].shape[1] // 8
    counts = [right.shape[1] // tile for _, right in pairs]
    total = sum(counts)
    fold = int(bool(others))
    in_specs = [pl.BlockSpec(left.shape, lambda i, n: (0, 0)) for left, _ in pairs]
    start = 0
    for (_, right), count in zip(pairs, counts):

        def at(i, n, start=start, count=count):
            return 0, jnp.clip(i - start, 0, count - 1)

        in_specs.append(pl.BlockSpec((right.shape[0], tile), at))
        start += count
    one = pl.BlockSpec((rows, tile), lambda i, n: (0, i))
    if fold:
        out_specs = (pl.BlockSpec((2, rows, tile), lambda i, n: (0, 0, i)),) * 2
        shapes = (jax.ShapeDtypeStruct((2, rows, total * tile), BF),) * 2
    else:
        out_specs = (one,) * 4
        shapes = (jax.ShapeDtypeStruct((rows, total * tile), BF),) * 4
    return pl.pallas_call(
        partial(grad_kernel, first, tuple(counts), fold),
        grid_spec=pltpu.PrefetchScalarGridSpec(
            num_scalar_prefetch=1,
            grid=(total,),
            in_specs=in_specs + [one] * (4 * fold),
            out_specs=out_specs,
            scratch_shapes=[pltpu.VMEM((4 * rows, left.shape[0]), BF) for left, _ in pairs],
        ),
        out_shape=shapes,
        compiler_params=pltpu.CompilerParams(vmem_limit_bytes=VMEM_LIMIT),
        cost_estimate=cost(2 * total),
    )(
        order,
        *[left for left, _ in pairs],
        *[right for _, right in pairs],
        *others,
    )


def upright_kernel(turned_ref, out_ref):
    out_ref[...] = turned_ref[...].T.astype(F32)


def upright(turned):
    near = pl.BlockSpec(memory_space=pltpu.VMEM)
    return pl.pallas_call(
        upright_kernel,
        out_shape=jax.ShapeDtypeStruct(turned.shape[::-1], F32),
        in_specs=[near],
        out_specs=near,
        compiler_params=pltpu.CompilerParams(vmem_limit_bytes=VMEM_LIMIT),
        cost_estimate=cost(3),
    )(turned)


def to_twin(blocks):
    return [hop(block, TWIN) for block in blocks]


def lanes(order_ref, k, size):
    return pl.ds(pl.multiple_of(order_ref[k] * size, size), size)


def one_hot(shape, test):
    row = lax.broadcasted_iota(jnp.int32, shape, 0)
    lane = lax.broadcasted_iota(jnp.int32, shape, 1)
    return test(row, lane)


def precise(left_side, right_side, dims=(((1,), (0,)), ((), ()))):
    return lax.dot_general(
        left_side, right_side, dims, precision=lax.Precision.HIGHEST, preferred_element_type=F32
    )


def tables_kernel(table_ref, lookup_ref, slide_ref, flat):
    for i in range(48):
        flat[i : i + 1, :] = table_ref[i]
    wide = one_hot((NB, 16), lambda r, c: r // 8 == c).astype(F32)
    mine = one_hot((NB, NB), lambda r, c: c // 16 == r % 8)
    heads = one_hot((HEADS, NB), lambda r, c: c % 16 == r).astype(F32)
    by_head = []
    for kind in range(3):
        rows = jnp.where(mine, precise(wide, flat[16 * kind : 16 * (kind + 1), :]), 0.0)
        by_head.append(precise(heads, rows, NT))
    spot = one_hot(
        (2 * PAGE, NB),
        lambda m, bucket: jnp.clip(jnp.where(m <= PAGE, -m, 2 * PAGE - m), -64, 63) + 64 == bucket,
    ).astype(F32)
    position = precise(by_head[0], spot, NT)
    left_all = pltpu.roll(by_head[1], 64, 1)
    top_all = pltpu.roll(by_head[2], 64, 1)
    same = one_hot((NB, NB), lambda r, c: (r < 64) == (c < 64))
    for head in range(HEADS):
        base = jnp.broadcast_to(position[head : head + 1, :], (PAGE, 2 * PAGE))
        slid = pltpu.roll(base, 0, 1, stride=1, stride_axis=0)
        half = (head % 2) * PAGE
        slide_ref[head // 2, :, half : half + PAGE] = slid[:, :PAGE]
        left = jnp.broadcast_to(left_all[head : head + 1, :], (64, NB))
        top = jnp.broadcast_to(top_all[head : head + 1, :], (64, NB))
        slid = pltpu.roll(
            jnp.concatenate([left, top], axis=0), 0, 1, stride=1, stride_axis=0
        )
        lookup_ref[:, head * NB : (head + 1) * NB] = jnp.where(same, slid, 0.0).astype(BF)


def make_tables(table):
    return pl.pallas_call(
        tables_kernel,
        out_shape=(
            jax.ShapeDtypeStruct((NB, HEADS * NB), BF),
            jax.ShapeDtypeStruct((PAIRS, PAGE, 2 * PAGE), F32),
        ),
        scratch_shapes=[pltpu.VMEM((48, NB), F32)],
        compiler_params=pltpu.CompilerParams(vmem_limit_bytes=VMEM_LIMIT),
        cost_estimate=cost(3),
    )(table)


def split_heads(tile):
    lane = lax.broadcasted_iota(jnp.int32, tile.shape, 1)
    zero = jnp.zeros_like(tile)
    return jnp.concatenate(
        [jnp.where(lane < HEAD_DIM, tile, zero), jnp.where(lane >= HEAD_DIM, tile, zero)],
        axis=0,
    )


def join_heads(tall):
    lane = lax.broadcasted_iota(jnp.int32, (PAGE, NB), 1)
    return jnp.where(lane < HEAD_DIM, tall[:PAGE, :NB], tall[PAGE:, :NB])


def attend_kernel(
    length_ref, q_ref, k_ref, v_ref, box_ref, lookup_ref, slide_ref, context_ref, prob_ref, logit
):
    length = length_ref[pl.program_id(0)]
    inside = lax.broadcasted_iota(jnp.int32, (PAGE, 2 * PAGE), 0) < length
    boxes = box_ref[...]
    for pair in range(PAIRS):
        at = slice(pair * NB, (pair + 1) * NB)
        looked = dot(boxes, lookup_ref[:, 2 * pair * NB : 2 * (pair + 1) * NB]).astype(BF)
        looked = jnp.concatenate([looked[:, :NB], looked[:, NB:]], axis=0)
        asked = jnp.concatenate([split_heads(q_ref[:, at]), looked], axis=1)
        offered = jnp.concatenate([k_ref[:, at], boxes], axis=1)
        logit[pair] = dot(offered, asked, NT)
    for pair in range(PAIRS):
        logits = jnp.where(inside, logit[pair] + slide_ref[pair], BLOCKED)
        peak = jnp.max(logits, axis=0, keepdims=True)
        grown = jnp.exp(logits - peak)
        total = jnp.sum(grown, axis=0, keepdims=True)
        prob_ref[0, pair] = (grown * (1.0 / total)).astype(BF)
    for pair in range(PAIRS):
        at = slice(pair * NB, (pair + 1) * NB)
        context_ref[:, at] = join_heads(dot(prob_ref[0, pair], v_ref[:, at], TN)).astype(BF)


def attend(lengths, queries, keys, values, boxes, lookup, slide):
    wide = pl.BlockSpec((PAGE, HEADS * HEAD_DIM), lambda i, n: (i, 0))
    return pl.pallas_call(
        attend_kernel,
        grid_spec=pltpu.PrefetchScalarGridSpec(
            num_scalar_prefetch=1,
            grid=(PAGES,),
            in_specs=[
                wide,
                wide,
                wide,
                pl.BlockSpec((PAGE, NB), lambda i, n: (i, 0)),
                pl.BlockSpec((NB, HEADS * NB), lambda i, n: (0, 0)),
                pl.BlockSpec((PAIRS, PAGE, 2 * PAGE), lambda i, n: (0, 0, 0)),
            ],
            out_specs=(
                wide,
                pl.BlockSpec((1, PAIRS, PAGE, 2 * PAGE), lambda i, n: (i, 0, 0, 0)),
            ),
            scratch_shapes=[pltpu.VMEM((PAIRS, PAGE, 2 * PAGE), F32)],
        ),
        out_shape=(
            jax.ShapeDtypeStruct((PAGES * PAGE, HEADS * HEAD_DIM), BF),
            jax.ShapeDtypeStruct((PAGES, PAIRS, PAGE, 2 * PAGE), BF),
        ),
        compiler_params=pltpu.CompilerParams(vmem_limit_bytes=VMEM_LIMIT),
        cost_estimate=cost(13.5),
    )(lengths, queries, keys, values, boxes, lookup, slide)


def attend_back_kernel(
    q_ref,
    k_ref,
    v_ref,
    g_ref,
    box_ref,
    flip_ref,
    prob_ref,
    grad_ref,
    slide_sum_ref,
    box_sum_ref,
    bias_sum_ref,
    slide_acc,
    box_acc,
    d_prob,
    d_logit,
    boxed,
):
    page = pl.program_id(0)

    @pl.when(page == 0)
    def _():
        slide_acc[...] = jnp.zeros_like(slide_acc)
        box_acc[...] = jnp.zeros_like(box_acc)
        bias_sum_ref[...] = jnp.zeros_like(bias_sum_ref)

    boxes = box_ref[...]
    width = HEADS * HEAD_DIM
    scale = HEAD_DIM ** (-0.5)
    for pair in range(PAIRS):
        at = slice(pair * NB, (pair + 1) * NB)
        pulled = split_heads(g_ref[:, at])
        d_prob[pair] = dot(v_ref[:, at], pulled, NT)
        grad_ref[:, 2 * width + pair * NB : 2 * width + (pair + 1) * NB] = dot(
            prob_ref[0, pair], pulled
        ).astype(BF)
    for pair in range(PAIRS):
        prob = prob_ref[0, pair].astype(F32)
        inner = jnp.sum(prob * d_prob[pair], axis=0, keepdims=True)
        found = prob * (d_prob[pair] - inner)
        slide_acc[pair] += found
        d_logit[pair] = found.astype(BF)
    for pair in range(PAIRS):
        at = slice(pair * NB, (pair + 1) * NB)
        offered = jnp.concatenate([k_ref[:, at], boxes], axis=1)
        back = dot(d_logit[pair], offered, TN)
        grad_ref[:, at] = (join_heads(back) * scale).astype(BF)
        grad_ref[:, width + pair * NB : width + (pair + 1) * NB] = dot(
            d_logit[pair], split_heads(q_ref[:, at])
        ).astype(BF)
        tall = back[:, NB:].astype(BF)
        boxed[:, 2 * pair * NB : 2 * (pair + 1) * NB] = jnp.concatenate(
            [tall[:PAGE], tall[PAGE:]], axis=1
        )
    box_acc[...] += dot(flip_ref[...], boxed[...])
    for part in range(3 * width // 512):
        at = slice(part * 512, (part + 1) * 512)
        bias_sum_ref[:, at] += fold_rows(grad_ref[:, at].astype(F32))

    @pl.when(page == PAGES - 1)
    def _():
        row = lax.broadcasted_iota(jnp.int32, (NB, NB), 0)
        lane = lax.broadcasted_iota(jnp.int32, (NB, NB), 1)
        mirror = (row + lane == NB - 1).astype(BF)
        same = (row < 64) == (lane >= 64)
        for head in range(HEADS):
            half = (head % 2) * PAGE
            block = slide_acc[head // 2, :, half : half + PAGE]
            high = block.astype(BF)
            low = (block - high.astype(F32)).astype(BF)
            block = dot(mirror, high) + dot(mirror, low)
            block = jnp.concatenate([block, jnp.zeros_like(block)], axis=1)
            slid = pltpu.roll(block, 0, 1, stride=1, stride_axis=0)
            slide_sum_ref[head : head + 1, :] = jnp.sum(slid, axis=0, keepdims=True)
            block = jnp.where(same, box_acc[:, head * NB : (head + 1) * NB], 0.0)
            slid = pltpu.roll(block, 0, 1, stride=1, stride_axis=0)
            box_sum_ref[1, head : head + 1, :] = jnp.sum(slid[:64], axis=0, keepdims=True)
            box_sum_ref[0, head : head + 1, :] = jnp.sum(slid[64:], axis=0, keepdims=True)


def attend_back(queries, keys, values, d_context, boxes, flipped, prob):
    width = HEADS * HEAD_DIM
    wide = pl.BlockSpec((PAGE, width), lambda i: (i, 0))
    return pl.pallas_call(
        attend_back_kernel,
        grid=(PAGES,),
        in_specs=[
            wide,
            wide,
            wide,
            wide,
            pl.BlockSpec((PAGE, NB), lambda i: (i, 0)),
            pl.BlockSpec((NB, PAGE), lambda i: (0, i)),
            pl.BlockSpec((1, PAIRS, PAGE, 2 * PAGE), lambda i: (i, 0, 0, 0)),
        ],
        out_specs=(
            pl.BlockSpec((PAGE, 3 * width), lambda i: (i, 0)),
            pl.BlockSpec((HEADS, 2 * PAGE), lambda i: (0, 0)),
            pl.BlockSpec((2, HEADS, NB), lambda i: (0, 0, 0)),
            pl.BlockSpec((8, 3 * width), lambda i: (0, 0)),
        ),
        out_shape=(
            jax.ShapeDtypeStruct((PAGES * PAGE, 3 * width), BF),
            jax.ShapeDtypeStruct((HEADS, 2 * PAGE), F32),
            jax.ShapeDtypeStruct((2, HEADS, NB), F32),
            jax.ShapeDtypeStruct((8, 3 * width), F32),
        ),
        scratch_shapes=[
            pltpu.VMEM((PAIRS, PAGE, 2 * PAGE), F32),
            pltpu.VMEM((NB, HEADS * NB), F32),
            pltpu.VMEM((PAIRS, PAGE, 2 * PAGE), F32),
            pltpu.VMEM((PAIRS, PAGE, 2 * PAGE), BF),
            pltpu.VMEM((PAGE, HEADS * NB), BF),
        ],
        compiler_params=pltpu.CompilerParams(vmem_limit_bytes=VMEM_LIMIT),
        cost_estimate=cost(14),
    )(queries, keys, values, d_context, boxes, flipped, prob)


ROWS_AT_ONCE = 32
Q_BIAS, V_BIAS, O_BIAS, GAIN1, SHIFT1, I_BIAS, U_BIAS, GAIN2, SHIFT2 = range(9)
SPOTS = (0, 1, 2, 3, 4, 5, 9, 10, 11)
TABLE_SPOT = 12


def fetch(blocks, held, sem):
    copies = [
        pltpu.make_async_copy(blocks[k], held.at[k], sem.at[k]) for k in range(len(blocks))
    ]
    for copy in copies:
        copy.start()
    return copies


def norm_parts(values):
    center = jnp.mean(values, axis=-1, keepdims=True)
    centered = values - center
    spread = lax.rsqrt(jnp.mean(centered * centered, axis=-1, keepdims=True) + EPSILON)
    return centered * spread, spread


def norm_back(normed, spread, pulled):
    level = jnp.mean(pulled, axis=-1, keepdims=True)
    slope = jnp.mean(pulled * normed, axis=-1, keepdims=True)
    return spread * (pulled - level - normed * slope)


def fold_rows(values):
    return jnp.sum(values.reshape(-1, 8, values.shape[-1]), axis=0)


def run(length, kernel, shapes, order, ins, blocks, scratch, far=()):
    near_spec = pl.BlockSpec(memory_space=pltpu.VMEM)
    far_spec = pl.BlockSpec(memory_space=pltpu.HBM)
    return pl.pallas_call(
        kernel,
        out_shape=tuple(jax.ShapeDtypeStruct(item[0], item[1]) for item in shapes),
        in_specs=[pl.BlockSpec(memory_space=pltpu.SMEM)]
        + [near_spec] * len(ins)
        + [far_spec] * (len(far) + len(blocks)),
        out_specs=tuple(far_spec if len(item) > 2 else near_spec for item in shapes),
        scratch_shapes=scratch,
        compiler_params=pltpu.CompilerParams(vmem_limit_bytes=VMEM_LIMIT),
        cost_estimate=cost(length),
    )(order, *ins, *far, *blocks)


def begin(source, target, sem):
    copy = pltpu.make_async_copy(source, target, sem)
    copy.start()
    return copy


def finish(copies):
    for copy in copies:
        copy.wait()


def each_rows(group, body, carry):
    for c in group:
        carry = body(pl.ds(c * ROWS_AT_ONCE, ROWS_AT_ONCE), carry)
    return carry


def row_groups(count):
    chunks = count // ROWS_AT_ONCE
    edges = sorted({chunks * i // 4 for i in range(5)})
    return [range(low, high) for low, high in zip(edges, edges[1:])]


def project_kernel(order_ref, x_ref, *refs):
    blocks = refs[:8]
    q_ref, k_ref, v_ref, vector_ref, table_ref, held, sem = refs[8:]
    copies = fetch(blocks, held, sem)
    x = jnp.concatenate([x_ref[:, lanes(order_ref, k, 128)] for k in range(8)], axis=1)
    for copy in copies:
        copy.wait()
    rows = (held.shape[1] - 16) // 3

    def piece(k, spot):
        return held[k, pl.ds(3 * rows, 16), pl.ds(spot % 8 * 128, 128)].astype(F32)[
            spot // 8 : spot // 8 + 1
        ]

    for k in range(8):
        for i, spot in enumerate(SPOTS):
            if i == I_BIAS:
                for part in range(4):
                    at = pl.multiple_of(order_ref[k] * 512 + part * 128, 128)
                    vector_ref[i : i + 1, pl.ds(at, 128)] = piece(k, spot + part)
            else:
                vector_ref[i : i + 1, lanes(order_ref, k, 128)] = piece(k, spot)
        for part in range(6):
            table_ref[order_ref[k] * 6 + part] = piece(k, TABLE_SPOT + part)
    half = q_ref.shape[1] // 2

    @pl.loop(0, 2)
    def _(part):
        at = pl.ds(pl.multiple_of(part * half, half), half)
        for j, out_ref in ((1, k_ref), (0, q_ref), (2, v_ref)):
            weight = jnp.concatenate(
                [held[k, j * rows : (j + 1) * rows, at] for k in range(8)], axis=0
            )
            found = dot(x, weight)
            if j == 0:
                found = (found + vector_ref[Q_BIAS : Q_BIAS + 1, at]) * HEAD_DIM ** (-0.5)
            if j == 2:
                found = found + vector_ref[V_BIAS : V_BIAS + 1, at]
            out_ref[:, at] = found.astype(BF)


def project(order, x, blocks):
    count, width = x.shape
    return run(
        12,
        project_kernel,
        [((count, width), BF)] * 3 + [((16, 4 * width), F32), ((48, 1, 128), F32)],
        order,
        [x],
        blocks,
        [pltpu.VMEM((8,) + blocks[0].shape, BF), pltpu.SemaphoreType.DMA((8,))],
    )


def output_kernel(order_ref, c_ref, spread_ref, hidden_ref, vector_ref, *refs):
    blocks = refs[:8]
    context_ref, normed_ref, deviation_ref, low_ref, held, sem = refs[8:]
    copies = fetch(blocks, held, sem)
    context_ref[...] = dot(spread_ref[...], c_ref[...]).astype(BF)
    x = jnp.concatenate([context_ref[:, lanes(order_ref, k, 128)] for k in range(8)], axis=1)
    for copy in copies:
        copy.wait()
    width = hidden_ref.shape[1]
    normed_ref[...] = dot(x, held[...].reshape(-1, width))
    bias = vector_ref[O_BIAS : O_BIAS + 1, :width]
    gain = vector_ref[GAIN1 : GAIN1 + 1, :width]
    offset = vector_ref[SHIFT1 : SHIFT1 + 1, :width]

    def body(at, carry):
        normed, deviation = norm_parts(
            hidden_ref[at, :].astype(F32) + (normed_ref[at, :] + bias)
        )
        normed_ref[at, :] = normed
        deviation_ref[at, :] = deviation
        low_ref[at, :] = (normed * gain + offset).astype(BF)
        return carry

    each_rows(range(hidden_ref.shape[0] // ROWS_AT_ONCE), body, 0)


def output_block(order, context, spread, hidden, vectors, blocks):
    count, width = hidden.shape
    return run(
        7,
        output_kernel,
        [((count, width), BF), ((count, width), F32), ((count, 1), F32), ((count, width), BF)],
        order,
        [context, spread, hidden, vectors],
        blocks,
        [pltpu.VMEM((8,) + blocks[0].shape, BF), pltpu.SemaphoreType.DMA((8,))],
    )


def inner_kernel(tiles, order_ref, x_ref, vector_ref, *refs):
    blocks = refs[:8]
    active_out, steep_out, held, first, second, active_ref, steep_ref, sem, out_sem = refs[8:]
    rows = blocks[0].shape[0]
    size = active_out.shape[1] // tiles
    for t in range(tiles):
        at = slice(t * size, (t + 1) * size)
        for k in range(8):
            begin(blocks[k].at[:, at], held.at[t, pl.ds(k * rows, rows), :], sem.at[t])
    x = jnp.concatenate([x_ref[:, lanes(order_ref, k, 128)] for k in range(8)], axis=1)

    def place(t):
        return pl.ds(pl.multiple_of(t * size, size), size)

    def multiply(t, target):
        for k in range(8):
            pltpu.make_async_copy(
                blocks[k].at[:, :size], held.at[t, pl.ds(k * rows, rows), :], sem.at[t]
            ).wait()
        target[...] = dot(x, held[t])

    def bend(t, source):
        bias = vector_ref[I_BIAS : I_BIAS + 1, place(t)]
        for c in range(x_ref.shape[0] // ROWS_AT_ONCE):
            row = slice(c * ROWS_AT_ONCE, (c + 1) * ROWS_AT_ONCE)
            inner = source[row] + bias
            share = 0.5 + 0.5 * lax.erf(inner * 0.5**0.5)
            active_ref[row, place(t)] = (inner * share).astype(BF)
            steep_ref[row, place(t)] = (
                share + inner * jnp.exp(-0.5 * inner * inner) * (2 * np.pi) ** -0.5
            ).astype(BF)

    def leave(t):
        at = place(t)
        return (
            pltpu.make_async_copy(active_ref.at[:, at], active_out.at[:, at], out_sem.at[0, t]),
            pltpu.make_async_copy(steep_ref.at[:, at], steep_out.at[:, at], out_sem.at[1, t]),
        )

    second[...] = jnp.zeros_like(second)

    @pl.loop(0, tiles // 2)
    def _(half):
        t = 2 * half
        before = jnp.maximum(t - 1, 0)
        multiply(t, first)
        bend(before, second)
        multiply(t + 1, second)
        bend(t, first)

        @pl.when(half > 0)
        def _():
            for copy in leave(before):
                copy.start()

        for copy in leave(t):
            copy.start()

    bend(tiles - 1, second)
    for copy in leave(tiles - 1):
        copy.start()
    for t in range(tiles):
        finish(leave(t))


def inner_block(order, x, vectors, blocks, tiles=8):
    count, width = x.shape
    wide = blocks[0].shape[1]
    return run(
        14,
        partial(inner_kernel, tiles),
        [((count, wide), BF, 1), ((count, wide), BF, 1)],
        order,
        [x, vectors],
        blocks,
        [
            pltpu.VMEM((tiles, width, wide // tiles), BF),
            pltpu.VMEM((count, wide // tiles), F32),
            pltpu.VMEM((count, wide // tiles), F32),
            pltpu.VMEM((count, wide), BF),
            pltpu.VMEM((count, wide), BF),
            pltpu.SemaphoreType.DMA((tiles,)),
            pltpu.SemaphoreType.DMA((2, tiles)),
        ],
    )


def outer_kernel(order_ref, vector_ref, a_far, normed_far, upstream_far, *refs):
    blocks = refs[:8]
    (
        out_far,
        second_far,
        d_outer_far,
        sum_ref,
        held,
        a_ref,
        normed_ref,
        upstream_ref,
        out_ref,
        second_ref,
        d_outer_ref,
        sem,
        in_sem,
        out_sem,
    ) = refs[8:]
    width = out_ref.shape[1]
    rows = blocks[0].shape[0]
    weights, lefts = [], []
    for k in range(8):
        at = lanes(order_ref, k, rows)
        lefts.append(begin(a_far.at[:, at], a_ref.at[k], in_sem.at[k]))
        weights.append(begin(blocks[k], held.at[k], sem.at[k]))
    late = [
        begin(normed_far, normed_ref, in_sem.at[8]),
        begin(upstream_far, upstream_ref, in_sem.at[9]),
    ]
    finish([lefts[0], weights[0]])
    second_ref[...] = dot(a_ref[0], held[0])

    @pl.loop(1, 8)
    def _(k):
        pltpu.make_async_copy(
            a_far.at[:, lanes(order_ref, k, rows)], a_ref.at[k], in_sem.at[k]
        ).wait()
        pltpu.make_async_copy(blocks[1], held.at[k], sem.at[k]).wait()
        second_ref[...] += dot(a_ref[k], held[k])

    finish(late)
    gain1 = vector_ref[GAIN1 : GAIN1 + 1, :width]
    shift1 = vector_ref[SHIFT1 : SHIFT1 + 1, :width]
    gain2 = vector_ref[GAIN2 : GAIN2 + 1, :width]
    shift2 = vector_ref[SHIFT2 : SHIFT2 + 1, :width]
    bias = vector_ref[U_BIAS : U_BIAS + 1, :width]
    sums = (jnp.zeros((8, width), F32),) * 3
    leaving = []
    for g, group in enumerate(row_groups(out_ref.shape[0])):

        def body(at, sums):
            first_out = normed_ref[at, :] * gain1 + shift1
            normed, deviation = norm_parts(first_out + (second_ref[at, :] + bias))
            out_ref[at, :] = (normed * gain2 + shift2).astype(BF)
            upstream = upstream_ref[at, :].astype(F32)
            d_second = norm_back(normed, deviation, upstream * gain2)
            second_ref[at, :] = d_second
            low = d_second.astype(BF)
            d_outer_ref[at, :] = low
            return (
                sums[0] + fold_rows(upstream * normed),
                sums[1] + fold_rows(upstream),
                sums[2] + fold_rows(low.astype(F32)),
            )

        sums = each_rows(group, body, sums)
        at = pl.ds(group[0] * ROWS_AT_ONCE, len(group) * ROWS_AT_ONCE)
        for i, (source, target) in enumerate(
            ((out_ref, out_far), (second_ref, second_far), (d_outer_ref, d_outer_far))
        ):
            leaving.append(begin(source.at[at], target.at[at], out_sem.at[i, g]))
    for i in range(3):
        sum_ref[i : i + 1, :] = jnp.sum(sums[i], axis=0, keepdims=True)
    finish(leaving)


def outer_block(order, active, normed, upstream, vectors, blocks):
    count, width = normed.shape
    return run(
        11.5,
        outer_kernel,
        [
            ((count, width), BF, 1),
            ((count, width), F32, 1),
            ((count, width), BF, 1),
            ((8, width), F32),
        ],
        order,
        [vectors],
        blocks,
        [
            pltpu.VMEM((8,) + blocks[0].shape, BF),
            pltpu.VMEM((8, count, active.shape[1] // 8), BF),
            pltpu.VMEM((count, width), F32),
            pltpu.VMEM((count, width), BF),
            pltpu.VMEM((count, width), BF),
            pltpu.VMEM((count, width), F32),
            pltpu.VMEM((count, width), BF),
            pltpu.SemaphoreType.DMA((8,)),
            pltpu.SemaphoreType.DMA((10,)),
            pltpu.SemaphoreType.DMA((3, 4)),
        ],
        [active, normed, upstream],
    )


def inner_back_kernel(order_ref, d_ref, steep_far, *refs):
    blocks = refs[:8]
    out_far, sum_ref, held, steep_ref, out_ref, sem, in_sem, out_sem = refs[8:]
    rows = blocks[0].shape[0]
    copies = []
    for k in range(8):
        at = lanes(order_ref, k, rows)
        copies.append(
            [
                begin(blocks[k], held.at[k], sem.at[k]),
                begin(steep_far.at[:, at], steep_ref.at[k], in_sem.at[k]),
            ]
        )

    @pl.loop(0, 8)
    def _(k):
        at = lanes(order_ref, k, rows)
        pltpu.make_async_copy(blocks[0], held.at[k], sem.at[k]).wait()
        pltpu.make_async_copy(steep_far.at[:, at], steep_ref.at[k], in_sem.at[k]).wait()
        low = (dot(d_ref[...], held[k], NT) * steep_ref[k].astype(F32)).astype(BF)
        out_ref[k] = low
        sum_ref[:, at] = fold_rows(low.astype(F32))
        begin(out_ref.at[k], out_far.at[:, at], out_sem.at[k])

    for k in range(8):
        pltpu.make_async_copy(
            out_ref.at[k], out_far.at[:, lanes(order_ref, k, rows)], out_sem.at[k]
        ).wait()


def inner_back(order, d_outer, steep, blocks):
    count, wide = steep.shape
    return run(
        10,
        inner_back_kernel,
        [((count, wide), BF, 1), ((8, wide), F32)],
        order,
        [d_outer],
        blocks,
        [
            pltpu.VMEM((8,) + blocks[0].shape, BF),
            pltpu.VMEM((8, count, wide // 8), BF),
            pltpu.VMEM((8, count, wide // 8), BF),
            pltpu.SemaphoreType.DMA((8,)),
            pltpu.SemaphoreType.DMA((8,)),
            pltpu.SemaphoreType.DMA((8,)),
        ],
        [steep],
    )


def first_back_kernel(
    order_ref, d_ref, deviation_ref, vector_ref, second_far, normed_far, *refs
):
    blocks = refs[:8]
    (
        summed_far,
        low_far,
        sum_ref,
        held,
        second_ref,
        normed_ref,
        summed_ref,
        low_ref,
        sem,
        in_sem,
        out_sem,
    ) = refs[8:]
    copies = fetch(blocks, held, sem)
    late = [
        begin(second_far, second_ref, in_sem.at[0]),
        begin(normed_far, normed_ref, in_sem.at[1]),
    ]
    width = summed_ref.shape[1]
    rows = blocks[0].shape[0]

    @pl.loop(0, 4)
    def _(pair):
        k = 2 * pair
        pltpu.make_async_copy(blocks[0], held.at[k], sem.at[k]).wait()
        pltpu.make_async_copy(blocks[0], held.at[k + 1], sem.at[k + 1]).wait()
        weight = jnp.concatenate([held[k], held[k + 1]], axis=0)
        part = dot(d_ref[...], weight, NT)
        summed_ref[:, lanes(order_ref, k, rows)] = part[:, :rows]
        summed_ref[:, lanes(order_ref, k + 1, rows)] = part[:, rows:]

    finish(late)
    gain = vector_ref[GAIN1 : GAIN1 + 1, :width]
    sums = (jnp.zeros((8, width), F32),) * 3
    leaving = []
    for g, group in enumerate(row_groups(summed_ref.shape[0])):

        def body(at, sums):
            d_first = second_ref[at, :] + summed_ref[at, :]
            normed = normed_ref[at, :]
            d_summed = norm_back(normed, deviation_ref[at, :], d_first * gain)
            summed_ref[at, :] = d_summed
            low = d_summed.astype(BF)
            low_ref[at, :] = low
            return (
                sums[0] + fold_rows(d_first * normed),
                sums[1] + fold_rows(d_first),
                sums[2] + fold_rows(low.astype(F32)),
            )

        sums = each_rows(group, body, sums)
        at = pl.ds(group[0] * ROWS_AT_ONCE, len(group) * ROWS_AT_ONCE)
        leaving.append(begin(summed_ref.at[at], summed_far.at[at], out_sem.at[0, g]))
        leaving.append(begin(low_ref.at[at], low_far.at[at], out_sem.at[1, g]))
    for i in range(3):
        sum_ref[i : i + 1, :] = jnp.sum(sums[i], axis=0, keepdims=True)
    finish(leaving)


def first_back(order, d_inner, d_second, normed, deviation, vectors, blocks):
    count, width = normed.shape
    return run(
        16,
        first_back_kernel,
        [((count, width), F32, 1), ((count, width), BF, 1), ((8, width), F32)],
        order,
        [d_inner, deviation, vectors],
        blocks,
        [
            pltpu.VMEM((8,) + blocks[0].shape, BF),
            pltpu.VMEM((count, width), F32),
            pltpu.VMEM((count, width), F32),
            pltpu.VMEM((count, width), F32),
            pltpu.VMEM((count, width), BF),
            pltpu.SemaphoreType.DMA((8,)),
            pltpu.SemaphoreType.DMA((2,)),
            pltpu.SemaphoreType.DMA((2, 4)),
        ],
        [d_second, normed],
    )


def context_back_kernel(order_ref, d_ref, spread_ref, *refs):
    blocks = refs[:8]
    out_ref, held, kept, sem = refs[8:]
    copies = fetch(blocks, held, sem)
    rows = blocks[0].shape[0]
    for copy in copies:
        copy.wait()

    @pl.loop(0, 4)
    def _(pair):
        k = 2 * pair
        weight = jnp.concatenate([held[k], held[k + 1]], axis=0)
        part = dot(d_ref[...], weight, NT).astype(BF)
        kept[:, lanes(order_ref, k, rows)] = part[:, :rows]
        kept[:, lanes(order_ref, k + 1, rows)] = part[:, rows:]

    out_ref[...] = dot(spread_ref[...], kept[...]).astype(BF)


def context_back(order, d_attn, spread, blocks):
    count, width = d_attn.shape
    return run(
        6.5,
        context_back_kernel,
        [((spread.shape[0], width), BF)],
        order,
        [d_attn, spread],
        blocks,
        [
            pltpu.VMEM((8,) + blocks[0].shape, BF),
            pltpu.VMEM((count, width), BF),
            pltpu.SemaphoreType.DMA((8,)),
        ],
    )[0]


def input_back_kernel(order_ref, d_ref, spread_ref, summed_far, *refs):
    blocks = refs[:8]
    out_far, held, kept, summed_ref, out_ref, sem, in_sem, out_sem = refs[8:]
    copies = fetch(blocks, held, sem)
    late = begin(summed_far, summed_ref, in_sem.at[0])
    rows = (blocks[0].shape[0] - 16) // 3
    width = summed_ref.shape[1]

    @pl.loop(0, 3)
    def _(j):
        at = pl.ds(pl.multiple_of(j * width, width), width)
        kept[:, at] = dot(spread_ref[...], d_ref[:, at]).astype(BF)

    finish(copies)
    late.wait()

    @pl.loop(0, 4)
    def _(pair):
        k = 2 * pair
        weight = jnp.concatenate(
            [
                jnp.concatenate(
                    [held[k, j * rows : (j + 1) * rows], held[k + 1, j * rows : (j + 1) * rows]],
                    axis=0,
                )
                for j in range(3)
            ],
            axis=1,
        )
        part = dot(kept[...], weight, NT)
        for i in range(2):
            at = lanes(order_ref, k + i, rows)
            out_ref[k + i] = summed_ref[:, at] + part[:, i * rows : (i + 1) * rows]
            begin(out_ref.at[k + i], out_far.at[:, at], out_sem.at[k + i])

    for k in range(8):
        at = lanes(order_ref, k, rows)
        pltpu.make_async_copy(out_ref.at[k], out_far.at[:, at], out_sem.at[k]).wait()


def input_back(order, d_mixed, spread, d_summed, blocks):
    count, width = d_summed.shape
    return run(
        12.5,
        input_back_kernel,
        [((count, width), F32, 1)],
        order,
        [d_mixed, spread],
        blocks,
        [
            pltpu.VMEM((8,) + blocks[0].shape, BF),
            pltpu.VMEM((count, 3 * width), BF),
            pltpu.VMEM((count, width), F32),
            pltpu.VMEM((8, count, width // 8), F32),
            pltpu.SemaphoreType.DMA((8,)),
            pltpu.SemaphoreType.DMA((1,)),
            pltpu.SemaphoreType.DMA((8,)),
        ],
        [d_summed],
    )[0]


def small_kernel(
    order_ref,
    slide_ref,
    box_ref,
    bias_ref,
    first_ref,
    inner_ref,
    second_ref,
    *refs,
):
    outs, flat = refs[:8], refs[8]
    spot = one_hot(
        (2 * PAGE, NB),
        lambda c, bucket: (jnp.clip(PAGE - 1 - c, -64, 63) + 64 == bucket) & (c < 2 * PAGE - 1),
    ).astype(F32)
    by_head = [precise(slide_ref[...], spot)]
    by_head += [pltpu.roll(box_ref[i], 65, 1) for i in range(2)]
    heads = one_hot((NB, HEADS), lambda r, c: r % 16 == c).astype(F32)
    mine = one_hot((NB, NB), lambda r, c: r // 16 == c % 8)
    rows = one_hot((16, NB), lambda r, c: c // 8 == r).astype(F32)
    for kind in range(3):
        spread = jnp.where(mine, precise(heads, by_head[kind]), 0.0)
        found = precise(rows, spread, NT)
        for i in range(16):
            flat[16 * kind + i] = found[i : i + 1]
    width = first_ref.shape[1]
    bias = jnp.sum(bias_ref[...], axis=0, keepdims=True)
    inner = jnp.sum(inner_ref[...], axis=0, keepdims=True)
    bias_ref[0:1, :] = bias
    inner_ref[0:1, :] = inner
    for k in range(8):
        out_ref = outs[k]
        at = lanes(order_ref, k, 128)
        out_ref[0:1, :] = bias_ref[0:1, at]
        out_ref[1:2, :] = bias_ref[
            0:1, pl.ds(pl.multiple_of(2 * width + order_ref[k] * 128, 128), 128)
        ]
        out_ref[2:3, :] = first_ref[2:3, at]
        out_ref[3:5, :] = first_ref[0:2, at]
        for part in range(4):
            piece = pl.ds(pl.multiple_of(order_ref[k] * 512 + part * 128, 128), 128)
            out_ref[5 + part : 6 + part, :] = inner_ref[0:1, piece]
        out_ref[9:10, :] = second_ref[2:3, at]
        out_ref[10:12, :] = second_ref[0:2, at]
        for part in range(6):
            out_ref[12 + part : 13 + part, :] = flat[order_ref[k] * 6 + part]
        out_ref[18:, :] = jnp.zeros((6, 128), F32)


def small_blocks(order, sums):
    return pl.pallas_call(
        small_kernel,
        out_shape=(jax.ShapeDtypeStruct((24, 128), F32),) * 8,
        in_specs=[pl.BlockSpec(memory_space=pltpu.SMEM)]
        + [pl.BlockSpec(memory_space=pltpu.VMEM)] * 6,
        out_specs=(pl.BlockSpec(memory_space=pltpu.VMEM),) * 8,
        scratch_shapes=[pltpu.VMEM((48, 1, 128), F32)],
        compiler_params=pltpu.CompilerParams(vmem_limit_bytes=VMEM_LIMIT),
        cost_estimate=cost(3),
    )(order, *sums)


def on_device(line, mesh_size, *args):
    (
        hidden_in,
        cotangent,
        segment_ids,
        box_left,
        box_top,
        query_weight,
        query_bias,
        key_weight,
        value_weight,
        value_bias,
        output_weight,
        output_bias,
        first_gain,
        first_shift,
        inner_weight,
        inner_bias,
        outer_weight,
        outer_bias,
        second_gain,
        second_shift,
        bucket_table,
    ) = args
    slot_count = segment_ids.shape[1]
    width = hidden_in.shape[1]
    vectors = (
        query_bias,
        value_bias,
        output_bias,
        first_gain,
        first_shift,
        inner_bias,
        outer_bias,
        second_gain,
        second_shift,
        bucket_table,
    )
    phase = lax.optimization_barrier
    if line:
        order = block_order(lax.axis_index("fsdp"))
        packed = pack((query_weight, key_weight, value_weight), vectors)
        in_blocks = [packed, hop(packed, NEAR), hop(packed, FAR)]
    else:
        order = jnp.arange(8, dtype=jnp.int32)

        def whole(shard):
            return lax.all_gather(shard, "fsdp", axis=0, tiled=True)

        def blocks_of(shard):
            full = whole(shard)
            return list(full.reshape(8, full.shape[0] // 8, full.shape[1]))

        small = jnp.concatenate([whole(item).reshape(8, -1) for item in vectors], axis=1)
        small = jnp.pad(small, ((0, 0), (0, 16 * width - small.shape[1])))
        in_blocks = jnp.concatenate(
            [whole(item).reshape(8, -1, width) for item in (query_weight, key_weight, value_weight)]
            + [small.reshape(8, 16, width)],
            axis=1,
        )
        in_blocks = list(in_blocks)
        output_blocks = blocks_of(output_weight)
        inner_blocks = blocks_of(inner_weight)
        outer_blocks = blocks_of(outer_weight)

    slot = lax.iota(jnp.int32, slot_count)
    pages = lax.iota(jnp.int32, PAGES)
    segments = segment_ids[0]
    member = segments[None, :] == pages[:, None]
    lengths = jnp.sum(member, axis=1, dtype=jnp.int32)
    starts = jnp.sum(segments[None, :] < pages[:, None], axis=1, dtype=jnp.int32)
    start_of = jnp.sum(jnp.where(member, starts[:, None], 0), axis=0)
    target = segments * PAGE + slot - start_of
    padded = lax.iota(jnp.int32, PAGES * PAGE)
    spread = (padded[:, None] == target[None, :]).astype(BF)
    gather = (padded[None, :] == target[:, None]).astype(BF)
    coords = lax.iota(jnp.int32, NB) % 64
    sides = jnp.where(padded[None, :NB] < 64, box_left[0][:, None], box_top[0][:, None])
    boxes = dot(spread, (sides == coords[None, :]).astype(BF)).astype(BF)
    turned = jnp.where(padded[:NB, None] < 64, box_top[0][None, :], box_left[0][None, :])
    turned = (turned == 63 - coords[:, None]).astype(BF)
    flipped = dot(turned, spread, NT).astype(BF)
    hidden = dot(spread, hidden_in).astype(BF)

    if line:
        in_blocks, hidden, boxes, flipped, gather, spread, inner_weight = phase(
            (in_blocks, hidden, boxes, flipped, gather, spread, inner_weight)
        )
        own, near, far = in_blocks
        both = hop(near, FAR)
        twins = [hop(item, TWIN) for item in (own, near, far)]
        inner_near = hop(inner_weight, NEAR)
        both, twins, inner_near, inner_weight, output_weight = phase(
            (both, twins, inner_near, inner_weight, output_weight)
        )
        in_blocks = [own, near, far, both] + twins + [hop(both, TWIN)]
        inner_far = hop(inner_weight, FAR)
        output_near, output_far = hop(output_weight, NEAR), hop(output_weight, FAR)
    queries, keys, values, vector, table = project(order, hidden, in_blocks)
    lookup, slide = make_tables(table)
    if line:
        (
            queries,
            keys,
            values,
            lookup,
            slide,
            inner_near,
            inner_far,
            output_near,
            output_far,
            outer_weight,
        ) = phase(
            (
                queries,
                keys,
                values,
                lookup,
                slide,
                inner_near,
                inner_far,
                output_near,
                output_far,
                outer_weight,
            )
        )
        outer_near = hop(outer_weight, NEAR)
        output_blocks = [output_weight, output_near, output_far, hop(output_near, FAR)]
    context, prob = attend(lengths, queries, keys, values, boxes, lookup, slide)
    if line:
        context, outer_near, output_blocks, inner_near, inner_far = phase(
            (context, outer_near, output_blocks, inner_near, inner_far)
        )
        inner_blocks = [inner_weight, inner_near, inner_far, hop(inner_near, FAR)]
        outer_far = hop(outer_weight, FAR)
        output_blocks = output_blocks + [hop(item, TWIN) for item in output_blocks]
        inner_twins = [hop(item, TWIN) for item in inner_blocks[:3]]
    context, normed, deviation, first_low = output_block(
        order, context, gather, hidden_in, vector, output_blocks
    )
    if line:
        first_low, inner_blocks, inner_twins, outer_near, outer_far = phase(
            (first_low, inner_blocks, inner_twins, outer_near, outer_far)
        )
        outer_blocks = [outer_weight, outer_near, outer_far, hop(outer_near, FAR)]
        inner_blocks = inner_blocks + inner_twins + [hop(inner_blocks[3], TWIN)]
        outer_twins = [hop(item, TWIN) for item in outer_blocks[:3]]
    active, steep = inner_block(order, first_low, vector, inner_blocks)
    if line:
        active, outer_blocks, outer_twins = phase((active, outer_blocks, outer_twins))
        outer_blocks = outer_blocks + outer_twins + [hop(outer_blocks[3], TWIN)]
    layer_out, d_second, d_outer, second_sums = outer_block(
        order, active, normed, cotangent, vector, outer_blocks
    )

    if line:
        send = turned_blocks(order, 4, active, d_outer)
        d_outer, send = phase((d_outer, send))
        other2 = to_twin(send)
    d_inner, inner_sums = inner_back(order, d_outer, steep, outer_blocks)
    if line:
        d_inner, other2 = phase((d_inner, other2))
        stay2, away2 = turned_blocks(order, 0, active, d_outer, other2)
        d_inner, stay2, away2 = phase((d_inner, stay2, away2))
        other2 = hop(away2, FAR)
        d_inner, stay2 = phase((d_inner, stay2))
    d_summed, d_attn, first_sums = first_back(
        order, d_inner, d_second, normed, deviation, vector, inner_blocks
    )
    if line:
        pairs1 = ((first_low, d_inner), (context, d_attn))
        send = grad_blocks(order, 4, pairs1, 1024)
        d_attn, send, stay2, other2 = phase((d_attn, send, stay2, other2))
        other1 = to_twin(send)
        stay2, away2 = fold_far(stay2, other2)
        other2 = hop(away2, NEAR)
    d_context = context_back(order, d_attn, spread, output_blocks)
    if line:
        d_context, other1, stay2 = phase((d_context, other1, stay2))
        stay1, away1 = grad_blocks(order, 0, pairs1, 1024, other1)
        d_context, stay1, away1, stay2, other2 = phase(
            (d_context, stay1, away1, stay2, other2)
        )
        other1 = hop(away1, FAR)
        kept2, sent2 = cut(stay2 + other2, 1)
        other2 = trade(sent2, 1)
    d_mixed, slide_sum, box_sum, bias_sum = attend_back(
        queries, keys, values, d_context, boxes, flipped, prob
    )
    sums = (slide_sum, box_sum, bias_sum, first_sums, inner_sums, second_sums)
    if line:
        pairs = ((hidden, d_mixed),)
        d_mixed, kept2, other2, stay1, sums = phase((d_mixed, kept2, other2, stay1, sums))
        kept2, sent2 = cut(kept2 + other2, 2)
        other2 = trade(sent2, 2)
        send = grad_blocks(order, 4, pairs, 1024)
        d_mixed, send, kept2, other2, stay1, other1, sums = phase(
            (d_mixed, send, kept2, other2, stay1, other1, sums)
        )
        other = to_twin(send)
        stay1, away1 = fold_far(stay1, other1)
        other1 = hop(away1, NEAR)
        kept2 = kept2 + other2
        other2 = trade(kept2, 2)
    small = small_blocks(order, sums)
    if line:
        d_mixed, other, small, stay1, kept2 = phase((d_mixed, other, small, stay1, kept2))
        stay, away = grad_blocks(order, 0, pairs, 1024, other)
        d_mixed, stay, away, stay1, other1, kept2, other2, small = phase(
            (d_mixed, stay, away, stay1, other1, kept2, other2, small)
        )
        other = hop(away, FAR)
        small_other = to_twin(small[4:])
        kept1, sent1 = cut(stay1 + other1, 1)
        other1 = trade(sent1, 1)
    input_grad = input_back(order, d_mixed, gather, d_summed, in_blocks)
    if line:
        stay, other, input_grad, small, small_other, kept1, other1, kept2, other2 = phase(
            (stay, other, input_grad, small, small_other, kept1, other1, kept2, other2)
        )
        stay, away = fold_far(stay, other)
        other = hop(away, NEAR)
        kept1, sent1 = cut(kept1 + other1, 2)
        other1 = trade(sent1, 2)
        kept2 = paste(kept2, other2, 2)
        other2 = trade(kept2, 1)
        small = [small[i] + small_other[i] for i in range(4)]
        small_other = hop(jnp.stack(small[2:]), FAR)
        stay, other, small, small_other, kept1, other1, kept2, other2 = phase(
            (stay, other, small, small_other, kept1, other1, kept2, other2)
        )
        kept, sent = cut(stay + other, 1)
        other = trade(sent, 1)
        kept1 = kept1 + other1
        other1 = trade(kept1, 2)
        small = small[0] + small_other[0], small[1] + small_other[1]
        small_other = hop(small[1], NEAR)
        kept, other, kept1, other1, small, small_other, kept2, other2 = phase(
            (kept, other, kept1, other1, small, small_other, kept2, other2)
        )
        kept, sent = cut(kept + other, 2)
        other = trade(sent, 2)
        kept1 = paste(kept1, other1, 2)
        other1 = trade(kept1, 1)
        small = small[0] + small_other
        small_other = trade(small, 1)
        outer_own = upright(paste(kept2, other2, 1))
        kept, other, kept1, other1, small, small_other, outer_own = phase(
            (kept, other, kept1, other1, small, small_other, outer_own)
        )
        kept = kept + other
        other = trade(kept, 2)
        small = small + small_other
        small_other = trade(small, 2)
        inner_own = paste(kept1, other1, 1).astype(F32)
        kept, other, small, small_other, inner_own = phase(
            (kept, other, small, small_other, inner_own)
        )
        kept = paste(kept, other, 2)
        other = trade(kept, 1)
        small = (small + small_other).reshape(-1)
        kept, other, small = phase((kept, other, small))
        in_own = paste(kept, other, 1)
        inner_own, output_own = inner_own[:, : 4 * width], inner_own[:, 4 * width :]
        cuts = np.cumsum([0] + [item.shape[0] for item in vectors])
        owned = [small[cuts[i] : cuts[i + 1]] for i in range(len(vectors))]
    else:

        def reduce(value):
            value = lax.psum_scatter(value, "fsdp", scatter_dimension=0, tiled=True)
            return lax.psum(value, "dp")

        small = jnp.stack(small)[:, :18].reshape(8, -1)
        edges = np.cumsum([0] + [item.shape[0] * mesh_size // 8 for item in vectors])
        owned = [
            reduce(small[:, edges[i] : edges[i + 1]].reshape(-1)) for i in range(len(vectors))
        ]
        outer_own = reduce(dot(active, d_outer, TN).astype(BF))
        inner_own = reduce(dot(first_low, d_inner, TN).astype(BF))
        output_own = reduce(dot(context, d_attn, TN).astype(BF))
        in_own = reduce(dot(hidden, d_mixed, TN).astype(BF))
    in_own = in_own.astype(F32)
    return (
        layer_out,
        input_grad,
        in_own[:, :width],
        owned[0],
        in_own[:, width : 2 * width],
        in_own[:, 2 * width :],
        owned[1],
        output_own.astype(F32),
        owned[2],
        owned[3],
        owned[4],
        inner_own.astype(F32),
        owned[5],
        outer_own.astype(F32),
        owned[6],
        owned[7],
        owned[8],
        owned[9],
    )


def solution(mesh):
    line = mesh.shape["fsdp"] == 8 and mesh.shape["dp"] == 4
    both, across, flat = P(("fsdp", "dp"), None), P("fsdp", None), P("fsdp")
    return jax.shard_map(
        partial(on_device, line, mesh.shape["fsdp"]),
        mesh=mesh,
        in_specs=(both,) * 5
        + (across, flat, across, across, flat, across, flat, flat, flat)
        + (across, flat, across, flat, flat, flat, flat),
        out_specs=(both, both)
        + (across, flat, across, across, flat, across, flat, flat, flat)
        + (across, flat, across, flat, flat, flat, flat),
        check_vma=False,
    )
```
